256 devices in a mesh: dp: 8 (over z), expert: 8 (over x, core), tensor: 4 (over y).
Axes of the slice: x: 4, y: 4, z: 8, core: 2. Of those that a mesh axis runs over, the one named last changes fastest.
Arguments:
- skip_stream_entry: bfloat16 [4096, 4096], P(('dp', 'expert', 'tensor')), may hold values from -6 to 6
- question_vectors: bfloat16 [4096, 2048], P(('dp', 'expert'), 'tensor'), may hold values from -5 to 5
- fresh_lookup_vectors: bfloat16 [4096, 512], P(('dp', 'expert'), 'tensor'), may hold values from -5 to 5
- fresh_content_vectors: bfloat16 [4096, 512], P(('dp', 'expert'), 'tensor'), may hold values from -10 to 10
- stored_lookup_sheets: bfloat16 [2560, 4, 128, 128], P(('dp', 'expert'), 'tensor'), may hold values from -5 to 5
- stored_content_sheets: bfloat16 [2560, 4, 128, 128], P(('dp', 'expert'), 'tensor'), may hold values from -10 to 10
- sequence_sheet_map: int32 [1088, 8], P(('dp', 'expert')), may hold values from 0 to 39
- stored_position_counts: int32 [1088], P(('dp', 'expert')), may hold values from 2 to 1024
- attention_merge_matrix: bfloat16 [2048, 4096], P('tensor'), may hold values from -0.59765625 to 0.59765625
- premix_scale_factor: bfloat16 [4096], replicated, may hold values from 0.5 to 1.5
- chosen_specialists: int32 [4096, 2], P(('dp', 'expert', 'tensor')), may hold values from 0 to 7, all different within a row; in each aligned block of 16 rows (0 to 15, 16 to 31, ...) at most 6 rows name the same one
- selection_shares: float32 [4096, 2], P(('dp', 'expert', 'tensor')), may hold values from 0.2 to 1
- allowed_placements: int32 [8], replicated, may hold values from 2 to 3
- favored_specialist: int32 [1], replicated, may hold values from 0 to 7
- gating_matrices: bfloat16 [8, 7168, 4096], P('expert', ('dp', 'tensor')), may hold values from -0.09375 to 0.09375
- expand_matrices: bfloat16 [8, 7168, 4096], P('expert', ('dp', 'tensor')), may hold values from -0.09375 to 0.09375
- contract_matrices: bfloat16 [8, 7168, 4096], P('expert', ('dp', 'tensor')), may hold values from -0.0625 to 0.0625
Outputs:
- layer_out: bfloat16 [4096, 4096], P(('dp', 'expert', 'tensor'))
The draws below stay inside these ranges and needn't reach their ends.
Inputs may be any that keep to these rules, and one draw needn't show every extreme that they name: `chosen_specialists`: in the 16 rows of one device no expert is named by more than 6 rows; a token names two different experts.
All inputs are finite; a program needn't handle non-finite values.
Results may differ from the reference program's by a relative error of at most 0.018.
Values may be sent and summed in bfloat16 or wider, within the bound.
A program may use at most 128 MiB of HBM per device.

```python
import math
from functools import reduce
import jax
import jax.numpy as jnp
import numpy as np
from jax import lax

D = 4096
HD = 128
SPECIALIST_COUNT = 8
FF = 7168
QH = 16
KVH = 4
PAGE = 128
MAXP = 8
POOL = 40
TOK_DEV = 16
GROUPS = 64
ROWS_GROUP = 64
REQ = 17
TOKENS = 4096
PLACEMENT_MOST = 6
CAP_MOST = 3
SHARDS = 32
FF_SHARD = 224


def draw_question_vectors(key, part):
    array_shape = (TOKENS, QH, HD)
    base = jnp.clip(jax.random.normal(jax.random.fold_in(key, 1), array_shape, jnp.float32), -5.0, 5.0)
    return base.reshape(TOKENS, QH * HD).astype(jnp.bfloat16)


def draw_stored_lookup_sheets(key, part):
    array_shape = (GROUPS * POOL, KVH, PAGE, HD)
    base = jnp.clip(jax.random.normal(jax.random.fold_in(key, 4), array_shape, jnp.float32), -5.0, 5.0)
    return base.astype(jnp.bfloat16)


def draw_stored_position_counts(key, part):
    longest = MAXP * PAGE
    drawn = jax.random.randint(jax.random.fold_in(key, 11), (GROUPS * REQ,), 2, longest + 1)
    target = jax.random.randint(jax.random.fold_in(key, 12), (), 0, GROUPS * REQ)
    return jnp.where(jnp.arange(GROUPS * REQ) == target, longest, drawn).astype(jnp.int32)


def draw_allowed_placements(key, part):
    drawn = jax.random.randint(jax.random.fold_in(key, 21), (SPECIALIST_COUNT,), 2, CAP_MOST + 1)
    target = jax.random.randint(jax.random.fold_in(key, 22), (), 0, SPECIALIST_COUNT)
    return jnp.where(jnp.arange(SPECIALIST_COUNT) == target, CAP_MOST, drawn).astype(jnp.int32)


def with_ends(result, stream_key, low, top_value):
    shape = result.shape
    spot = [jax.random.randint(jax.random.fold_in(stream_key, axis), (), 0, shape[axis]) for axis in range(len(shape))]
    result = result.at[tuple(spot)].set(low)
    longest = shape.index(max(shape))
    spot[longest] = (spot[longest] + 1) % shape[longest]
    return result.at[tuple(spot)].set(top_value)


def block_levels(own_key, extent, pieces, smallest, largest):
    factor_of = 1.0
    for axis_at, blocks in pieces:
        steps = jax.random.uniform(jax.random.fold_in(jax.random.fold_in(own_key, 6), axis_at), (blocks,), jnp.float32, smallest / len(pieces), largest / len(pieces))
        factor_of = factor_of * jnp.repeat(jnp.exp(steps), extent[axis_at] // blocks).reshape((-1,) + (1,) * (len(extent) - 1 - axis_at))
    return factor_of


def assign_block(own_key, own, number, rows, amount, top, bound, lean):
    order = jax.random.permutation(own_key, amount)
    crowded, ordinary = shares(amount, rows * top, bound, lean, True), shares(amount, rows * top, bound, lean, False)
    places = jnp.arange(amount)

    def named(tallies, offset_by):
        used = int((tallies > 0).sum())
        fixed = max(1, used // 4)
        passed = fixed + (places - fixed + offset_by * (used - fixed)) % max(1, amount - fixed)
        return jnp.zeros((amount,), jnp.int32).at[order[jnp.where(places < fixed, places, passed)]].set(jnp.asarray(tallies, jnp.int32))

    tallies = jnp.where(number % 4 == 0, named(crowded, number // 4), named(ordinary, number - number // 4 - 1))
    mixed = jax.random.permutation(jax.random.fold_in(own, 3), amount)
    giver, sink = mixed[0:amount // 2 * 2:2], mixed[1:amount // 2 * 2:2]
    slack = jnp.minimum(tallies[giver] - 1, bound - tallies[sink]) // 2
    slack = jnp.where((giver == order[0]) | (sink == order[0]) | (tallies[sink] == 0), 0, jnp.maximum(slack, 0))
    passed = jax.random.randint(jax.random.fold_in(own, 4), (amount // 2,), 0, 1 << 20) % (slack + 1)
    tallies = tallies.at[giver].add(-passed).at[sink].add(passed)
    labels = jnp.searchsorted(jnp.cumsum(tallies), jnp.arange(rows * top), side="right").astype(jnp.int32)
    grid = labels.reshape(top, rows).T
    grid = grid[jax.random.permutation(jax.random.fold_in(own, 1), rows)]
    offset_by = jax.random.randint(jax.random.fold_in(own, 2), (rows, 1), 0, top)
    return jnp.take_along_axis(grid, (jnp.arange(top)[None, :] + offset_by) % top, axis=1)


def shares(amount, total, reach, slope, full):
    weights = [(1 << 20) // math.isqrt(standing ** slope) + 1 for standing in range(1, amount + 1)]
    largest = reach if full else min(reach, max(-(-total // amount), total * weights[0] // sum(weights)))
    least = 1 if total - largest >= amount - 1 else 0
    counts, spare = [largest] + [least] * (amount - 1), total - largest - least * (amount - 1)
    while spare > 0:
        candidates = [i for i in range(1, amount) if counts[i] < largest] or [i for i in range(1, amount) if counts[i] < reach]
        pool, remaining = sum([weights[i] for i in candidates]), spare
        for i in candidates:
            extra = min(reach - counts[i], max(1, remaining * weights[i] // pool), spare)
            counts[i] = counts[i] + extra
            spare = spare - extra
    return np.array(counts)


def bell_draw(key, dims, spread, most, split=(), kind=jnp.bfloat16):
    entries = spread * jax.random.normal(key, dims, jnp.float32)
    if split:
        entries = entries * block_levels(key, dims, split, -0.22, 0.18)
    return jnp.clip(entries, -most, most).astype(kind)


def setup_inputs(seed: int = 0) -> dict:
    keys = jax.random.split(jax.random.key(seed), 18)
    skip_stream_entry = bell_draw(keys[0], (TOKENS, D), 1.0, 6.0, ((0, 256),))
    question_vectors = draw_question_vectors(jax.random.fold_in(keys[17], 71), 0)
    fresh_lookup_vectors = bell_draw(keys[2], (TOKENS, KVH * HD), 1.0, 5.0, ((0, 64), (1, 4)))
    fresh_content_vectors = bell_draw(keys[3], (TOKENS, KVH * HD), 2.0, 10.0, ((0, 64), (1, 4)))
    stored_lookup_sheets = draw_stored_lookup_sheets(jax.random.fold_in(keys[17], 71), 0)
    stored_content_sheets = bell_draw(keys[5], (GROUPS * POOL, KVH, PAGE, HD), 2.0, 10.0, ((0, 64), (1, 4)))
    sequence_sheet_map = with_ends(jax.random.randint(keys[6], (GROUPS * REQ, MAXP), 0, POOL), jax.random.fold_in(keys[6], 1), 0, POOL - 1).astype(jnp.int32)
    stored_position_counts = draw_stored_position_counts(jax.random.fold_in(keys[17], 71), 0)
    attention_merge_matrix = bell_draw(keys[8], (QH * HD, D), 0.1, 0.59765625, ((0, 4),))
    premix_scale_factor = jnp.clip(1.0 + 0.1 * jax.random.normal(keys[9], (D,), jnp.float32), 0.5, 1.5).astype(jnp.bfloat16)
    chosen_specialists_keys = jax.random.split(jax.random.fold_in(keys[10], 1), TOKENS // TOK_DEV)
    chosen_specialists_turns = jax.random.permutation(jax.random.fold_in(keys[10], 3), TOKENS // TOK_DEV)
    chosen_specialists = jax.vmap(lambda own, number: assign_block(jax.random.fold_in(keys[10], 2), own, number, TOK_DEV, SPECIALIST_COUNT, 2, PLACEMENT_MOST, 2))(chosen_specialists_keys, chosen_specialists_turns).reshape((TOKENS, 2))
    selection_shares = jnp.clip(0.2 + 0.8 * jax.random.uniform(keys[11], (TOKENS, 2), jnp.float32) ** block_levels(keys[11], (TOKENS, 2), ((0, 256),), -0.2, 0.2), 0.2, 1.0)
    allowed_placements = draw_allowed_placements(jax.random.fold_in(keys[17], 71), 0)
    favored_specialist = jax.random.randint(keys[13], (1,), 0, SPECIALIST_COUNT).astype(jnp.int32)
    gating_matrices = bell_draw(keys[14], (SPECIALIST_COUNT, FF, D), D ** -0.5, 0.09375, ((0, 8), (1, 32)))
    expand_matrices = bell_draw(keys[15], (SPECIALIST_COUNT, FF, D), D ** -0.5, 0.09375, ((0, 8), (1, 32)))
    contract_matrices = bell_draw(keys[16], (SPECIALIST_COUNT, FF, D), FF ** -0.5, 0.0625, ((0, 8), (1, 32)))
    return dict(skip_stream_entry=skip_stream_entry, question_vectors=question_vectors, fresh_lookup_vectors=fresh_lookup_vectors, fresh_content_vectors=fresh_content_vectors, stored_lookup_sheets=stored_lookup_sheets, stored_content_sheets=stored_content_sheets, sequence_sheet_map=sequence_sheet_map, stored_position_counts=stored_position_counts, attention_merge_matrix=attention_merge_matrix, premix_scale_factor=premix_scale_factor, chosen_specialists=chosen_specialists, selection_shares=selection_shares, allowed_placements=allowed_placements, favored_specialist=favored_specialist, gating_matrices=gating_matrices, expand_matrices=expand_matrices, contract_matrices=contract_matrices)


def normalize(parts):
    highest = reduce(jnp.maximum, [lax.optimization_barrier(jnp.max(jnp.where(visible, scores, -jnp.inf), axis=-1, keepdims=True)) for scores, visible in parts])
    portions = [jnp.where(visible, jnp.exp(scores - highest), 0.0) for scores, visible in parts]
    denominator = reduce(jnp.add, [lax.optimization_barrier(jnp.sum(portion, axis=-1, keepdims=True)) for portion in portions])
    return [(portion / denominator).astype(jnp.bfloat16) for portion in portions]

def attend(question_vectors, new_keys, new_values, key_pages, value_pages, table, spans):
    rows_all, head_count, head_width = question_vectors.shape
    kv_heads = new_keys.shape[1]
    group_size = head_count // kv_heads
    single_count = spans.shape[0] - 1
    page_count = table.shape[1]
    page_width = key_pages.shape[2]
    context = page_count * page_width
    inverse_root = 1.0 / math.sqrt(head_width)
    page_keys = key_pages[table].astype(jnp.float32)
    page_values = value_pages[table].astype(jnp.float32)
    grouped = question_vectors.astype(jnp.float32).reshape(rows_all, kv_heads, group_size, head_width)
    fresh_keys = new_keys.astype(jnp.float32)
    fresh_values = new_values.astype(jnp.float32)
    positions = jnp.arange(context, dtype=jnp.int32)
    single_q = grouped[:single_count]
    cache_dec = jnp.einsum('rkgh,rmkph->rkgmp', single_q, page_keys[:single_count]).reshape(single_count, kv_heads, group_size, context) * inverse_root
    seen_dec = (positions[None, :] < spans[:single_count, None])[:, None, None, :]
    own_dec = jnp.einsum('rkgh,rkh->rkg', single_q, fresh_keys[:single_count])[..., None] * inverse_root
    weight_cache, weight_own = normalize([(cache_dec, seen_dec), (own_dec, jnp.full(own_dec.shape, True))])
    out_dec = jnp.einsum('rkgmp,rmkph->rkgh', weight_cache.astype(jnp.float32).reshape(single_count, kv_heads, group_size, page_count, page_width), page_values[:single_count])
    out_dec = out_dec + weight_own.astype(jnp.float32) * fresh_values[:single_count][:, :, None, :]
    prompt_q = grouped[single_count:]
    prompt_rows = rows_all - single_count
    cache_pro = jnp.einsum('rkgh,mkph->rkgmp', prompt_q, page_keys[single_count]).reshape(prompt_rows, kv_heads, group_size, context) * inverse_root
    seen_pro = (positions < spans[single_count])[None, None, None, :]
    new_pro = jnp.einsum('rkgh,mkh->rkgm', prompt_q, fresh_keys[single_count:]) * inverse_root
    prompt_index = jnp.arange(prompt_rows, dtype=jnp.int32)
    causal = (prompt_index[:, None] >= prompt_index[None, :])[:, None, None, :]
    weight_cpro, weight_npro = normalize([(cache_pro, seen_pro), (new_pro, causal)])
    out_pro = jnp.einsum('rkgmp,mkph->rkgh', weight_cpro.astype(jnp.float32).reshape(prompt_rows, kv_heads, group_size, page_count, page_width), page_values[single_count])
    out_pro = out_pro + jnp.einsum('rkgm,mkh->rkgh', weight_npro.astype(jnp.float32), fresh_values[single_count:])
    joined = jnp.concatenate([out_dec, out_pro], axis=0).astype(jnp.bfloat16)
    return joined.reshape(rows_all, head_count * head_width)

def expert_rows(buffer, gate_w, up_w, down_w):
    gate_part = jnp.dot(buffer, gate_w.T, preferred_element_type=jnp.float32)
    up_part = jnp.dot(buffer, up_w.T, preferred_element_type=jnp.float32)
    hidden = (jax.nn.silu(gate_part) * up_part).astype(jnp.bfloat16)
    blocks = hidden.reshape(hidden.shape[0], SHARDS, FF_SHARD).transpose(1, 0, 2)
    downs = down_w.reshape(SHARDS, FF_SHARD, D)

    def add_block(running, pair):
        partial_out = jnp.dot(pair[0], pair[1], preferred_element_type=jnp.float32).astype(jnp.bfloat16)
        partial_out = lax.optimization_barrier(partial_out)
        return (running + partial_out.astype(jnp.float32), None)
    summed, unused = lax.scan(add_block, jnp.zeros((hidden.shape[0], D), jnp.float32), (blocks, downs))
    return summed.astype(jnp.bfloat16)

def reference(skip_stream_entry, question_vectors, fresh_lookup_vectors, fresh_content_vectors, stored_lookup_sheets, stored_content_sheets, sequence_sheet_map, stored_position_counts, attention_merge_matrix, premix_scale_factor, chosen_specialists, selection_shares, allowed_placements, favored_specialist, gating_matrices, expand_matrices, contract_matrices):
    group_q = question_vectors.reshape(GROUPS, ROWS_GROUP, QH, HD)
    group_k = fresh_lookup_vectors.reshape(GROUPS, ROWS_GROUP, KVH, HD)
    group_v = fresh_content_vectors.reshape(GROUPS, ROWS_GROUP, KVH, HD)
    cache_k = stored_lookup_sheets.reshape(GROUPS, POOL, KVH, PAGE, HD)
    cache_v = stored_content_sheets.reshape(GROUPS, POOL, KVH, PAGE, HD)
    tables = sequence_sheet_map.reshape(GROUPS, REQ, MAXP)
    spans = stored_position_counts.reshape(GROUPS, REQ)
    heads_out = lax.map(lambda items: attend(*items), (group_q, group_k, group_v, cache_k, cache_v, tables, spans))
    heads_out = heads_out.reshape(TOKENS, QH * HD)
    attn_sum = jnp.dot(heads_out, attention_merge_matrix, preferred_element_type=jnp.float32)
    stream = (skip_stream_entry.astype(jnp.float32) + attn_sum).astype(jnp.bfloat16)
    wide = stream.astype(jnp.float32)
    squares = lax.optimization_barrier(jnp.mean(wide * wide, axis=1, keepdims=True))
    normed = (wide * lax.rsqrt(squares + 1e-05) * premix_scale_factor.astype(jnp.float32)).astype(jnp.bfloat16)
    picked = (chosen_specialists[:, :, None] == jnp.arange(SPECIALIST_COUNT, dtype=jnp.int32)[None, None, :]).astype(jnp.int32)
    busiest_specialist = favored_specialist[0]
    nblock = TOKENS // TOK_DEV
    flat_blocks = picked.reshape(nblock, TOK_DEV * 2, SPECIALIST_COUNT)
    before = (jnp.cumsum(flat_blocks, axis=1) - flat_blocks).reshape(TOKENS, 2, SPECIALIST_COUNT)
    ranking = lax.optimization_barrier(jnp.sum(before * picked, axis=2))
    placement_ceiling = jnp.where(jnp.arange(SPECIALIST_COUNT, dtype=jnp.int32) == busiest_specialist, PLACEMENT_MOST, allowed_placements)
    keeping = ranking < lax.optimization_barrier(jnp.sum(picked * placement_ceiling[None, None, :], axis=2))
    slot_hit = ranking[:, :, None] == jnp.arange(PLACEMENT_MOST, dtype=jnp.int32)[None, None, :]
    table_all = (picked[..., None] > 0) & keeping[:, :, None, None] & slot_hit[:, :, None, :]
    table_f = table_all.reshape(nblock, TOK_DEV, 2, SPECIALIST_COUNT, PLACEMENT_MOST).astype(jnp.float32)
    send = jnp.einsum('bnkes,bnd->ebsd', table_f, normed.reshape(nblock, TOK_DEV, D).astype(jnp.float32)).astype(jnp.bfloat16)
    outputs = lax.map(lambda items: expert_rows(items[0].reshape(nblock * PLACEMENT_MOST, D), items[1], items[2], items[3]), (send, gating_matrices, expand_matrices, contract_matrices))
    outputs = outputs.reshape(SPECIALIST_COUNT, nblock, PLACEMENT_MOST, D).astype(jnp.float32)
    chosen = jnp.einsum('bnkes,ebsd->bnkd', table_f, outputs).reshape(TOKENS, 2, D)
    mixed = lax.optimization_barrier(jnp.sum(selection_shares[:, :, None] * chosen, axis=1))
    return (wide + mixed).astype(jnp.bfloat16)
```

```python
from functools import reduce
import math

import jax
import jax.numpy as jnp
from jax import lax
from jax.sharding import PartitionSpec as P

HD = 128
PLACEMENT_MOST = 6


def normalize(parts):
    highest = reduce(
        jnp.maximum,
        [
            jnp.max(jnp.where(visible, scores, -jnp.inf), axis=-1, keepdims=True)
            for scores, visible in parts
        ],
    )
    portions = [jnp.where(visible, jnp.exp(scores - highest), 0.0) for scores, visible in parts]
    denominator = reduce(
        jnp.add, [jnp.sum(portion, axis=-1, keepdims=True) for portion in portions]
    )
    return [(portion / denominator).astype(jnp.bfloat16) for portion in portions]


def attend(question_vectors, new_keys, new_values, key_pages, value_pages, table, spans):
    rows_all, head_count, head_width = question_vectors.shape
    kv_heads = new_keys.shape[1]
    group_size = head_count // kv_heads
    single_count = spans.shape[0] - 1
    page_count = table.shape[1]
    page_width = key_pages.shape[2]
    context = page_count * page_width
    inverse_root = 1.0 / math.sqrt(head_width)
    page_keys = key_pages[table]
    page_values = value_pages[table]
    grouped = question_vectors.reshape(rows_all, kv_heads, group_size, head_width)
    positions = jnp.arange(context, dtype=jnp.int32)
    single_q = grouped[:single_count]
    cache_dec = (
        jnp.einsum(
            "rkgh,rmkph->rkgmp",
            single_q,
            page_keys[:single_count],
            preferred_element_type=jnp.float32,
        ).reshape(single_count, kv_heads, group_size, context)
        * inverse_root
    )
    seen_dec = (positions[None, :] < spans[:single_count, None])[:, None, None, :]
    own_dec = (
        jnp.einsum(
            "rkgh,rkh->rkg", single_q, new_keys[:single_count], preferred_element_type=jnp.float32
        )[..., None]
        * inverse_root
    )
    weight_cache, weight_own = normalize(
        [(cache_dec, seen_dec), (own_dec, jnp.full(own_dec.shape, True))]
    )
    out_dec = jnp.einsum(
        "rkgmp,rmkph->rkgh",
        weight_cache.reshape(single_count, kv_heads, group_size, page_count, page_width),
        page_values[:single_count],
        preferred_element_type=jnp.float32,
    )
    out_dec = (
        out_dec
        + weight_own.astype(jnp.float32)
        * new_values[:single_count].astype(jnp.float32)[:, :, None, :]
    )
    prompt_q = grouped[single_count:]
    prompt_rows = rows_all - single_count
    cache_pro = (
        jnp.einsum(
            "rkgh,mkph->rkgmp",
            prompt_q,
            page_keys[single_count],
            preferred_element_type=jnp.float32,
        ).reshape(prompt_rows, kv_heads, group_size, context)
        * inverse_root
    )
    seen_pro = (positions < spans[single_count])[None, None, None, :]
    new_pro = (
        jnp.einsum(
            "rkgh,mkh->rkgm", prompt_q, new_keys[single_count:], preferred_element_type=jnp.float32
        )
        * inverse_root
    )
    prompt_index = jnp.arange(prompt_rows, dtype=jnp.int32)
    causal = (prompt_index[:, None] >= prompt_index[None, :])[:, None, None, :]
    weight_cpro, weight_npro = normalize([(cache_pro, seen_pro), (new_pro, causal)])
    out_pro = jnp.einsum(
        "rkgmp,mkph->rkgh",
        weight_cpro.reshape(prompt_rows, kv_heads, group_size, page_count, page_width),
        page_values[single_count],
        preferred_element_type=jnp.float32,
    )
    out_pro = out_pro + jnp.einsum(
        "rkgm,mkh->rkgh", weight_npro, new_values[single_count:], preferred_element_type=jnp.float32
    )
    joined = jnp.concatenate([out_dec, out_pro], axis=0).astype(jnp.bfloat16)
    return joined.reshape(rows_all, head_count * head_width)


def slot_table(member, ranking, keeping, slot_count):
    slot_hit = (
        ranking[:, :, None, None] == jnp.arange(slot_count, dtype=jnp.int32)[None, None, None, :]
    )
    return ((member[..., None] > 0) & keeping[:, :, None, None] & slot_hit).astype(jnp.bfloat16)


def expert_pass(send, gating_matrices, expand_matrices, contract_matrices):
    specialist_index, slot_count, model_width = send.shape
    holders = lax.axis_size("expert")
    local_count = gating_matrices.shape[0]
    arrived = lax.all_to_all(
        send.reshape(holders, local_count, slot_count, model_width),
        "expert",
        split_axis=0,
        concat_axis=0,
        tiled=True,
    )
    row_piece = lax.all_gather(arrived, ("dp", "tensor"), axis=0, tiled=True)
    gate_part = jnp.einsum(
        "qesd,efd->qesf", row_piece, gating_matrices, preferred_element_type=jnp.float32
    )
    up_part = jnp.einsum(
        "qesd,efd->qesf", row_piece, expand_matrices, preferred_element_type=jnp.float32
    )
    hidden = (jax.nn.silu(gate_part) * up_part).astype(jnp.bfloat16)
    summed = lax.psum_scatter(
        jnp.einsum(
            "qesf,efd->qesd", hidden, contract_matrices, preferred_element_type=jnp.float32
        ).astype(jnp.bfloat16),
        ("dp", "tensor"),
        scatter_dimension=0,
        tiled=True,
    )
    arrived_back = lax.all_to_all(summed, "expert", split_axis=0, concat_axis=0, tiled=True)
    return arrived_back.reshape(specialist_index, slot_count, model_width)


def local(
    skip_stream_entry,
    question_vectors,
    fresh_lookup_vectors,
    fresh_content_vectors,
    stored_lookup_sheets,
    stored_content_sheets,
    sequence_sheet_map,
    stored_position_counts,
    attention_merge_matrix,
    premix_scale_factor,
    chosen_specialists,
    selection_shares,
    allowed_placements,
    favored_specialist,
    gating_matrices,
    expand_matrices,
    contract_matrices,
):
    token_count = chosen_specialists.shape[0]
    specialist_index = allowed_placements.shape[0]
    picked = (
        chosen_specialists[:, :, None]
        == jnp.arange(specialist_index, dtype=jnp.int32)[None, None, :]
    ).astype(jnp.int32)
    flat_routes = picked.reshape(token_count * 2, specialist_index)
    busiest_specialist = favored_specialist[0]
    before = (jnp.cumsum(flat_routes, axis=0) - flat_routes).reshape(
        token_count, 2, specialist_index
    )
    ranking = jnp.sum(before * picked, axis=2)
    placement_ceiling = jnp.where(
        jnp.arange(specialist_index, dtype=jnp.int32) == busiest_specialist,
        PLACEMENT_MOST,
        allowed_placements,
    )
    keeping = ranking < jnp.sum(picked * placement_ceiling[None, None, :], axis=2)
    row_total = question_vectors.shape[0]
    heads_out = attend(
        question_vectors.reshape(row_total, -1, HD),
        fresh_lookup_vectors.reshape(row_total, -1, HD),
        fresh_content_vectors.reshape(row_total, -1, HD),
        stored_lookup_sheets,
        stored_content_sheets,
        sequence_sheet_map,
        stored_position_counts,
    )
    own_attn = lax.psum_scatter(
        jnp.dot(heads_out, attention_merge_matrix, preferred_element_type=jnp.float32).astype(
            jnp.bfloat16
        ),
        "tensor",
        scatter_dimension=0,
        tiled=True,
    ).astype(jnp.float32)
    stream = (skip_stream_entry.astype(jnp.float32) + own_attn).astype(jnp.bfloat16)
    wide = stream.astype(jnp.float32)
    squares = jnp.mean(wide * wide, axis=1, keepdims=True)
    normed = (wide * lax.rsqrt(squares + 1e-05) * premix_scale_factor.astype(jnp.float32)).astype(
        jnp.bfloat16
    )
    main_slots = PLACEMENT_MOST
    table_main = slot_table(picked, ranking, keeping, main_slots)
    send = jnp.einsum(
        "nkes,nd->esd", table_main, normed, preferred_element_type=jnp.float32
    ).astype(jnp.bfloat16)
    expert_out = expert_pass(send, gating_matrices, expand_matrices, contract_matrices)
    chosen = jnp.einsum("nkes,esd->nkd", table_main, expert_out, preferred_element_type=jnp.float32)
    mixed = jnp.sum(selection_shares[:, :, None] * chosen, axis=1)
    return (wide + mixed).astype(jnp.bfloat16)


def solution(mesh):
    placed = (
        P(("dp", "expert", "tensor"), None),
        P(("dp", "expert"), "tensor"),
        P(("dp", "expert"), "tensor"),
        P(("dp", "expert"), "tensor"),
        P(("dp", "expert"), "tensor", None, None),
        P(("dp", "expert"), "tensor", None, None),
        P(("dp", "expert"), None),
        P(("dp", "expert")),
        P("tensor", None),
        P(),
        P(("dp", "expert", "tensor"), None),
        P(("dp", "expert", "tensor"), None),
        P(),
        P(),
        P("expert", ("dp", "tensor"), None),
        P("expert", ("dp", "tensor"), None),
        P("expert", ("dp", "tensor"), None),
    )
    return jax.shard_map(
        local,
        mesh=mesh,
        in_specs=placed,
        out_specs=P(("dp", "expert", "tensor"), None),
        check_vma=False,
    )
```

```python
from functools import reduce
import math

import jax
import jax.numpy as jnp
from jax import lax
from jax.sharding import PartitionSpec as P

HD = 128
PLACEMENT_MOST = 6


def normalize(parts):
    highest = reduce(
        jnp.maximum,
        [
            jnp.max(jnp.where(visible, scores, -jnp.inf), axis=-1, keepdims=True)
            for scores, visible in parts
        ],
    )
    portions = [jnp.where(visible, jnp.exp(scores - highest), 0.0) for scores, visible in parts]
    denominator = reduce(
        jnp.add, [jnp.sum(portion, axis=-1, keepdims=True) for portion in portions]
    )
    return [(portion / denominator).astype(jnp.bfloat16) for portion in portions]


def attend(question_vectors, new_keys, new_values, key_pages, value_pages, table, spans):
    rows_all, head_count, head_width = question_vectors.shape
    kv_heads = new_keys.shape[1]
    group_size = head_count // kv_heads
    single_count = spans.shape[0] - 1
    page_count = table.shape[1]
    page_width = key_pages.shape[2]
    context = page_count * page_width
    inverse_root = 1.0 / math.sqrt(head_width)
    page_keys = key_pages[table]
    page_values = value_pages[table]
    grouped = question_vectors.reshape(rows_all, kv_heads, group_size, head_width)
    positions = jnp.arange(context, dtype=jnp.int32)
    single_q = grouped[:single_count]
    cache_dec = (
        jnp.einsum(
            "rkgh,rmkph->rkgmp",
            single_q,
            page_keys[:single_count],
            preferred_element_type=jnp.float32,
        ).reshape(single_count, kv_heads, group_size, context)
        * inverse_root
    )
    seen_dec = (positions[None, :] < spans[:single_count, None])[:, None, None, :]
    own_dec = (
        jnp.einsum(
            "rkgh,rkh->rkg", single_q, new_keys[:single_count], preferred_element_type=jnp.float32
        )[..., None]
        * inverse_root
    )
    weight_cache, weight_own = normalize(
        [(cache_dec, seen_dec), (own_dec, jnp.full(own_dec.shape, True))]
    )
    out_dec = jnp.einsum(
        "rkgmp,rmkph->rkgh",
        weight_cache.reshape(single_count, kv_heads, group_size, page_count, page_width),
        page_values[:single_count],
        preferred_element_type=jnp.float32,
    )
    out_dec = (
        out_dec
        + weight_own.astype(jnp.float32)
        * new_values[:single_count].astype(jnp.float32)[:, :, None, :]
    )
    prompt_q = grouped[single_count:]
    prompt_rows = rows_all - single_count
    cache_pro = (
        jnp.einsum(
            "rkgh,mkph->rkgmp",
            prompt_q,
            page_keys[single_count],
            preferred_element_type=jnp.float32,
        ).reshape(prompt_rows, kv_heads, group_size, context)
        * inverse_root
    )
    seen_pro = (positions < spans[single_count])[None, None, None, :]
    new_pro = (
        jnp.einsum(
            "rkgh,mkh->rkgm", prompt_q, new_keys[single_count:], preferred_element_type=jnp.float32
        )
        * inverse_root
    )
    prompt_index = jnp.arange(prompt_rows, dtype=jnp.int32)
    causal = (prompt_index[:, None] >= prompt_index[None, :])[:, None, None, :]
    weight_cpro, weight_npro = normalize([(cache_pro, seen_pro), (new_pro, causal)])
    out_pro = jnp.einsum(
        "rkgmp,mkph->rkgh",
        weight_cpro.reshape(prompt_rows, kv_heads, group_size, page_count, page_width),
        page_values[single_count],
        preferred_element_type=jnp.float32,
    )
    out_pro = out_pro + jnp.einsum(
        "rkgm,mkh->rkgh", weight_npro, new_values[single_count:], preferred_element_type=jnp.float32
    )
    joined = jnp.concatenate([out_dec, out_pro], axis=0).astype(jnp.bfloat16)
    return joined.reshape(rows_all, head_count * head_width)


def slot_table(member, ranking, keeping, slot_count):
    slot_hit = (
        ranking[:, :, None, None] == jnp.arange(slot_count, dtype=jnp.int32)[None, None, None, :]
    )
    return ((member[..., None] > 0) & keeping[:, :, None, None] & slot_hit).astype(jnp.bfloat16)


def expert_pass(send, gating_matrices, expand_matrices, contract_matrices):
    specialist_index, slot_count, model_width = send.shape
    holders = lax.axis_size("expert")
    local_count = gating_matrices.shape[0]
    arrived = lax.all_to_all(
        send.reshape(holders, local_count, slot_count, model_width),
        "expert",
        split_axis=0,
        concat_axis=0,
        tiled=True,
    )
    row_piece = lax.all_gather(arrived, ("dp", "tensor"), axis=0, tiled=True)
    gate_part = jnp.einsum(
        "qesd,efd->qesf", row_piece, gating_matrices, preferred_element_type=jnp.float32
    )
    up_part = jnp.einsum(
        "qesd,efd->qesf", row_piece, expand_matrices, preferred_element_type=jnp.float32
    )
    hidden = (jax.nn.silu(gate_part) * up_part).astype(jnp.bfloat16)
    partial_out = jnp.einsum(
        "qesf,efd->qesd", hidden, contract_matrices, preferred_element_type=jnp.float32
    ).astype(jnp.bfloat16)
    summed = lax.psum_scatter(
        lax.psum_scatter(partial_out, "dp", scatter_dimension=0, tiled=True),
        "tensor",
        scatter_dimension=0,
        tiled=True,
    )
    arrived_back = lax.all_to_all(summed, "expert", split_axis=0, concat_axis=0, tiled=True)
    return arrived_back.reshape(specialist_index, slot_count, model_width)


def local(
    skip_stream_entry,
    question_vectors,
    fresh_lookup_vectors,
    fresh_content_vectors,
    stored_lookup_sheets,
    stored_content_sheets,
    sequence_sheet_map,
    stored_position_counts,
    attention_merge_matrix,
    premix_scale_factor,
    chosen_specialists,
    selection_shares,
    allowed_placements,
    favored_specialist,
    gating_matrices,
    expand_matrices,
    contract_matrices,
):
    token_count = chosen_specialists.shape[0]
    specialist_index = allowed_placements.shape[0]
    picked = (
        chosen_specialists[:, :, None]
        == jnp.arange(specialist_index, dtype=jnp.int32)[None, None, :]
    ).astype(jnp.int32)
    flat_routes = picked.reshape(token_count * 2, specialist_index)
    busiest_specialist = favored_specialist[0]
    before = (jnp.cumsum(flat_routes, axis=0) - flat_routes).reshape(
        token_count, 2, specialist_index
    )
    ranking = jnp.sum(before * picked, axis=2)
    placement_ceiling = jnp.where(
        jnp.arange(specialist_index, dtype=jnp.int32) == busiest_specialist,
        PLACEMENT_MOST,
        allowed_placements,
    )
    keeping = ranking < jnp.sum(picked * placement_ceiling[None, None, :], axis=2)
    row_total = question_vectors.shape[0]
    heads_out = attend(
        question_vectors.reshape(row_total, -1, HD),
        fresh_lookup_vectors.reshape(row_total, -1, HD),
        fresh_content_vectors.reshape(row_total, -1, HD),
        stored_lookup_sheets,
        stored_content_sheets,
        sequence_sheet_map,
        stored_position_counts,
    )
    own_attn = lax.psum_scatter(
        jnp.dot(heads_out, attention_merge_matrix, preferred_element_type=jnp.float32).astype(
            jnp.bfloat16
        ),
        "tensor",
        scatter_dimension=0,
        tiled=True,
    ).astype(jnp.float32)
    stream = (skip_stream_entry.astype(jnp.float32) + own_attn).astype(jnp.bfloat16)
    wide = stream.astype(jnp.float32)
    squares = jnp.mean(wide * wide, axis=1, keepdims=True)
    normed = (wide * lax.rsqrt(squares + 1e-05) * premix_scale_factor.astype(jnp.float32)).astype(
        jnp.bfloat16
    )
    main_slots = PLACEMENT_MOST
    table_main = slot_table(picked, ranking, keeping, main_slots)
    send = jnp.einsum(
        "nkes,nd->esd", table_main, normed, preferred_element_type=jnp.float32
    ).astype(jnp.bfloat16)
    expert_out = expert_pass(send, gating_matrices, expand_matrices, contract_matrices)
    chosen = jnp.einsum("nkes,esd->nkd", table_main, expert_out, preferred_element_type=jnp.float32)
    mixed = jnp.sum(selection_shares[:, :, None] * chosen, axis=1)
    return (wide + mixed).astype(jnp.bfloat16)


def solution(mesh):
    placed = (
        P(("dp", "expert", "tensor"), None),
        P(("dp", "expert"), "tensor"),
        P(("dp", "expert"), "tensor"),
        P(("dp", "expert"), "tensor"),
        P(("dp", "expert"), "tensor", None, None),
        P(("dp", "expert"), "tensor", None, None),
        P(("dp", "expert"), None),
        P(("dp", "expert")),
        P("tensor", None),
        P(),
        P(("dp", "expert", "tensor"), None),
        P(("dp", "expert", "tensor"), None),
        P(),
        P(),
        P("expert", ("dp", "tensor"), None),
        P("expert", ("dp", "tensor"), None),
        P("expert", ("dp", "tensor"), None),
    )
    return jax.shard_map(
        local,
        mesh=mesh,
        in_specs=placed,
        out_specs=P(("dp", "expert", "tensor"), None),
        check_vma=False,
    )
```

```python
from functools import reduce
import functools
import math

import jax
import jax.numpy as jnp
from jax import lax
from jax.experimental import pallas as pl
from jax.experimental.pallas import tpu as pltpu
from jax.sharding import PartitionSpec as P

HD = 128
PLACEMENT_MOST = 6


MESH_ID = pl.DeviceIdType.MESH


def ring_phase(n, me, step_to, own, chunk_lead, recv, send0, send_sems, recv_sems, first_sem, finish):
    copies = []
    for s in range(n - 1):
        c = lax.rem(me + n * 2 - step_to[1] * (s + 1), n)
        if s == 0:
            for i in range(chunk_lead):
                send0[i] = own(c, i).astype(send0.dtype)
            src = send0
        else:
            copies[-1].wait_recv()
            for i in range(chunk_lead):
                recv[s - 1, i] = (own(c, i) + recv[s - 1, i].astype(jnp.float32)).astype(recv.dtype)
            src = recv.at[s - 1]
        copy = pltpu.make_async_remote_copy(
            src_ref=src,
            dst_ref=recv.at[s],
            send_sem=send_sems.at[first_sem + s],
            recv_sem=recv_sems.at[first_sem + s],
            device_id=step_to[0],
            device_id_type=MESH_ID,
        )
        copy.start()
        copies.append(copy)
        yield copies
    copies[-1].wait_recv()
    for i in range(chunk_lead):
        finish(i, own(me, i) + recv[n - 2, i].astype(jnp.float32))
    yield copies


def moe_sum_kernel(n_dp, n_t, p_ref, o_ref, *scratch):
    recv_sems, send_sems = scratch[-2], scratch[-1]
    bufs = scratch[:-2]
    me_dp = lax.axis_index("dp")
    me_t = lax.axis_index("tensor")
    me_e = lax.axis_index("expert")
    width = o_ref.shape[1] // 4

    def dp_dev(d):
        return (lax.rem(me_dp + n_dp + d, n_dp), me_e, me_t)

    def t_dev(d):
        return (me_dp, me_e, lax.rem(me_t + n_t + d, n_t))

    barrier = pltpu.get_barrier_semaphore()
    for dev in (dp_dev(1), dp_dev(-1), t_dev(1), t_dev(-1)):
        pl.semaphore_signal(barrier, 1, device_id=dev, device_id_type=MESH_ID)
    pl.semaphore_wait(barrier, 4)

    streams = []
    sem_at = 0
    for block in range(4):
        cols = pl.ds(block * width, width)
        direction = 1 if block % 2 == 0 else -1
        r1, s1, acc, r2, s2 = bufs[block * 5: block * 5 + 5]
        if block < 2:
            first = (n_dp, me_dp, (dp_dev(direction), direction), n_t)
            own1 = lambda c, i, cols=cols: p_ref[c, i, :, cols].astype(jnp.float32)
            second = (n_t, me_t, (t_dev(direction), direction))
        else:
            first = (n_t, me_t, (t_dev(direction), direction), n_dp)
            own1 = lambda c, i, cols=cols: p_ref[i, c, :, cols].astype(jnp.float32)
            second = (n_dp, me_dp, (dp_dev(direction), direction))

        def fin1(i, v, acc=acc):
            acc[i] = v

        def fin2(i, v, cols=cols):
            o_ref[:, cols] = v.astype(o_ref.dtype)

        own2 = lambda c, i, acc=acc: acc[c]

        def stream(first=first, second=second, own1=own1, own2=own2, r1=r1, s1=s1, r2=r2, s2=s2,
                   fin1=fin1, fin2=fin2, base=sem_at):
            n1, me1, to1, lead = first
            copies = []
            for copies in ring_phase(n1, me1, to1, own1, lead, r1, s1, send_sems, recv_sems, base, fin1):
                yield
            done1 = copies
            n2, me2, to2 = second
            for copies in ring_phase(n2, me2, to2, own2, 1, r2, s2, send_sems, recv_sems, base + n1 - 1,
                                     lambda i, v: fin2(i, v)):
                yield
            for copy in done1 + copies:
                copy.wait_send()

        streams.append(stream())
        sem_at += n_dp + n_t - 2

    live = list(streams)
    while live:
        nxt = []
        for st in live:
            try:
                next(st)
                nxt.append(st)
            except StopIteration:
                pass
        live = nxt


def moe_sum(partial, n_dp, n_t):
    rows, model_width = partial.shape[2], partial.shape[3]
    width = model_width // 4
    scratch = []
    for block in range(4):
        if block < 2:
            n1, lead, n2 = n_dp, n_t, n_t
        else:
            n1, lead, n2 = n_t, n_dp, n_dp
        scratch += [
            pltpu.VMEM((n1 - 1, lead, rows, width), jnp.bfloat16),
            pltpu.VMEM((lead, rows, width), jnp.bfloat16),
            pltpu.VMEM((lead, rows, width), jnp.float32),
            pltpu.VMEM((n2 - 1, 1, rows, width), jnp.bfloat16),
            pltpu.VMEM((1, rows, width), jnp.bfloat16),
        ]
    copies = 4 * (n_dp + n_t - 2)
    scratch += [pltpu.SemaphoreType.DMA((copies,)), pltpu.SemaphoreType.DMA((copies,))]
    return pl.pallas_call(
        functools.partial(moe_sum_kernel, n_dp, n_t),
        out_shape=jax.ShapeDtypeStruct((rows, model_width), jnp.bfloat16),
        in_specs=[pl.BlockSpec(memory_space=pltpu.VMEM)],
        out_specs=pl.BlockSpec(memory_space=pltpu.VMEM),
        scratch_shapes=scratch,
        compiler_params=pltpu.CompilerParams(
            collective_id=0, has_side_effects=True, vmem_limit_bytes=60 * 1024 * 1024
        ),
    )(partial)


def normalize(parts):
    highest = reduce(
        jnp.maximum,
        [
            jnp.max(jnp.where(visible, scores, -jnp.inf), axis=-1, keepdims=True)
            for scores, visible in parts
        ],
    )
    portions = [jnp.where(visible, jnp.exp(scores - highest), 0.0) for scores, visible in parts]
    denominator = reduce(
        jnp.add, [jnp.sum(portion, axis=-1, keepdims=True) for portion in portions]
    )
    return [(portion / denominator).astype(jnp.bfloat16) for portion in portions]


def attend(question_vectors, new_keys, new_values, key_pages, value_pages, table, spans):
    rows_all, head_count, head_width = question_vectors.shape
    kv_heads = new_keys.shape[1]
    group_size = head_count // kv_heads
    single_count = spans.shape[0] - 1
    page_count = table.shape[1]
    page_width = key_pages.shape[2]
    context = page_count * page_width
    inverse_root = 1.0 / math.sqrt(head_width)
    page_keys = key_pages[table]
    page_values = value_pages[table]
    grouped = question_vectors.reshape(rows_all, kv_heads, group_size, head_width)
    positions = jnp.arange(context, dtype=jnp.int32)
    single_q = grouped[:single_count]
    cache_dec = (
        jnp.einsum(
            "rkgh,rmkph->rkgmp",
            single_q,
            page_keys[:single_count],
            preferred_element_type=jnp.float32,
        ).reshape(single_count, kv_heads, group_size, context)
        * inverse_root
    )
    seen_dec = (positions[None, :] < spans[:single_count, None])[:, None, None, :]
    own_dec = (
        jnp.einsum(
            "rkgh,rkh->rkg", single_q, new_keys[:single_count], preferred_element_type=jnp.float32
        )[..., None]
        * inverse_root
    )
    weight_cache, weight_own = normalize(
        [(cache_dec, seen_dec), (own_dec, jnp.full(own_dec.shape, True))]
    )
    out_dec = jnp.einsum(
        "rkgmp,rmkph->rkgh",
        weight_cache.reshape(single_count, kv_heads, group_size, page_count, page_width),
        page_values[:single_count],
        preferred_element_type=jnp.float32,
    )
    out_dec = (
        out_dec
        + weight_own.astype(jnp.float32)
        * new_values[:single_count].astype(jnp.float32)[:, :, None, :]
    )
    prompt_q = grouped[single_count:]
    prompt_rows = rows_all - single_count
    cache_pro = (
        jnp.einsum(
            "rkgh,mkph->rkgmp",
            prompt_q,
            page_keys[single_count],
            preferred_element_type=jnp.float32,
        ).reshape(prompt_rows, kv_heads, group_size, context)
        * inverse_root
    )
    seen_pro = (positions < spans[single_count])[None, None, None, :]
    new_pro = (
        jnp.einsum(
            "rkgh,mkh->rkgm", prompt_q, new_keys[single_count:], preferred_element_type=jnp.float32
        )
        * inverse_root
    )
    prompt_index = jnp.arange(prompt_rows, dtype=jnp.int32)
    causal = (prompt_index[:, None] >= prompt_index[None, :])[:, None, None, :]
    weight_cpro, weight_npro = normalize([(cache_pro, seen_pro), (new_pro, causal)])
    out_pro = jnp.einsum(
        "rkgmp,mkph->rkgh",
        weight_cpro.reshape(prompt_rows, kv_heads, group_size, page_count, page_width),
        page_values[single_count],
        preferred_element_type=jnp.float32,
    )
    out_pro = out_pro + jnp.einsum(
        "rkgm,mkh->rkgh", weight_npro, new_values[single_count:], preferred_element_type=jnp.float32
    )
    joined = jnp.concatenate([out_dec, out_pro], axis=0).astype(jnp.bfloat16)
    return joined.reshape(rows_all, head_count * head_width)


def slot_table(member, ranking, keeping, slot_count):
    slot_hit = (
        ranking[:, :, None, None] == jnp.arange(slot_count, dtype=jnp.int32)[None, None, None, :]
    )
    return ((member[..., None] > 0) & keeping[:, :, None, None] & slot_hit).astype(jnp.bfloat16)


def expert_pass(send, gating_matrices, expand_matrices, contract_matrices):
    specialist_index, slot_count, model_width = send.shape
    holders = lax.axis_size("expert")
    local_count = gating_matrices.shape[0]
    arrived = lax.all_to_all(
        send.reshape(holders, local_count, slot_count, model_width),
        "expert",
        split_axis=0,
        concat_axis=0,
        tiled=True,
    )
    row_piece = lax.all_gather(arrived, ("dp", "tensor"), axis=0, tiled=True)
    gate_part = jnp.einsum(
        "qesd,efd->qesf", row_piece, gating_matrices, preferred_element_type=jnp.float32
    )
    up_part = jnp.einsum(
        "qesd,efd->qesf", row_piece, expand_matrices, preferred_element_type=jnp.float32
    )
    hidden = (jax.nn.silu(gate_part) * up_part).astype(jnp.bfloat16)
    partial_out = jnp.einsum(
        "qesf,efd->qesd", hidden, contract_matrices, preferred_element_type=jnp.float32
    ).astype(jnp.bfloat16)
    n_dp, n_t = lax.axis_size("dp"), lax.axis_size("tensor")
    summed = moe_sum(
        partial_out.reshape(n_dp, n_t, -1, model_width), n_dp, n_t
    ).reshape(holders, local_count, slot_count, model_width)
    arrived_back = lax.all_to_all(summed, "expert", split_axis=0, concat_axis=0, tiled=True)
    return arrived_back.reshape(specialist_index, slot_count, model_width)


def local(
    skip_stream_entry,
    question_vectors,
    fresh_lookup_vectors,
    fresh_content_vectors,
    stored_lookup_sheets,
    stored_content_sheets,
    sequence_sheet_map,
    stored_position_counts,
    attention_merge_matrix,
    premix_scale_factor,
    chosen_specialists,
    selection_shares,
    allowed_placements,
    favored_specialist,
    gating_matrices,
    expand_matrices,
    contract_matrices,
):
    token_count = chosen_specialists.shape[0]
    specialist_index = allowed_placements.shape[0]
    picked = (
        chosen_specialists[:, :, None]
        == jnp.arange(specialist_index, dtype=jnp.int32)[None, None, :]
    ).astype(jnp.int32)
    flat_routes = picked.reshape(token_count * 2, specialist_index)
    busiest_specialist = favored_specialist[0]
    before = (jnp.cumsum(flat_routes, axis=0) - flat_routes).reshape(
        token_count, 2, specialist_index
    )
    ranking = jnp.sum(before * picked, axis=2)
    placement_ceiling = jnp.where(
        jnp.arange(specialist_index, dtype=jnp.int32) == busiest_specialist,
        PLACEMENT_MOST,
        allowed_placements,
    )
    keeping = ranking < jnp.sum(picked * placement_ceiling[None, None, :], axis=2)
    row_total = question_vectors.shape[0]
    heads_out = attend(
        question_vectors.reshape(row_total, -1, HD),
        fresh_lookup_vectors.reshape(row_total, -1, HD),
        fresh_content_vectors.reshape(row_total, -1, HD),
        stored_lookup_sheets,
        stored_content_sheets,
        sequence_sheet_map,
        stored_position_counts,
    )
    own_attn = lax.psum_scatter(
        jnp.dot(heads_out, attention_merge_matrix, preferred_element_type=jnp.float32).astype(
            jnp.bfloat16
        ),
        "tensor",
        scatter_dimension=0,
        tiled=True,
    ).astype(jnp.float32)
    stream = (skip_stream_entry.astype(jnp.float32) + own_attn).astype(jnp.bfloat16)
    wide = stream.astype(jnp.float32)
    squares = jnp.mean(wide * wide, axis=1, keepdims=True)
    normed = (wide * lax.rsqrt(squares + 1e-05) * premix_scale_factor.astype(jnp.float32)).astype(
        jnp.bfloat16
    )
    main_slots = PLACEMENT_MOST
    table_main = slot_table(picked, ranking, keeping, main_slots)
    send = jnp.einsum(
        "nkes,nd->esd", table_main, normed, preferred_element_type=jnp.float32
    ).astype(jnp.bfloat16)
    expert_out = expert_pass(send, gating_matrices, expand_matrices, contract_matrices)
    chosen = jnp.einsum("nkes,esd->nkd", table_main, expert_out, preferred_element_type=jnp.float32)
    mixed = jnp.sum(selection_shares[:, :, None] * chosen, axis=1)
    return (wide + mixed).astype(jnp.bfloat16)


def solution(mesh):
    placed = (
        P(("dp", "expert", "tensor"), None),
        P(("dp", "expert"), "tensor"),
        P(("dp", "expert"), "tensor"),
        P(("dp", "expert"), "tensor"),
        P(("dp", "expert"), "tensor", None, None),
        P(("dp", "expert"), "tensor", None, None),
        P(("dp", "expert"), None),
        P(("dp", "expert")),
        P("tensor", None),
        P(),
        P(("dp", "expert", "tensor"), None),
        P(("dp", "expert", "tensor"), None),
        P(),
        P(),
        P("expert", ("dp", "tensor"), None),
        P("expert", ("dp", "tensor"), None),
        P("expert", ("dp", "tensor"), None),
    )
    return jax.shard_map(
        local,
        mesh=mesh,
        in_specs=placed,
        out_specs=P(("dp", "expert", "tensor"), None),
        check_vma=False,
    )
```

```python
from functools import reduce
import functools
import math

import jax
import jax.numpy as jnp
from jax import lax
from jax.experimental import pallas as pl
from jax.experimental.pallas import tpu as pltpu
from jax.sharding import PartitionSpec as P

HD = 128
PLACEMENT_MOST = 6


MESH_ID = pl.DeviceIdType.MESH


def ring_phase(n, me, step_to, own, chunk_lead, recv, send0, send_sems, recv_sems, first_sem, finish):
    copies = []
    for s in range(n - 1):
        c = lax.rem(me + n * 2 - step_to[1] * (s + 1), n)
        if s == 0:
            for i in range(chunk_lead):
                send0[i] = own(c, i).astype(send0.dtype)
            src = send0
        else:
            copies[-1].wait_recv()
            for i in range(chunk_lead):
                recv[s - 1, i] = (own(c, i) + recv[s - 1, i].astype(jnp.float32)).astype(recv.dtype)
            src = recv.at[s - 1]
        copy = pltpu.make_async_remote_copy(
            src_ref=src,
            dst_ref=recv.at[s],
            send_sem=send_sems.at[first_sem + s],
            recv_sem=recv_sems.at[first_sem + s],
            device_id=step_to[0],
            device_id_type=MESH_ID,
        )
        copy.start()
        copies.append(copy)
        yield copies
    copies[-1].wait_recv()
    for i in range(chunk_lead):
        finish(i, own(me, i) + recv[n - 2, i].astype(jnp.float32))
    yield copies


def moe_sum_kernel(n_dp, n_t, p_ref, o_ref, *scratch):
    recv_sems, send_sems = scratch[-2], scratch[-1]
    bufs = scratch[:-2]
    me_dp = lax.axis_index("dp")
    me_t = lax.axis_index("tensor")
    me_e = lax.axis_index("expert")
    width = o_ref.shape[1] // 4

    def dp_dev(d):
        return (lax.rem(me_dp + n_dp + d, n_dp), me_e, me_t)

    def t_dev(d):
        return (me_dp, me_e, lax.rem(me_t + n_t + d, n_t))

    barrier = pltpu.get_barrier_semaphore()
    for dev in (dp_dev(1), dp_dev(-1), t_dev(1), t_dev(-1)):
        pl.semaphore_signal(barrier, 1, device_id=dev, device_id_type=MESH_ID)
    pl.semaphore_wait(barrier, 4)

    streams = []
    sem_at = 0
    for block in range(4):
        cols = pl.ds(block * width, width)
        direction = 1 if block % 2 == 0 else -1
        r1, s1, acc, r2, s2 = bufs[block * 5: block * 5 + 5]
        if block < 2:
            first = (n_dp, me_dp, (dp_dev(direction), direction), n_t)
            own1 = lambda c, i, cols=cols: p_ref[c, i, :, cols].astype(jnp.float32)
            second = (n_t, me_t, (t_dev(direction), direction))
        else:
            first = (n_t, me_t, (t_dev(direction), direction), n_dp)
            own1 = lambda c, i, cols=cols: p_ref[i, c, :, cols].astype(jnp.float32)
            second = (n_dp, me_dp, (dp_dev(direction), direction))

        def fin1(i, v, acc=acc):
            acc[i] = v

        def fin2(i, v, cols=cols):
            o_ref[:, cols] = v.astype(o_ref.dtype)

        own2 = lambda c, i, acc=acc: acc[c]

        def stream(first=first, second=second, own1=own1, own2=own2, r1=r1, s1=s1, r2=r2, s2=s2,
                   fin1=fin1, fin2=fin2, base=sem_at):
            n1, me1, to1, lead = first
            copies = []
            for copies in ring_phase(n1, me1, to1, own1, lead, r1, s1, send_sems, recv_sems, base, fin1):
                yield
            done1 = copies
            n2, me2, to2 = second
            for copies in ring_phase(n2, me2, to2, own2, 1, r2, s2, send_sems, recv_sems, base + n1 - 1,
                                     lambda i, v: fin2(i, v)):
                yield
            for copy in done1 + copies:
                copy.wait_send()

        streams.append(stream())
        sem_at += n_dp + n_t - 2

    live = list(streams)
    while live:
        nxt = []
        for st in live:
            try:
                next(st)
                nxt.append(st)
            except StopIteration:
                pass
        live = nxt


def moe_sum(partial, n_dp, n_t):
    rows, model_width = partial.shape[2], partial.shape[3]
    width = model_width // 4
    scratch = []
    for block in range(4):
        if block < 2:
            n1, lead, n2 = n_dp, n_t, n_t
        else:
            n1, lead, n2 = n_t, n_dp, n_dp
        scratch += [
            pltpu.VMEM((n1 - 1, lead, rows, width), jnp.bfloat16),
            pltpu.VMEM((lead, rows, width), jnp.bfloat16),
            pltpu.VMEM((lead, rows, width), jnp.float32),
            pltpu.VMEM((n2 - 1, 1, rows, width), jnp.bfloat16),
            pltpu.VMEM((1, rows, width), jnp.bfloat16),
        ]
    copies = 4 * (n_dp + n_t - 2)
    scratch += [pltpu.SemaphoreType.DMA((copies,)), pltpu.SemaphoreType.DMA((copies,))]
    return pl.pallas_call(
        functools.partial(moe_sum_kernel, n_dp, n_t),
        out_shape=jax.ShapeDtypeStruct((rows, model_width), jnp.bfloat16),
        in_specs=[pl.BlockSpec(memory_space=pltpu.VMEM)],
        out_specs=pl.BlockSpec(memory_space=pltpu.VMEM),
        scratch_shapes=scratch,
        compiler_params=pltpu.CompilerParams(
            collective_id=0, has_side_effects=True, vmem_limit_bytes=60 * 1024 * 1024
        ),
    )(partial)


def normalize(parts):
    highest = reduce(
        jnp.maximum,
        [
            jnp.max(jnp.where(visible, scores, -jnp.inf), axis=-1, keepdims=True)
            for scores, visible in parts
        ],
    )
    portions = [jnp.where(visible, jnp.exp(scores - highest), 0.0) for scores, visible in parts]
    denominator = reduce(
        jnp.add, [jnp.sum(portion, axis=-1, keepdims=True) for portion in portions]
    )
    return [(portion / denominator).astype(jnp.bfloat16) for portion in portions]


def attend(question_vectors, new_keys, new_values, key_pages, value_pages, table, spans):
    rows_all, head_count, head_width = question_vectors.shape
    kv_heads = new_keys.shape[1]
    group_size = head_count // kv_heads
    single_count = spans.shape[0] - 1
    page_count = table.shape[1]
    page_width = key_pages.shape[2]
    context = page_count * page_width
    inverse_root = 1.0 / math.sqrt(head_width)
    page_keys = key_pages[table]
    page_values = value_pages[table]
    grouped = question_vectors.reshape(rows_all, kv_heads, group_size, head_width)
    positions = jnp.arange(context, dtype=jnp.int32)
    single_q = grouped[:single_count]
    cache_dec = (
        jnp.einsum(
            "rkgh,rmkph->rkgmp",
            single_q,
            page_keys[:single_count],
            preferred_element_type=jnp.float32,
        ).reshape(single_count, kv_heads, group_size, context)
        * inverse_root
    )
    seen_dec = (positions[None, :] < spans[:single_count, None])[:, None, None, :]
    own_dec = (
        jnp.einsum(
            "rkgh,rkh->rkg", single_q, new_keys[:single_count], preferred_element_type=jnp.float32
        )[..., None]
        * inverse_root
    )
    weight_cache, weight_own = normalize(
        [(cache_dec, seen_dec), (own_dec, jnp.full(own_dec.shape, True))]
    )
    out_dec = jnp.einsum(
        "rkgmp,rmkph->rkgh",
        weight_cache.reshape(single_count, kv_heads, group_size, page_count, page_width),
        page_values[:single_count],
        preferred_element_type=jnp.float32,
    )
    out_dec = (
        out_dec
        + weight_own.astype(jnp.float32)
        * new_values[:single_count].astype(jnp.float32)[:, :, None, :]
    )
    prompt_q = grouped[single_count:]
    prompt_rows = rows_all - single_count
    cache_pro = (
        jnp.einsum(
            "rkgh,mkph->rkgmp",
            prompt_q,
            page_keys[single_count],
            preferred_element_type=jnp.float32,
        ).reshape(prompt_rows, kv_heads, group_size, context)
        * inverse_root
    )
    seen_pro = (positions < spans[single_count])[None, None, None, :]
    new_pro = (
        jnp.einsum(
            "rkgh,mkh->rkgm", prompt_q, new_keys[single_count:], preferred_element_type=jnp.float32
        )
        * inverse_root
    )
    prompt_index = jnp.arange(prompt_rows, dtype=jnp.int32)
    causal = (prompt_index[:, None] >= prompt_index[None, :])[:, None, None, :]
    weight_cpro, weight_npro = normalize([(cache_pro, seen_pro), (new_pro, causal)])
    out_pro = jnp.einsum(
        "rkgmp,mkph->rkgh",
        weight_cpro.reshape(prompt_rows, kv_heads, group_size, page_count, page_width),
        page_values[single_count],
        preferred_element_type=jnp.float32,
    )
    out_pro = out_pro + jnp.einsum(
        "rkgm,mkh->rkgh", weight_npro, new_values[single_count:], preferred_element_type=jnp.float32
    )
    joined = jnp.concatenate([out_dec, out_pro], axis=0).astype(jnp.bfloat16)
    return joined.reshape(rows_all, head_count * head_width)


def slot_table(member, ranking, keeping, slot_count):
    slot_hit = (
        ranking[:, :, None, None] == jnp.arange(slot_count, dtype=jnp.int32)[None, None, None, :]
    )
    return ((member[..., None] > 0) & keeping[:, :, None, None] & slot_hit).astype(jnp.bfloat16)


def expert_pass(send, gating_matrices, expand_matrices, contract_matrices):
    specialist_index, slot_count, model_width = send.shape
    local_count = gating_matrices.shape[0]
    flat = send.reshape(specialist_index * slot_count, model_width)
    arrived = lax.all_to_all(flat, "expert", split_axis=0, concat_axis=0, tiled=True)
    row_piece = lax.all_gather(arrived, ("dp", "tensor"), axis=0, tiled=True)
    assert local_count == 1
    gate_part = lax.dot_general(
        row_piece, gating_matrices[0], (((1,), (1,)), ((), ())), preferred_element_type=jnp.float32
    )
    up_part = lax.dot_general(
        row_piece, expand_matrices[0], (((1,), (1,)), ((), ())), preferred_element_type=jnp.float32
    )
    hidden = (jax.nn.silu(gate_part) * up_part).astype(jnp.bfloat16)
    partial_out = jnp.dot(
        hidden, contract_matrices[0], preferred_element_type=jnp.float32
    ).astype(jnp.bfloat16)
    n_dp, n_t = lax.axis_size("dp"), lax.axis_size("tensor")
    summed = moe_sum(partial_out.reshape(n_dp, n_t, -1, model_width), n_dp, n_t)
    arrived_back = lax.all_to_all(summed, "expert", split_axis=0, concat_axis=0, tiled=True)
    return arrived_back.reshape(specialist_index, slot_count, model_width)


def local(
    skip_stream_entry,
    question_vectors,
    fresh_lookup_vectors,
    fresh_content_vectors,
    stored_lookup_sheets,
    stored_content_sheets,
    sequence_sheet_map,
    stored_position_counts,
    attention_merge_matrix,
    premix_scale_factor,
    chosen_specialists,
    selection_shares,
    allowed_placements,
    favored_specialist,
    gating_matrices,
    expand_matrices,
    contract_matrices,
):
    token_count = chosen_specialists.shape[0]
    specialist_index = allowed_placements.shape[0]
    picked = (
        chosen_specialists[:, :, None]
        == jnp.arange(specialist_index, dtype=jnp.int32)[None, None, :]
    ).astype(jnp.int32)
    flat_routes = picked.reshape(token_count * 2, specialist_index)
    busiest_specialist = favored_specialist[0]
    before = (jnp.cumsum(flat_routes, axis=0) - flat_routes).reshape(
        token_count, 2, specialist_index
    )
    ranking = jnp.sum(before * picked, axis=2)
    placement_ceiling = jnp.where(
        jnp.arange(specialist_index, dtype=jnp.int32) == busiest_specialist,
        PLACEMENT_MOST,
        allowed_placements,
    )
    keeping = ranking < jnp.sum(picked * placement_ceiling[None, None, :], axis=2)
    row_total = question_vectors.shape[0]
    heads_out = attend(
        question_vectors.reshape(row_total, -1, HD),
        fresh_lookup_vectors.reshape(row_total, -1, HD),
        fresh_content_vectors.reshape(row_total, -1, HD),
        stored_lookup_sheets,
        stored_content_sheets,
        sequence_sheet_map,
        stored_position_counts,
    )
    own_attn = lax.psum_scatter(
        jnp.dot(heads_out, attention_merge_matrix, preferred_element_type=jnp.float32).astype(
            jnp.bfloat16
        ),
        "tensor",
        scatter_dimension=0,
        tiled=True,
    ).astype(jnp.float32)
    stream = (skip_stream_entry.astype(jnp.float32) + own_attn).astype(jnp.bfloat16)
    wide = stream.astype(jnp.float32)
    squares = jnp.mean(wide * wide, axis=1, keepdims=True)
    normed = (wide * lax.rsqrt(squares + 1e-05) * premix_scale_factor.astype(jnp.float32)).astype(
        jnp.bfloat16
    )
    main_slots = PLACEMENT_MOST
    table_main = slot_table(picked, ranking, keeping, main_slots)
    send = jnp.einsum(
        "nkes,nd->esd", table_main, normed, preferred_element_type=jnp.float32
    ).astype(jnp.bfloat16)
    expert_out = expert_pass(send, gating_matrices, expand_matrices, contract_matrices)
    chosen = jnp.einsum("nkes,esd->nkd", table_main, expert_out, preferred_element_type=jnp.float32)
    mixed = jnp.sum(selection_shares[:, :, None] * chosen, axis=1)
    return (wide + mixed).astype(jnp.bfloat16)


def solution(mesh):
    placed = (
        P(("dp", "expert", "tensor"), None),
        P(("dp", "expert"), "tensor"),
        P(("dp", "expert"), "tensor"),
        P(("dp", "expert"), "tensor"),
        P(("dp", "expert"), "tensor", None, None),
        P(("dp", "expert"), "tensor", None, None),
        P(("dp", "expert"), None),
        P(("dp", "expert")),
        P("tensor", None),
        P(),
        P(("dp", "expert", "tensor"), None),
        P(("dp", "expert", "tensor"), None),
        P(),
        P(),
        P("expert", ("dp", "tensor"), None),
        P("expert", ("dp", "tensor"), None),
        P("expert", ("dp", "tensor"), None),
    )
    return jax.shard_map(
        local,
        mesh=mesh,
        in_specs=placed,
        out_specs=P(("dp", "expert", "tensor"), None),
        check_vma=False,
    )
```

```python
from functools import reduce
import functools
import math

import jax
import jax.numpy as jnp
from jax import lax
from jax.experimental import pallas as pl
from jax.experimental.pallas import tpu as pltpu
from jax.sharding import PartitionSpec as P

HD = 128
PLACEMENT_MOST = 6


MESH_ID = pl.DeviceIdType.MESH


def ring_phase(n, me, step_to, own, chunk_lead, recv, send0, send_sems, recv_sems, first_sem, finish):
    copies = []
    for s in range(n - 1):
        c = lax.rem(me + n * 2 - step_to[1] * (s + 1), n)
        if s == 0:
            for i in range(chunk_lead):
                send0[i] = own(c, i).astype(send0.dtype)
            src = send0
        else:
            copies[-1].wait_recv()
            for i in range(chunk_lead):
                recv[s - 1, i] = (own(c, i) + recv[s - 1, i].astype(jnp.float32)).astype(recv.dtype)
            src = recv.at[s - 1]
        copy = pltpu.make_async_remote_copy(
            src_ref=src,
            dst_ref=recv.at[s],
            send_sem=send_sems.at[first_sem + s],
            recv_sem=recv_sems.at[first_sem + s],
            device_id=step_to[0],
            device_id_type=MESH_ID,
        )
        copy.start()
        copies.append(copy)
        yield copies
    copies[-1].wait_recv()
    for i in range(chunk_lead):
        finish(i, own(me, i) + recv[n - 2, i].astype(jnp.float32))
    yield copies


def moe_sum_kernel(n_dp, n_t, p_ref, o_ref, *scratch):
    recv_sems, send_sems = scratch[-2], scratch[-1]
    bufs = scratch[:-2]
    me_dp = lax.axis_index("dp")
    me_t = lax.axis_index("tensor")
    me_e = lax.axis_index("expert")
    width = o_ref.shape[1] // 4

    def dp_dev(d):
        return (lax.rem(me_dp + n_dp + d, n_dp), me_e, me_t)

    def t_dev(d):
        return (me_dp, me_e, lax.rem(me_t + n_t + d, n_t))

    barrier = pltpu.get_barrier_semaphore()
    for dev in (dp_dev(1), dp_dev(-1), t_dev(1), t_dev(-1)):
        pl.semaphore_signal(barrier, 1, device_id=dev, device_id_type=MESH_ID)
    pl.semaphore_wait(barrier, 4)

    streams = []
    sem_at = 0
    for block in range(4):
        cols = pl.ds(block * width, width)
        direction = 1 if block % 2 == 0 else -1
        r1, s1, acc, r2, s2 = bufs[block * 5: block * 5 + 5]
        if block < 2:
            first = (n_dp, me_dp, (dp_dev(direction), direction), n_t)
            own1 = lambda c, i, cols=cols: p_ref[c, i, :, cols].astype(jnp.float32)
            second = (n_t, me_t, (t_dev(direction), direction))
        else:
            first = (n_t, me_t, (t_dev(direction), direction), n_dp)
            own1 = lambda c, i, cols=cols: p_ref[i, c, :, cols].astype(jnp.float32)
            second = (n_dp, me_dp, (dp_dev(direction), direction))

        def fin1(i, v, acc=acc):
            acc[i] = v

        def fin2(i, v, cols=cols):
            o_ref[:, cols] = v.astype(o_ref.dtype)

        own2 = lambda c, i, acc=acc: acc[c]

        def stream(first=first, second=second, own1=own1, own2=own2, r1=r1, s1=s1, r2=r2, s2=s2,
                   fin1=fin1, fin2=fin2, base=sem_at):
            n1, me1, to1, lead = first
            copies = []
            for copies in ring_phase(n1, me1, to1, own1, lead, r1, s1, send_sems, recv_sems, base, fin1):
                yield
            done1 = copies
            n2, me2, to2 = second
            for copies in ring_phase(n2, me2, to2, own2, 1, r2, s2, send_sems, recv_sems, base + n1 - 1,
                                     lambda i, v: fin2(i, v)):
                yield
            for copy in done1 + copies:
                copy.wait_send()

        streams.append(stream())
        sem_at += n_dp + n_t - 2

    live = list(streams)
    while live:
        nxt = []
        for st in live:
            try:
                next(st)
                nxt.append(st)
            except StopIteration:
                pass
        live = nxt


def gather_phase(n, me, step_to, chunk, send_sems, recv_sems, first_sem):
    copies = []
    for s in range(n - 1):
        c = lax.rem(me + n * 2 - step_to[1] * s, n)
        if s > 0:
            copies[-1].wait_recv()
        copy = pltpu.make_async_remote_copy(
            src_ref=chunk(c),
            dst_ref=chunk(c),
            send_sem=send_sems.at[first_sem + s],
            recv_sem=recv_sems.at[first_sem + s],
            device_id=step_to[0],
            device_id_type=MESH_ID,
        )
        copy.start()
        copies.append(copy)
        yield copies
    copies[-1].wait_recv()
    yield copies


def row_gather_kernel(n_dp, n_t, x_ref, o_ref, *scratch):
    recv_sems, send_sems = scratch[-2], scratch[-1]
    bufs = scratch[:-2]
    me_dp = lax.axis_index("dp")
    me_t = lax.axis_index("tensor")
    me_e = lax.axis_index("expert")
    rows = x_ref.shape[0]
    width = x_ref.shape[1] // 4

    def dp_dev(d):
        return (lax.rem(me_dp + n_dp + d, n_dp), me_e, me_t)

    def t_dev(d):
        return (me_dp, me_e, lax.rem(me_t + n_t + d, n_t))

    for block in range(4):
        cols = pl.ds(block * width, width)
        if block < 2:
            bufs[block][me_t, me_dp] = x_ref[:, cols]
        else:
            bufs[block][me_dp, me_t] = x_ref[:, cols]

    barrier = pltpu.get_barrier_semaphore()
    for dev in (dp_dev(1), dp_dev(-1), t_dev(1), t_dev(-1)):
        pl.semaphore_signal(barrier, 1, device_id=dev, device_id_type=MESH_ID)
    pl.semaphore_wait(barrier, 4)

    streams = []
    sem_at = 0
    for block in range(4):
        direction = 1 if block % 2 == 0 else -1
        g = bufs[block]
        if block < 2:
            first = (n_dp, me_dp, (dp_dev(direction), direction), lambda c, g=g: g.at[me_t, c])
            second = (n_t, me_t, (t_dev(direction), direction), lambda c, g=g: g.at[c])
        else:
            first = (n_t, me_t, (t_dev(direction), direction), lambda c, g=g: g.at[me_dp, c])
            second = (n_dp, me_dp, (dp_dev(direction), direction), lambda c, g=g: g.at[c])

        def stream(first=first, second=second, base=sem_at):
            n1, me1, to1, chunk1 = first
            copies = []
            for copies in gather_phase(n1, me1, to1, chunk1, send_sems, recv_sems, base):
                yield
            done1 = copies
            n2, me2, to2, chunk2 = second
            for copies in gather_phase(n2, me2, to2, chunk2, send_sems, recv_sems, base + n1 - 1):
                yield
            for copy in done1 + copies:
                copy.wait_send()

        streams.append(stream())
        sem_at += n_dp + n_t - 2

    live = list(streams)
    while live:
        nxt = []
        for st in live:
            try:
                next(st)
                nxt.append(st)
            except StopIteration:
                pass
        live = nxt

    for block in range(4):
        cols = pl.ds(block * width, width)
        for d in range(n_dp):
            for t in range(n_t):
                piece = bufs[block][t, d] if block < 2 else bufs[block][d, t]
                o_ref[pl.ds((d * n_t + t) * rows, rows), cols] = piece


def row_gather(x, n_dp, n_t):
    rows, model_width = x.shape
    width = model_width // 4
    scratch = [
        pltpu.VMEM((n_t, n_dp, rows, width), jnp.bfloat16),
        pltpu.VMEM((n_t, n_dp, rows, width), jnp.bfloat16),
        pltpu.VMEM((n_dp, n_t, rows, width), jnp.bfloat16),
        pltpu.VMEM((n_dp, n_t, rows, width), jnp.bfloat16),
    ]
    copies = 4 * (n_dp + n_t - 2)
    scratch += [pltpu.SemaphoreType.DMA((copies,)), pltpu.SemaphoreType.DMA((copies,))]
    return pl.pallas_call(
        functools.partial(row_gather_kernel, n_dp, n_t),
        out_shape=jax.ShapeDtypeStruct((n_dp * n_t * rows, model_width), jnp.bfloat16),
        in_specs=[pl.BlockSpec(memory_space=pltpu.VMEM)],
        out_specs=pl.BlockSpec(memory_space=pltpu.VMEM),
        scratch_shapes=scratch,
        compiler_params=pltpu.CompilerParams(
            collective_id=1, has_side_effects=True, vmem_limit_bytes=60 * 1024 * 1024
        ),
    )(x)


def moe_sum(partial, n_dp, n_t):
    rows, model_width = partial.shape[2], partial.shape[3]
    width = model_width // 4
    scratch = []
    for block in range(4):
        if block < 2:
            n1, lead, n2 = n_dp, n_t, n_t
        else:
            n1, lead, n2 = n_t, n_dp, n_dp
        scratch += [
            pltpu.VMEM((n1 - 1, lead, rows, width), jnp.bfloat16),
            pltpu.VMEM((lead, rows, width), jnp.bfloat16),
            pltpu.VMEM((lead, rows, width), jnp.float32),
            pltpu.VMEM((n2 - 1, 1, rows, width), jnp.bfloat16),
            pltpu.VMEM((1, rows, width), jnp.bfloat16),
        ]
    copies = 4 * (n_dp + n_t - 2)
    scratch += [pltpu.SemaphoreType.DMA((copies,)), pltpu.SemaphoreType.DMA((copies,))]
    return pl.pallas_call(
        functools.partial(moe_sum_kernel, n_dp, n_t),
        out_shape=jax.ShapeDtypeStruct((rows, model_width), jnp.bfloat16),
        in_specs=[pl.BlockSpec(memory_space=pltpu.VMEM)],
        out_specs=pl.BlockSpec(memory_space=pltpu.VMEM),
        scratch_shapes=scratch,
        compiler_params=pltpu.CompilerParams(
            collective_id=0, has_side_effects=True, vmem_limit_bytes=60 * 1024 * 1024
        ),
    )(partial)


def normalize(parts):
    highest = reduce(
        jnp.maximum,
        [
            jnp.max(jnp.where(visible, scores, -jnp.inf), axis=-1, keepdims=True)
            for scores, visible in parts
        ],
    )
    portions = [jnp.where(visible, jnp.exp(scores - highest), 0.0) for scores, visible in parts]
    denominator = reduce(
        jnp.add, [jnp.sum(portion, axis=-1, keepdims=True) for portion in portions]
    )
    return [(portion / denominator).astype(jnp.bfloat16) for portion in portions]


def attend(question_vectors, new_keys, new_values, key_pages, value_pages, table, spans):
    rows_all, head_count, head_width = question_vectors.shape
    kv_heads = new_keys.shape[1]
    group_size = head_count // kv_heads
    single_count = spans.shape[0] - 1
    page_count = table.shape[1]
    page_width = key_pages.shape[2]
    context = page_count * page_width
    inverse_root = 1.0 / math.sqrt(head_width)
    page_keys = key_pages[table]
    page_values = value_pages[table]
    grouped = question_vectors.reshape(rows_all, kv_heads, group_size, head_width)
    positions = jnp.arange(context, dtype=jnp.int32)
    single_q = grouped[:single_count]
    cache_dec = (
        jnp.einsum(
            "rkgh,rmkph->rkgmp",
            single_q,
            page_keys[:single_count],
            preferred_element_type=jnp.float32,
        ).reshape(single_count, kv_heads, group_size, context)
        * inverse_root
    )
    seen_dec = (positions[None, :] < spans[:single_count, None])[:, None, None, :]
    own_dec = (
        jnp.einsum(
            "rkgh,rkh->rkg", single_q, new_keys[:single_count], preferred_element_type=jnp.float32
        )[..., None]
        * inverse_root
    )
    weight_cache, weight_own = normalize(
        [(cache_dec, seen_dec), (own_dec, jnp.full(own_dec.shape, True))]
    )
    out_dec = jnp.einsum(
        "rkgmp,rmkph->rkgh",
        weight_cache.reshape(single_count, kv_heads, group_size, page_count, page_width),
        page_values[:single_count],
        preferred_element_type=jnp.float32,
    )
    out_dec = (
        out_dec
        + weight_own.astype(jnp.float32)
        * new_values[:single_count].astype(jnp.float32)[:, :, None, :]
    )
    prompt_q = grouped[single_count:]
    prompt_rows = rows_all - single_count
    cache_pro = (
        jnp.einsum(
            "rkgh,mkph->rkgmp",
            prompt_q,
            page_keys[single_count],
            preferred_element_type=jnp.float32,
        ).reshape(prompt_rows, kv_heads, group_size, context)
        * inverse_root
    )
    seen_pro = (positions < spans[single_count])[None, None, None, :]
    new_pro = (
        jnp.einsum(
            "rkgh,mkh->rkgm", prompt_q, new_keys[single_count:], preferred_element_type=jnp.float32
        )
        * inverse_root
    )
    prompt_index = jnp.arange(prompt_rows, dtype=jnp.int32)
    causal = (prompt_index[:, None] >= prompt_index[None, :])[:, None, None, :]
    weight_cpro, weight_npro = normalize([(cache_pro, seen_pro), (new_pro, causal)])
    out_pro = jnp.einsum(
        "rkgmp,mkph->rkgh",
        weight_cpro.reshape(prompt_rows, kv_heads, group_size, page_count, page_width),
        page_values[single_count],
        preferred_element_type=jnp.float32,
    )
    out_pro = out_pro + jnp.einsum(
        "rkgm,mkh->rkgh", weight_npro, new_values[single_count:], preferred_element_type=jnp.float32
    )
    joined = jnp.concatenate([out_dec, out_pro], axis=0).astype(jnp.bfloat16)
    return joined.reshape(rows_all, head_count * head_width)


def slot_table(member, ranking, keeping, slot_count):
    slot_hit = (
        ranking[:, :, None, None] == jnp.arange(slot_count, dtype=jnp.int32)[None, None, None, :]
    )
    return ((member[..., None] > 0) & keeping[:, :, None, None] & slot_hit).astype(jnp.bfloat16)


def expert_pass(send, gating_matrices, expand_matrices, contract_matrices):
    specialist_index, slot_count, model_width = send.shape
    local_count = gating_matrices.shape[0]
    flat = send.reshape(specialist_index * slot_count, model_width)
    arrived = lax.all_to_all(flat, "expert", split_axis=0, concat_axis=0, tiled=True)
    row_piece = row_gather(arrived, lax.axis_size("dp"), lax.axis_size("tensor"))
    assert local_count == 1
    gate_part = lax.dot_general(
        row_piece, gating_matrices[0], (((1,), (1,)), ((), ())), preferred_element_type=jnp.float32
    )
    up_part = lax.dot_general(
        row_piece, expand_matrices[0], (((1,), (1,)), ((), ())), preferred_element_type=jnp.float32
    )
    hidden = (jax.nn.silu(gate_part) * up_part).astype(jnp.bfloat16)
    partial_out = jnp.dot(
        hidden, contract_matrices[0], preferred_element_type=jnp.float32
    ).astype(jnp.bfloat16)
    n_dp, n_t = lax.axis_size("dp"), lax.axis_size("tensor")
    summed = moe_sum(partial_out.reshape(n_dp, n_t, -1, model_width), n_dp, n_t)
    arrived_back = lax.all_to_all(summed, "expert", split_axis=0, concat_axis=0, tiled=True)
    return arrived_back.reshape(specialist_index, slot_count, model_width)


def local(
    skip_stream_entry,
    question_vectors,
    fresh_lookup_vectors,
    fresh_content_vectors,
    stored_lookup_sheets,
    stored_content_sheets,
    sequence_sheet_map,
    stored_position_counts,
    attention_merge_matrix,
    premix_scale_factor,
    chosen_specialists,
    selection_shares,
    allowed_placements,
    favored_specialist,
    gating_matrices,
    expand_matrices,
    contract_matrices,
):
    token_count = chosen_specialists.shape[0]
    specialist_index = allowed_placements.shape[0]
    picked = (
        chosen_specialists[:, :, None]
        == jnp.arange(specialist_index, dtype=jnp.int32)[None, None, :]
    ).astype(jnp.int32)
    flat_routes = picked.reshape(token_count * 2, specialist_index)
    busiest_specialist = favored_specialist[0]
    before = (jnp.cumsum(flat_routes, axis=0) - flat_routes).reshape(
        token_count, 2, specialist_index
    )
    ranking = jnp.sum(before * picked, axis=2)
    placement_ceiling = jnp.where(
        jnp.arange(specialist_index, dtype=jnp.int32) == busiest_specialist,
        PLACEMENT_MOST,
        allowed_placements,
    )
    keeping = ranking < jnp.sum(picked * placement_ceiling[None, None, :], axis=2)
    row_total = question_vectors.shape[0]
    heads_out = attend(
        question_vectors.reshape(row_total, -1, HD),
        fresh_lookup_vectors.reshape(row_total, -1, HD),
        fresh_content_vectors.reshape(row_total, -1, HD),
        stored_lookup_sheets,
        stored_content_sheets,
        sequence_sheet_map,
        stored_position_counts,
    )
    own_attn = lax.psum_scatter(
        jnp.dot(heads_out, attention_merge_matrix, preferred_element_type=jnp.float32).astype(
            jnp.bfloat16
        ),
        "tensor",
        scatter_dimension=0,
        tiled=True,
    ).astype(jnp.float32)
    stream = (skip_stream_entry.astype(jnp.float32) + own_attn).astype(jnp.bfloat16)
    wide = stream.astype(jnp.float32)
    squares = jnp.mean(wide * wide, axis=1, keepdims=True)
    normed = (wide * lax.rsqrt(squares + 1e-05) * premix_scale_factor.astype(jnp.float32)).astype(
        jnp.bfloat16
    )
    main_slots = PLACEMENT_MOST
    table_main = slot_table(picked, ranking, keeping, main_slots)
    send = jnp.einsum(
        "nkes,nd->esd", table_main, normed, preferred_element_type=jnp.float32
    ).astype(jnp.bfloat16)
    expert_out = expert_pass(send, gating_matrices, expand_matrices, contract_matrices)
    chosen = jnp.einsum("nkes,esd->nkd", table_main, expert_out, preferred_element_type=jnp.float32)
    mixed = jnp.sum(selection_shares[:, :, None] * chosen, axis=1)
    return (wide + mixed).astype(jnp.bfloat16)


def solution(mesh):
    placed = (
        P(("dp", "expert", "tensor"), None),
        P(("dp", "expert"), "tensor"),
        P(("dp", "expert"), "tensor"),
        P(("dp", "expert"), "tensor"),
        P(("dp", "expert"), "tensor", None, None),
        P(("dp", "expert"), "tensor", None, None),
        P(("dp", "expert"), None),
        P(("dp", "expert")),
        P("tensor", None),
        P(),
        P(("dp", "expert", "tensor"), None),
        P(("dp", "expert", "tensor"), None),
        P(),
        P(),
        P("expert", ("dp", "tensor"), None),
        P("expert", ("dp", "tensor"), None),
        P("expert", ("dp", "tensor"), None),
    )
    return jax.shard_map(
        local,
        mesh=mesh,
        in_specs=placed,
        out_specs=P(("dp", "expert", "tensor"), None),
        check_vma=False,
    )
```

```python
from functools import reduce
import functools
import math

import jax
import jax.numpy as jnp
from jax import lax
from jax.experimental import pallas as pl
from jax.experimental.pallas import tpu as pltpu
from jax.sharding import PartitionSpec as P

HD = 128
PLACEMENT_MOST = 6


MESH_ID = pl.DeviceIdType.MESH


def plan_order(events, rate=50000.0, latency=1.5, per_step=0.3):
    ready = [0.0] * len(events)
    at = [0] * len(events)
    free = {}
    clock = 0.0
    order = []
    while True:
        live = [i for i in range(len(events)) if at[i] < len(events[i])]
        if not live:
            return order, clock
        i = min(live, key=lambda k: (ready[k], k))
        clock = max(clock, ready[i]) + per_step
        send = events[i][at[i]]
        if send is None:
            ready[i] = clock
        else:
            link, size = send
            start = max(clock, free.get(link, 0.0))
            free[link] = start + size / rate
            ready[i] = free[link] + latency
        order.append(i)
        at[i] += 1


def ring_events(n1, n2, link1, link2, size1, size2):
    return [(link1, size1)] * (n1 - 1) + [None] + [(link2, size2)] * (n2 - 1) + [None]


def split_plan(n_dp, n_t, rows, model_width, reduce):
    best = None
    for first_dp in range(128, model_width // 2, 128):
        widths = [first_dp, first_dp, model_width // 2 - first_dp, model_width // 2 - first_dp]
        events = []
        for block, width in enumerate(widths):
            unit = rows * width * 2
            sign = "+" if block % 2 == 0 else "-"
            if block < 2:
                big1, big2 = (n_t * unit, unit) if reduce else (unit, n_dp * unit)
                events.append(ring_events(n_dp, n_t, "z" + sign, "y" + sign, big1, big2))
            else:
                big1, big2 = (n_dp * unit, unit) if reduce else (unit, n_t * unit)
                events.append(ring_events(n_t, n_dp, "y" + sign, "z" + sign, big1, big2))
        order, finish = plan_order(events)
        if best is None or finish < best[0]:
            best = (finish, widths, order)
    return best[1], best[2]


def run_in_order(streams, order):
    for i in order:
        next(streams[i])
    for st in streams:
        for _ in st:
            pass


def ring_phase(n, me, step_to, own, chunk_lead, recv, send0, send_sems, recv_sems, first_sem, finish):
    copies = []
    for s in range(n - 1):
        c = lax.rem(me + n * 2 - step_to[1] * (s + 1), n)
        if s == 0:
            for i in range(chunk_lead):
                send0[i] = own(c, i).astype(send0.dtype)
            src = send0
        else:
            copies[-1].wait_recv()
            for i in range(chunk_lead):
                recv[s - 1, i] = (own(c, i) + recv[s - 1, i].astype(jnp.float32)).astype(recv.dtype)
            src = recv.at[s - 1]
        copy = pltpu.make_async_remote_copy(
            src_ref=src,
            dst_ref=recv.at[s],
            send_sem=send_sems.at[first_sem + s],
            recv_sem=recv_sems.at[first_sem + s],
            device_id=step_to[0],
            device_id_type=MESH_ID,
        )
        copy.start()
        copies.append(copy)
        yield copies
    copies[-1].wait_recv()
    for i in range(chunk_lead):
        finish(i, own(me, i) + recv[n - 2, i].astype(jnp.float32))
    yield copies


def moe_sum_kernel(n_dp, n_t, widths, order, p_ref, o_ref, *scratch):
    recv_sems, send_sems = scratch[-2], scratch[-1]
    bufs = scratch[:-2]
    me_dp = lax.axis_index("dp")
    me_t = lax.axis_index("tensor")
    me_e = lax.axis_index("expert")

    def dp_dev(d):
        return (lax.rem(me_dp + n_dp + d, n_dp), me_e, me_t)

    def t_dev(d):
        return (me_dp, me_e, lax.rem(me_t + n_t + d, n_t))

    barrier = pltpu.get_barrier_semaphore()
    for dev in (dp_dev(1), dp_dev(-1), t_dev(1), t_dev(-1)):
        pl.semaphore_signal(barrier, 1, device_id=dev, device_id_type=MESH_ID)
    pl.semaphore_wait(barrier, 4)

    streams = []
    sem_at = 0
    for block in range(4):
        cols = pl.ds(sum(widths[:block]), widths[block])
        direction = 1 if block % 2 == 0 else -1
        r1, s1, acc, r2, s2 = bufs[block * 5: block * 5 + 5]
        if block < 2:
            first = (n_dp, me_dp, (dp_dev(direction), direction), n_t)
            own1 = lambda c, i, cols=cols: p_ref[c, i, :, cols].astype(jnp.float32)
            second = (n_t, me_t, (t_dev(direction), direction))
        else:
            first = (n_t, me_t, (t_dev(direction), direction), n_dp)
            own1 = lambda c, i, cols=cols: p_ref[i, c, :, cols].astype(jnp.float32)
            second = (n_dp, me_dp, (dp_dev(direction), direction))

        def fin1(i, v, acc=acc):
            acc[i] = v

        def fin2(i, v, cols=cols):
            o_ref[:, cols] = v.astype(o_ref.dtype)

        own2 = lambda c, i, acc=acc: acc[c]

        def stream(first=first, second=second, own1=own1, own2=own2, r1=r1, s1=s1, r2=r2, s2=s2,
                   fin1=fin1, fin2=fin2, base=sem_at):
            n1, me1, to1, lead = first
            copies = []
            for copies in ring_phase(n1, me1, to1, own1, lead, r1, s1, send_sems, recv_sems, base, fin1):
                yield
            done1 = copies
            n2, me2, to2 = second
            for copies in ring_phase(n2, me2, to2, own2, 1, r2, s2, send_sems, recv_sems, base + n1 - 1,
                                     lambda i, v: fin2(i, v)):
                yield
            for copy in done1 + copies:
                copy.wait_send()

        streams.append(stream())
        sem_at += n_dp + n_t - 2

    run_in_order(streams, order)


def gather_phase(n, me, step_to, chunk, send_sems, recv_sems, first_sem):
    copies = []
    for s in range(n - 1):
        c = lax.rem(me + n * 2 - step_to[1] * s, n)
        if s > 0:
            copies[-1].wait_recv()
        copy = pltpu.make_async_remote_copy(
            src_ref=chunk(c),
            dst_ref=chunk(c),
            send_sem=send_sems.at[first_sem + s],
            recv_sem=recv_sems.at[first_sem + s],
            device_id=step_to[0],
            device_id_type=MESH_ID,
        )
        copy.start()
        copies.append(copy)
        yield copies
    copies[-1].wait_recv()
    yield copies


def row_gather_kernel(n_dp, n_t, widths, order, x_ref, o_ref, *scratch):
    recv_sems, send_sems = scratch[-2], scratch[-1]
    bufs = scratch[:-2]
    me_dp = lax.axis_index("dp")
    me_t = lax.axis_index("tensor")
    me_e = lax.axis_index("expert")
    rows = x_ref.shape[0]

    def dp_dev(d):
        return (lax.rem(me_dp + n_dp + d, n_dp), me_e, me_t)

    def t_dev(d):
        return (me_dp, me_e, lax.rem(me_t + n_t + d, n_t))

    for block in range(4):
        cols = pl.ds(sum(widths[:block]), widths[block])
        if block < 2:
            bufs[block][me_t, me_dp] = x_ref[:, cols]
        else:
            bufs[block][me_dp, me_t] = x_ref[:, cols]

    barrier = pltpu.get_barrier_semaphore()
    for dev in (dp_dev(1), dp_dev(-1), t_dev(1), t_dev(-1)):
        pl.semaphore_signal(barrier, 1, device_id=dev, device_id_type=MESH_ID)
    pl.semaphore_wait(barrier, 4)

    streams = []
    sem_at = 0
    for block in range(4):
        direction = 1 if block % 2 == 0 else -1
        g = bufs[block]
        if block < 2:
            first = (n_dp, me_dp, (dp_dev(direction), direction), lambda c, g=g: g.at[me_t, c])
            second = (n_t, me_t, (t_dev(direction), direction), lambda c, g=g: g.at[c])
        else:
            first = (n_t, me_t, (t_dev(direction), direction), lambda c, g=g: g.at[me_dp, c])
            second = (n_dp, me_dp, (dp_dev(direction), direction), lambda c, g=g: g.at[c])

        def stream(first=first, second=second, base=sem_at):
            n1, me1, to1, chunk1 = first
            copies = []
            for copies in gather_phase(n1, me1, to1, chunk1, send_sems, recv_sems, base):
                yield
            done1 = copies
            n2, me2, to2, chunk2 = second
            for copies in gather_phase(n2, me2, to2, chunk2, send_sems, recv_sems, base + n1 - 1):
                yield
            for copy in done1 + copies:
                copy.wait_send()

        streams.append(stream())
        sem_at += n_dp + n_t - 2

    run_in_order(streams, order)

    for block in range(4):
        cols = pl.ds(sum(widths[:block]), widths[block])
        for d in range(n_dp):
            for t in range(n_t):
                piece = bufs[block][t, d] if block < 2 else bufs[block][d, t]
                o_ref[pl.ds((d * n_t + t) * rows, rows), cols] = piece


def row_gather(x, n_dp, n_t):
    rows, model_width = x.shape
    widths, order = split_plan(n_dp, n_t, rows, model_width, False)
    scratch = [
        pltpu.VMEM((n_t, n_dp, rows, widths[0]), jnp.bfloat16),
        pltpu.VMEM((n_t, n_dp, rows, widths[1]), jnp.bfloat16),
        pltpu.VMEM((n_dp, n_t, rows, widths[2]), jnp.bfloat16),
        pltpu.VMEM((n_dp, n_t, rows, widths[3]), jnp.bfloat16),
    ]
    copies = 4 * (n_dp + n_t - 2)
    scratch += [pltpu.SemaphoreType.DMA((copies,)), pltpu.SemaphoreType.DMA((copies,))]
    return pl.pallas_call(
        functools.partial(row_gather_kernel, n_dp, n_t, tuple(widths), tuple(order)),
        out_shape=jax.ShapeDtypeStruct((n_dp * n_t * rows, model_width), jnp.bfloat16),
        in_specs=[pl.BlockSpec(memory_space=pltpu.VMEM)],
        out_specs=pl.BlockSpec(memory_space=pltpu.VMEM),
        scratch_shapes=scratch,
        compiler_params=pltpu.CompilerParams(
            collective_id=1, has_side_effects=True, vmem_limit_bytes=60 * 1024 * 1024
        ),
    )(x)


def moe_sum(partial, n_dp, n_t):
    rows, model_width = partial.shape[2], partial.shape[3]
    widths, order = split_plan(n_dp, n_t, rows, model_width, True)
    scratch = []
    for block in range(4):
        width = widths[block]
        if block < 2:
            n1, lead, n2 = n_dp, n_t, n_t
        else:
            n1, lead, n2 = n_t, n_dp, n_dp
        scratch += [
            pltpu.VMEM((n1 - 1, lead, rows, width), jnp.bfloat16),
            pltpu.VMEM((lead, rows, width), jnp.bfloat16),
            pltpu.VMEM((lead, rows, width), jnp.float32),
            pltpu.VMEM((n2 - 1, 1, rows, width), jnp.bfloat16),
            pltpu.VMEM((1, rows, width), jnp.bfloat16),
        ]
    copies = 4 * (n_dp + n_t - 2)
    scratch += [pltpu.SemaphoreType.DMA((copies,)), pltpu.SemaphoreType.DMA((copies,))]
    return pl.pallas_call(
        functools.partial(moe_sum_kernel, n_dp, n_t, tuple(widths), tuple(order)),
        out_shape=jax.ShapeDtypeStruct((rows, model_width), jnp.bfloat16),
        in_specs=[pl.BlockSpec(memory_space=pltpu.VMEM)],
        out_specs=pl.BlockSpec(memory_space=pltpu.VMEM),
        scratch_shapes=scratch,
        compiler_params=pltpu.CompilerParams(
            collective_id=0, has_side_effects=True, vmem_limit_bytes=60 * 1024 * 1024
        ),
    )(partial)


def normalize(parts):
    highest = reduce(
        jnp.maximum,
        [
            jnp.max(jnp.where(visible, scores, -jnp.inf), axis=-1, keepdims=True)
            for scores, visible in parts
        ],
    )
    portions = [jnp.where(visible, jnp.exp(scores - highest), 0.0) for scores, visible in parts]
    denominator = reduce(
        jnp.add, [jnp.sum(portion, axis=-1, keepdims=True) for portion in portions]
    )
    return [(portion / denominator).astype(jnp.bfloat16) for portion in portions]


def attend(question_vectors, new_keys, new_values, key_pages, value_pages, table, spans):
    rows_all, head_count, head_width = question_vectors.shape
    kv_heads = new_keys.shape[1]
    group_size = head_count // kv_heads
    single_count = spans.shape[0] - 1
    page_count = table.shape[1]
    page_width = key_pages.shape[2]
    context = page_count * page_width
    inverse_root = 1.0 / math.sqrt(head_width)
    page_keys = key_pages[table]
    page_values = value_pages[table]
    grouped = question_vectors.reshape(rows_all, kv_heads, group_size, head_width)
    positions = jnp.arange(context, dtype=jnp.int32)
    single_q = grouped[:single_count]
    cache_dec = (
        jnp.einsum(
            "rkgh,rmkph->rkgmp",
            single_q,
            page_keys[:single_count],
            preferred_element_type=jnp.float32,
        ).reshape(single_count, kv_heads, group_size, context)
        * inverse_root
    )
    seen_dec = (positions[None, :] < spans[:single_count, None])[:, None, None, :]
    own_dec = (
        jnp.einsum(
            "rkgh,rkh->rkg", single_q, new_keys[:single_count], preferred_element_type=jnp.float32
        )[..., None]
        * inverse_root
    )
    weight_cache, weight_own = normalize(
        [(cache_dec, seen_dec), (own_dec, jnp.full(own_dec.shape, True))]
    )
    out_dec = jnp.einsum(
        "rkgmp,rmkph->rkgh",
        weight_cache.reshape(single_count, kv_heads, group_size, page_count, page_width),
        page_values[:single_count],
        preferred_element_type=jnp.float32,
    )
    out_dec = (
        out_dec
        + weight_own.astype(jnp.float32)
        * new_values[:single_count].astype(jnp.float32)[:, :, None, :]
    )
    prompt_q = grouped[single_count:]
    prompt_rows = rows_all - single_count
    cache_pro = (
        jnp.einsum(
            "rkgh,mkph->rkgmp",
            prompt_q,
            page_keys[single_count],
            preferred_element_type=jnp.float32,
        ).reshape(prompt_rows, kv_heads, group_size, context)
        * inverse_root
    )
    seen_pro = (positions < spans[single_count])[None, None, None, :]
    new_pro = (
        jnp.einsum(
            "rkgh,mkh->rkgm", prompt_q, new_keys[single_count:], preferred_element_type=jnp.float32
        )
        * inverse_root
    )
    prompt_index = jnp.arange(prompt_rows, dtype=jnp.int32)
    causal = (prompt_index[:, None] >= prompt_index[None, :])[:, None, None, :]
    weight_cpro, weight_npro = normalize([(cache_pro, seen_pro), (new_pro, causal)])
    out_pro = jnp.einsum(
        "rkgmp,mkph->rkgh",
        weight_cpro.reshape(prompt_rows, kv_heads, group_size, page_count, page_width),
        page_values[single_count],
        preferred_element_type=jnp.float32,
    )
    out_pro = out_pro + jnp.einsum(
        "rkgm,mkh->rkgh", weight_npro, new_values[single_count:], preferred_element_type=jnp.float32
    )
    joined = jnp.concatenate([out_dec, out_pro], axis=0).astype(jnp.bfloat16)
    return joined.reshape(rows_all, head_count * head_width)


def slot_table(member, ranking, keeping, slot_count):
    slot_hit = (
        ranking[:, :, None, None] == jnp.arange(slot_count, dtype=jnp.int32)[None, None, None, :]
    )
    return ((member[..., None] > 0) & keeping[:, :, None, None] & slot_hit).astype(jnp.bfloat16)


def expert_pass(send, gating_matrices, expand_matrices, contract_matrices):
    specialist_index, slot_count, model_width = send.shape
    local_count = gating_matrices.shape[0]
    flat = send.reshape(specialist_index * slot_count, model_width)
    arrived = lax.all_to_all(flat, "expert", split_axis=0, concat_axis=0, tiled=True)
    row_piece = row_gather(arrived, lax.axis_size("dp"), lax.axis_size("tensor"))
    assert local_count == 1
    gate_part = lax.dot_general(
        row_piece, gating_matrices[0], (((1,), (1,)), ((), ())), preferred_element_type=jnp.float32
    )
    up_part = lax.dot_general(
        row_piece, expand_matrices[0], (((1,), (1,)), ((), ())), preferred_element_type=jnp.float32
    )
    hidden = (jax.nn.silu(gate_part) * up_part).astype(jnp.bfloat16)
    partial_out = jnp.dot(
        hidden, contract_matrices[0], preferred_element_type=jnp.float32
    ).astype(jnp.bfloat16)
    n_dp, n_t = lax.axis_size("dp"), lax.axis_size("tensor")
    summed = moe_sum(partial_out.reshape(n_dp, n_t, -1, model_width), n_dp, n_t)
    arrived_back = lax.all_to_all(summed, "expert", split_axis=0, concat_axis=0, tiled=True)
    return arrived_back.reshape(specialist_index, slot_count, model_width)


def local(
    skip_stream_entry,
    question_vectors,
    fresh_lookup_vectors,
    fresh_content_vectors,
    stored_lookup_sheets,
    stored_content_sheets,
    sequence_sheet_map,
    stored_position_counts,
    attention_merge_matrix,
    premix_scale_factor,
    chosen_specialists,
    selection_shares,
    allowed_placements,
    favored_specialist,
    gating_matrices,
    expand_matrices,
    contract_matrices,
):
    token_count = chosen_specialists.shape[0]
    specialist_index = allowed_placements.shape[0]
    picked = (
        chosen_specialists[:, :, None]
        == jnp.arange(specialist_index, dtype=jnp.int32)[None, None, :]
    ).astype(jnp.int32)
    flat_routes = picked.reshape(token_count * 2, specialist_index)
    busiest_specialist = favored_specialist[0]
    before = (jnp.cumsum(flat_routes, axis=0) - flat_routes).reshape(
        token_count, 2, specialist_index
    )
    ranking = jnp.sum(before * picked, axis=2)
    placement_ceiling = jnp.where(
        jnp.arange(specialist_index, dtype=jnp.int32) == busiest_specialist,
        PLACEMENT_MOST,
        allowed_placements,
    )
    keeping = ranking < jnp.sum(picked * placement_ceiling[None, None, :], axis=2)
    row_total = question_vectors.shape[0]
    heads_out = attend(
        question_vectors.reshape(row_total, -1, HD),
        fresh_lookup_vectors.reshape(row_total, -1, HD),
        fresh_content_vectors.reshape(row_total, -1, HD),
        stored_lookup_sheets,
        stored_content_sheets,
        sequence_sheet_map,
        stored_position_counts,
    )
    own_attn = lax.psum_scatter(
        jnp.dot(heads_out, attention_merge_matrix, preferred_element_type=jnp.float32).astype(
            jnp.bfloat16
        ),
        "tensor",
        scatter_dimension=0,
        tiled=True,
    ).astype(jnp.float32)
    stream = (skip_stream_entry.astype(jnp.float32) + own_attn).astype(jnp.bfloat16)
    wide = stream.astype(jnp.float32)
    squares = jnp.mean(wide * wide, axis=1, keepdims=True)
    normed = (wide * lax.rsqrt(squares + 1e-05) * premix_scale_factor.astype(jnp.float32)).astype(
        jnp.bfloat16
    )
    main_slots = PLACEMENT_MOST
    table_main = slot_table(picked, ranking, keeping, main_slots)
    send = jnp.einsum(
        "nkes,nd->esd", table_main, normed, preferred_element_type=jnp.float32
    ).astype(jnp.bfloat16)
    expert_out = expert_pass(send, gating_matrices, expand_matrices, contract_matrices)
    chosen = jnp.einsum("nkes,esd->nkd", table_main, expert_out, preferred_element_type=jnp.float32)
    mixed = jnp.sum(selection_shares[:, :, None] * chosen, axis=1)
    return (wide + mixed).astype(jnp.bfloat16)


def solution(mesh):
    placed = (
        P(("dp", "expert", "tensor"), None),
        P(("dp", "expert"), "tensor"),
        P(("dp", "expert"), "tensor"),
        P(("dp", "expert"), "tensor"),
        P(("dp", "expert"), "tensor", None, None),
        P(("dp", "expert"), "tensor", None, None),
        P(("dp", "expert"), None),
        P(("dp", "expert")),
        P("tensor", None),
        P(),
        P(("dp", "expert", "tensor"), None),
        P(("dp", "expert", "tensor"), None),
        P(),
        P(),
        P("expert", ("dp", "tensor"), None),
        P("expert", ("dp", "tensor"), None),
        P("expert", ("dp", "tensor"), None),
    )
    return jax.shard_map(
        local,
        mesh=mesh,
        in_specs=placed,
        out_specs=P(("dp", "expert", "tensor"), None),
        check_vma=False,
    )
```

```python
from functools import reduce
import functools
import math

import jax
import jax.numpy as jnp
from jax import lax
from jax.experimental import pallas as pl
from jax.experimental.pallas import tpu as pltpu
from jax.sharding import PartitionSpec as P

HD = 128
PLACEMENT_MOST = 6


MESH_ID = pl.DeviceIdType.MESH


def plan_order(events, rate=50000.0, latency=1.5, per_step=0.3):
    ready = [0.0] * len(events)
    at = [0] * len(events)
    free = {}
    clock = 0.0
    order = []
    while True:
        live = [i for i in range(len(events)) if at[i] < len(events[i])]
        if not live:
            return order, clock
        i = min(live, key=lambda k: (ready[k], k))
        clock = max(clock, ready[i]) + per_step
        send = events[i][at[i]]
        if send is None:
            ready[i] = clock
        else:
            link, size = send
            start = max(clock, free.get(link, 0.0))
            free[link] = start + size / rate
            ready[i] = free[link] + latency
        order.append(i)
        at[i] += 1


def ring_events(n1, n2, link1, link2, size1, size2):
    return [(link1, size1)] * (n1 - 1) + [None] + [(link2, size2)] * (n2 - 1) + [None]


def split_plan(n_dp, n_t, rows, model_width, reduce):
    best = None
    for first_dp in range(128, model_width // 2, 128):
        widths = [first_dp, first_dp, model_width // 2 - first_dp, model_width // 2 - first_dp]
        events = []
        for block, width in enumerate(widths):
            unit = rows * width * 2
            sign = "+" if block % 2 == 0 else "-"
            if block < 2:
                big1, big2 = (n_t * unit, unit) if reduce else (unit, n_dp * unit)
                events.append(ring_events(n_dp, n_t, "z" + sign, "y" + sign, big1, big2))
            else:
                big1, big2 = (n_dp * unit, unit) if reduce else (unit, n_t * unit)
                events.append(ring_events(n_t, n_dp, "y" + sign, "z" + sign, big1, big2))
        order, finish = plan_order(events)
        if best is None or finish < best[0]:
            best = (finish, widths, order)
    return best[1], best[2]


def run_in_order(streams, order):
    for i in order:
        next(streams[i])
    for st in streams:
        for _ in st:
            pass


def ring_phase(n, me, step_to, own, chunk_lead, recv, send0, send_sems, recv_sems, first_sem, finish):
    copies = []
    for s in range(n - 1):
        c = lax.rem(me + n * 2 - step_to[1] * (s + 1), n)
        if s == 0:
            for i in range(chunk_lead):
                send0[i] = own(c, i).astype(send0.dtype)
            src = send0
        else:
            copies[-1].wait_recv()
            for i in range(chunk_lead):
                recv[s - 1, i] = (own(c, i) + recv[s - 1, i].astype(jnp.float32)).astype(recv.dtype)
            src = recv.at[s - 1]
        copy = pltpu.make_async_remote_copy(
            src_ref=src,
            dst_ref=recv.at[s],
            send_sem=send_sems.at[first_sem + s],
            recv_sem=recv_sems.at[first_sem + s],
            device_id=step_to[0],
            device_id_type=MESH_ID,
        )
        copy.start()
        copies.append(copy)
        yield copies
    copies[-1].wait_recv()
    for i in range(chunk_lead):
        finish(i, own(me, i) + recv[n - 2, i].astype(jnp.float32))
    yield copies


def block_product(h_ref, w_ref, chunk, cols, rows):
    start = pl.multiple_of(chunk * rows, 16)
    product = jnp.dot(h_ref[pl.ds(start, rows), :], w_ref[:, cols], preferred_element_type=jnp.float32)
    return product.astype(jnp.bfloat16).astype(jnp.float32)


def moe_sum_kernel(n_dp, n_t, widths, order, h_ref, w_ref, o_ref, *scratch):
    recv_sems, send_sems = scratch[-2], scratch[-1]
    bufs = scratch[:-2]
    me_dp = lax.axis_index("dp")
    me_t = lax.axis_index("tensor")
    me_e = lax.axis_index("expert")

    def dp_dev(d):
        return (lax.rem(me_dp + n_dp + d, n_dp), me_e, me_t)

    def t_dev(d):
        return (me_dp, me_e, lax.rem(me_t + n_t + d, n_t))

    barrier = pltpu.get_barrier_semaphore()
    for dev in (dp_dev(1), dp_dev(-1), t_dev(1), t_dev(-1)):
        pl.semaphore_signal(barrier, 1, device_id=dev, device_id_type=MESH_ID)
    pl.semaphore_wait(barrier, 4)

    streams = []
    sem_at = 0
    for block in range(4):
        cols = pl.ds(sum(widths[:block]), widths[block])
        direction = 1 if block % 2 == 0 else -1
        r1, s1, acc, r2, s2 = bufs[block * 5: block * 5 + 5]
        if block < 2:
            first = (n_dp, me_dp, (dp_dev(direction), direction), n_t)
            own1 = lambda c, i, cols=cols: block_product(h_ref, w_ref, c * n_t + i, cols, o_ref.shape[0])
            second = (n_t, me_t, (t_dev(direction), direction))
        else:
            first = (n_t, me_t, (t_dev(direction), direction), n_dp)
            own1 = lambda c, i, cols=cols: block_product(h_ref, w_ref, i * n_t + c, cols, o_ref.shape[0])
            second = (n_dp, me_dp, (dp_dev(direction), direction))

        def fin1(i, v, acc=acc):
            acc[i] = v

        def fin2(i, v, cols=cols):
            o_ref[:, cols] = v.astype(o_ref.dtype)

        own2 = lambda c, i, acc=acc: acc[c]

        def stream(first=first, second=second, own1=own1, own2=own2, r1=r1, s1=s1, r2=r2, s2=s2,
                   fin1=fin1, fin2=fin2, base=sem_at):
            n1, me1, to1, lead = first
            copies = []
            for copies in ring_phase(n1, me1, to1, own1, lead, r1, s1, send_sems, recv_sems, base, fin1):
                yield
            done1 = copies
            n2, me2, to2 = second
            for copies in ring_phase(n2, me2, to2, own2, 1, r2, s2, send_sems, recv_sems, base + n1 - 1,
                                     lambda i, v: fin2(i, v)):
                yield
            for copy in done1 + copies:
                copy.wait_send()

        streams.append(stream())
        sem_at += n_dp + n_t - 2

    run_in_order(streams, order)


def gather_phase(n, me, step_to, chunk, send_sems, recv_sems, first_sem):
    copies = []
    for s in range(n - 1):
        c = lax.rem(me + n * 2 - step_to[1] * s, n)
        if s > 0:
            copies[-1].wait_recv()
        copy = pltpu.make_async_remote_copy(
            src_ref=chunk(c),
            dst_ref=chunk(c),
            send_sem=send_sems.at[first_sem + s],
            recv_sem=recv_sems.at[first_sem + s],
            device_id=step_to[0],
            device_id_type=MESH_ID,
        )
        copy.start()
        copies.append(copy)
        yield copies
    copies[-1].wait_recv()
    yield copies


def row_gather_kernel(n_dp, n_t, widths, order, x_ref, o_ref, *scratch):
    recv_sems, send_sems = scratch[-2], scratch[-1]
    bufs = scratch[:-2]
    me_dp = lax.axis_index("dp")
    me_t = lax.axis_index("tensor")
    me_e = lax.axis_index("expert")
    rows = x_ref.shape[0]

    def dp_dev(d):
        return (lax.rem(me_dp + n_dp + d, n_dp), me_e, me_t)

    def t_dev(d):
        return (me_dp, me_e, lax.rem(me_t + n_t + d, n_t))

    for block in range(4):
        cols = pl.ds(sum(widths[:block]), widths[block])
        if block < 2:
            bufs[block][me_t, me_dp] = x_ref[:, cols]
        else:
            bufs[block][me_dp, me_t] = x_ref[:, cols]

    barrier = pltpu.get_barrier_semaphore()
    for dev in (dp_dev(1), dp_dev(-1), t_dev(1), t_dev(-1)):
        pl.semaphore_signal(barrier, 1, device_id=dev, device_id_type=MESH_ID)
    pl.semaphore_wait(barrier, 4)

    streams = []
    sem_at = 0
    for block in range(4):
        direction = 1 if block % 2 == 0 else -1
        g = bufs[block]
        if block < 2:
            first = (n_dp, me_dp, (dp_dev(direction), direction), lambda c, g=g: g.at[me_t, c])
            second = (n_t, me_t, (t_dev(direction), direction), lambda c, g=g: g.at[c])
        else:
            first = (n_t, me_t, (t_dev(direction), direction), lambda c, g=g: g.at[me_dp, c])
            second = (n_dp, me_dp, (dp_dev(direction), direction), lambda c, g=g: g.at[c])

        def stream(first=first, second=second, base=sem_at):
            n1, me1, to1, chunk1 = first
            copies = []
            for copies in gather_phase(n1, me1, to1, chunk1, send_sems, recv_sems, base):
                yield
            done1 = copies
            n2, me2, to2, chunk2 = second
            for copies in gather_phase(n2, me2, to2, chunk2, send_sems, recv_sems, base + n1 - 1):
                yield
            for copy in done1 + copies:
                copy.wait_send()

        streams.append(stream())
        sem_at += n_dp + n_t - 2

    run_in_order(streams, order)

    for block in range(4):
        cols = pl.ds(sum(widths[:block]), widths[block])
        for d in range(n_dp):
            for t in range(n_t):
                piece = bufs[block][t, d] if block < 2 else bufs[block][d, t]
                o_ref[pl.ds((d * n_t + t) * rows, rows), cols] = piece


def row_gather(x, n_dp, n_t):
    rows, model_width = x.shape
    widths, order = split_plan(n_dp, n_t, rows, model_width, False)
    scratch = [
        pltpu.VMEM((n_t, n_dp, rows, widths[0]), jnp.bfloat16),
        pltpu.VMEM((n_t, n_dp, rows, widths[1]), jnp.bfloat16),
        pltpu.VMEM((n_dp, n_t, rows, widths[2]), jnp.bfloat16),
        pltpu.VMEM((n_dp, n_t, rows, widths[3]), jnp.bfloat16),
    ]
    copies = 4 * (n_dp + n_t - 2)
    scratch += [pltpu.SemaphoreType.DMA((copies,)), pltpu.SemaphoreType.DMA((copies,))]
    return pl.pallas_call(
        functools.partial(row_gather_kernel, n_dp, n_t, tuple(widths), tuple(order)),
        out_shape=jax.ShapeDtypeStruct((n_dp * n_t * rows, model_width), jnp.bfloat16),
        in_specs=[pl.BlockSpec(memory_space=pltpu.VMEM)],
        out_specs=pl.BlockSpec(memory_space=pltpu.VMEM),
        scratch_shapes=scratch,
        compiler_params=pltpu.CompilerParams(
            collective_id=1, has_side_effects=True, vmem_limit_bytes=60 * 1024 * 1024
        ),
    )(x)


def moe_sum(hidden, down, n_dp, n_t):
    rows, model_width = hidden.shape[0] // (n_dp * n_t), down.shape[1]
    widths, order = split_plan(n_dp, n_t, rows, model_width, True)
    scratch = []
    for block in range(4):
        width = widths[block]
        if block < 2:
            n1, lead, n2 = n_dp, n_t, n_t
        else:
            n1, lead, n2 = n_t, n_dp, n_dp
        scratch += [
            pltpu.VMEM((n1 - 1, lead, rows, width), jnp.bfloat16),
            pltpu.VMEM((lead, rows, width), jnp.bfloat16),
            pltpu.VMEM((lead, rows, width), jnp.float32),
            pltpu.VMEM((n2 - 1, 1, rows, width), jnp.bfloat16),
            pltpu.VMEM((1, rows, width), jnp.bfloat16),
        ]
    copies = 4 * (n_dp + n_t - 2)
    scratch += [pltpu.SemaphoreType.DMA((copies,)), pltpu.SemaphoreType.DMA((copies,))]
    return pl.pallas_call(
        functools.partial(moe_sum_kernel, n_dp, n_t, tuple(widths), tuple(order)),
        out_shape=jax.ShapeDtypeStruct((rows, model_width), jnp.bfloat16),
        in_specs=[pl.BlockSpec(memory_space=pltpu.VMEM)] * 2,
        out_specs=pl.BlockSpec(memory_space=pltpu.VMEM),
        scratch_shapes=scratch,
        compiler_params=pltpu.CompilerParams(
            collective_id=0, has_side_effects=True, vmem_limit_bytes=60 * 1024 * 1024
        ),
    )(hidden, down)


def normalize(parts):
    highest = reduce(
        jnp.maximum,
        [
            jnp.max(jnp.where(visible, scores, -jnp.inf), axis=-1, keepdims=True)
            for scores, visible in parts
        ],
    )
    portions = [jnp.where(visible, jnp.exp(scores - highest), 0.0) for scores, visible in parts]
    denominator = reduce(
        jnp.add, [jnp.sum(portion, axis=-1, keepdims=True) for portion in portions]
    )
    return [(portion / denominator).astype(jnp.bfloat16) for portion in portions]


def attend(question_vectors, new_keys, new_values, key_pages, value_pages, table, spans):
    rows_all, head_count, head_width = question_vectors.shape
    kv_heads = new_keys.shape[1]
    group_size = head_count // kv_heads
    single_count = spans.shape[0] - 1
    page_count = table.shape[1]
    page_width = key_pages.shape[2]
    context = page_count * page_width
    inverse_root = 1.0 / math.sqrt(head_width)
    page_keys = key_pages[table]
    page_values = value_pages[table]
    grouped = question_vectors.reshape(rows_all, kv_heads, group_size, head_width)
    positions = jnp.arange(context, dtype=jnp.int32)
    single_q = grouped[:single_count]
    cache_dec = (
        jnp.einsum(
            "rkgh,rmkph->rkgmp",
            single_q,
            page_keys[:single_count],
            preferred_element_type=jnp.float32,
        ).reshape(single_count, kv_heads, group_size, context)
        * inverse_root
    )
    seen_dec = (positions[None, :] < spans[:single_count, None])[:, None, None, :]
    own_dec = (
        jnp.einsum(
            "rkgh,rkh->rkg", single_q, new_keys[:single_count], preferred_element_type=jnp.float32
        )[..., None]
        * inverse_root
    )
    weight_cache, weight_own = normalize(
        [(cache_dec, seen_dec), (own_dec, jnp.full(own_dec.shape, True))]
    )
    out_dec = jnp.einsum(
        "rkgmp,rmkph->rkgh",
        weight_cache.reshape(single_count, kv_heads, group_size, page_count, page_width),
        page_values[:single_count],
        preferred_element_type=jnp.float32,
    )
    out_dec = (
        out_dec
        + weight_own.astype(jnp.float32)
        * new_values[:single_count].astype(jnp.float32)[:, :, None, :]
    )
    prompt_q = grouped[single_count:]
    prompt_rows = rows_all - single_count
    cache_pro = (
        jnp.einsum(
            "rkgh,mkph->rkgmp",
            prompt_q,
            page_keys[single_count],
            preferred_element_type=jnp.float32,
        ).reshape(prompt_rows, kv_heads, group_size, context)
        * inverse_root
    )
    seen_pro = (positions < spans[single_count])[None, None, None, :]
    new_pro = (
        jnp.einsum(
            "rkgh,mkh->rkgm", prompt_q, new_keys[single_count:], preferred_element_type=jnp.float32
        )
        * inverse_root
    )
    prompt_index = jnp.arange(prompt_rows, dtype=jnp.int32)
    causal = (prompt_index[:, None] >= prompt_index[None, :])[:, None, None, :]
    weight_cpro, weight_npro = normalize([(cache_pro, seen_pro), (new_pro, causal)])
    out_pro = jnp.einsum(
        "rkgmp,mkph->rkgh",
        weight_cpro.reshape(prompt_rows, kv_heads, group_size, page_count, page_width),
        page_values[single_count],
        preferred_element_type=jnp.float32,
    )
    out_pro = out_pro + jnp.einsum(
        "rkgm,mkh->rkgh", weight_npro, new_values[single_count:], preferred_element_type=jnp.float32
    )
    joined = jnp.concatenate([out_dec, out_pro], axis=0).astype(jnp.bfloat16)
    return joined.reshape(rows_all, head_count * head_width)


def slot_table(member, ranking, keeping, slot_count):
    slot_hit = (
        ranking[:, :, None, None] == jnp.arange(slot_count, dtype=jnp.int32)[None, None, None, :]
    )
    return ((member[..., None] > 0) & keeping[:, :, None, None] & slot_hit).astype(jnp.bfloat16)


def expert_pass(send, gating_matrices, expand_matrices, contract_matrices):
    specialist_index, slot_count, model_width = send.shape
    local_count = gating_matrices.shape[0]
    flat = send.reshape(specialist_index * slot_count, model_width)
    arrived = lax.all_to_all(flat, "expert", split_axis=0, concat_axis=0, tiled=True)
    row_piece = row_gather(arrived, lax.axis_size("dp"), lax.axis_size("tensor"))
    assert local_count == 1
    gate_part = lax.dot_general(
        row_piece, gating_matrices[0], (((1,), (1,)), ((), ())), preferred_element_type=jnp.float32
    )
    up_part = lax.dot_general(
        row_piece, expand_matrices[0], (((1,), (1,)), ((), ())), preferred_element_type=jnp.float32
    )
    hidden = (jax.nn.silu(gate_part) * up_part).astype(jnp.bfloat16)
    inner = hidden.shape[1]
    padded = -(-inner // 128) * 128
    hidden = jnp.pad(hidden, ((0, 0), (0, padded - inner)))
    down = jnp.pad(contract_matrices[0], ((0, padded - inner), (0, 0)))
    n_dp, n_t = lax.axis_size("dp"), lax.axis_size("tensor")
    summed = moe_sum(hidden, down, n_dp, n_t)
    arrived_back = lax.all_to_all(summed, "expert", split_axis=0, concat_axis=0, tiled=True)
    return arrived_back.reshape(specialist_index, slot_count, model_width)


def local(
    skip_stream_entry,
    question_vectors,
    fresh_lookup_vectors,
    fresh_content_vectors,
    stored_lookup_sheets,
    stored_content_sheets,
    sequence_sheet_map,
    stored_position_counts,
    attention_merge_matrix,
    premix_scale_factor,
    chosen_specialists,
    selection_shares,
    allowed_placements,
    favored_specialist,
    gating_matrices,
    expand_matrices,
    contract_matrices,
):
    token_count = chosen_specialists.shape[0]
    specialist_index = allowed_placements.shape[0]
    picked = (
        chosen_specialists[:, :, None]
        == jnp.arange(specialist_index, dtype=jnp.int32)[None, None, :]
    ).astype(jnp.int32)
    flat_routes = picked.reshape(token_count * 2, specialist_index)
    busiest_specialist = favored_specialist[0]
    before = (jnp.cumsum(flat_routes, axis=0) - flat_routes).reshape(
        token_count, 2, specialist_index
    )
    ranking = jnp.sum(before * picked, axis=2)
    placement_ceiling = jnp.where(
        jnp.arange(specialist_index, dtype=jnp.int32) == busiest_specialist,
        PLACEMENT_MOST,
        allowed_placements,
    )
    keeping = ranking < jnp.sum(picked * placement_ceiling[None, None, :], axis=2)
    row_total = question_vectors.shape[0]
    heads_out = attend(
        question_vectors.reshape(row_total, -1, HD),
        fresh_lookup_vectors.reshape(row_total, -1, HD),
        fresh_content_vectors.reshape(row_total, -1, HD),
        stored_lookup_sheets,
        stored_content_sheets,
        sequence_sheet_map,
        stored_position_counts,
    )
    own_attn = lax.psum_scatter(
        jnp.dot(heads_out, attention_merge_matrix, preferred_element_type=jnp.float32).astype(
            jnp.bfloat16
        ),
        "tensor",
        scatter_dimension=0,
        tiled=True,
    ).astype(jnp.float32)
    stream = (skip_stream_entry.astype(jnp.float32) + own_attn).astype(jnp.bfloat16)
    wide = stream.astype(jnp.float32)
    squares = jnp.mean(wide * wide, axis=1, keepdims=True)
    normed = (wide * lax.rsqrt(squares + 1e-05) * premix_scale_factor.astype(jnp.float32)).astype(
        jnp.bfloat16
    )
    main_slots = PLACEMENT_MOST
    table_main = slot_table(picked, ranking, keeping, main_slots)
    send = jnp.einsum(
        "nkes,nd->esd", table_main, normed, preferred_element_type=jnp.float32
    ).astype(jnp.bfloat16)
    expert_out = expert_pass(send, gating_matrices, expand_matrices, contract_matrices)
    chosen = jnp.einsum("nkes,esd->nkd", table_main, expert_out, preferred_element_type=jnp.float32)
    mixed = jnp.sum(selection_shares[:, :, None] * chosen, axis=1)
    return (wide + mixed).astype(jnp.bfloat16)


def solution(mesh):
    placed = (
        P(("dp", "expert", "tensor"), None),
        P(("dp", "expert"), "tensor"),
        P(("dp", "expert"), "tensor"),
        P(("dp", "expert"), "tensor"),
        P(("dp", "expert"), "tensor", None, None),
        P(("dp", "expert"), "tensor", None, None),
        P(("dp", "expert"), None),
        P(("dp", "expert")),
        P("tensor", None),
        P(),
        P(("dp", "expert", "tensor"), None),
        P(("dp", "expert", "tensor"), None),
        P(),
        P(),
        P("expert", ("dp", "tensor"), None),
        P("expert", ("dp", "tensor"), None),
        P("expert", ("dp", "tensor"), None),
    )
    return jax.shard_map(
        local,
        mesh=mesh,
        in_specs=placed,
        out_specs=P(("dp", "expert", "tensor"), None),
        check_vma=False,
    )
```

```python
from functools import reduce
import functools
import math

import jax
import jax.numpy as jnp
from jax import lax
from jax.experimental import pallas as pl
from jax.experimental.pallas import tpu as pltpu
from jax.sharding import PartitionSpec as P

HD = 128
PLACEMENT_MOST = 6


MESH_ID = pl.DeviceIdType.MESH


def plan_order(events, rate=50000.0, latency=1.5, per_step=0.3):
    ready = [0.0] * len(events)
    at = [0] * len(events)
    free = {}
    clock = 0.0
    order = []
    while True:
        live = [i for i in range(len(events)) if at[i] < len(events[i])]
        if not live:
            return order, clock
        i = min(live, key=lambda k: (ready[k], k))
        clock = max(clock, ready[i]) + per_step
        send = events[i][at[i]]
        if send is None:
            ready[i] = clock
        else:
            link, size = send
            start = max(clock, free.get(link, 0.0))
            free[link] = start + size / rate
            ready[i] = free[link] + latency
        order.append(i)
        at[i] += 1


def ring_events(n1, n2, link1, link2, size1, size2):
    return [(link1, size1)] * (n1 - 1) + [None] + [(link2, size2)] * (n2 - 1) + [None]


def split_plan(n_dp, n_t, rows, model_width, reduce):
    best = None
    for first_dp in range(128, model_width // 2, 128):
        widths = [first_dp, first_dp, model_width // 2 - first_dp, model_width // 2 - first_dp]
        events = []
        for block, width in enumerate(widths):
            unit = rows * width * 2
            sign = "+" if block % 2 == 0 else "-"
            if block < 2:
                big1, big2 = (n_t * unit, unit) if reduce else (unit, n_dp * unit)
                events.append(ring_events(n_dp, n_t, "z" + sign, "y" + sign, big1, big2))
            else:
                big1, big2 = (n_dp * unit, unit) if reduce else (unit, n_t * unit)
                events.append(ring_events(n_t, n_dp, "y" + sign, "z" + sign, big1, big2))
        order, finish = plan_order(events)
        if best is None or finish < best[0]:
            best = (finish, widths, order)
    return best[1], best[2]


def run_in_order(streams, order):
    for i in order:
        next(streams[i])
    for st in streams:
        for _ in st:
            pass


def ring_phase(n, me, step_to, own, chunk_lead, recv, send0, send_sems, recv_sems, first_sem, finish):
    copies = []
    for s in range(n - 1):
        c = lax.rem(me + n * 2 - step_to[1] * (s + 1), n)
        if s == 0:
            for i in range(chunk_lead):
                send0[i] = own(c, i).astype(send0.dtype)
            src = send0
        else:
            copies[-1].wait_recv()
            for i in range(chunk_lead):
                recv[s - 1, i] = (own(c, i) + recv[s - 1, i].astype(jnp.float32)).astype(recv.dtype)
            src = recv.at[s - 1]
        copy = pltpu.make_async_remote_copy(
            src_ref=src,
            dst_ref=recv.at[s],
            send_sem=send_sems.at[first_sem + s],
            recv_sem=recv_sems.at[first_sem + s],
            device_id=step_to[0],
            device_id_type=MESH_ID,
        )
        copy.start()
        copies.append(copy)
        yield copies
    copies[-1].wait_recv()
    for i in range(chunk_lead):
        finish(i, own(me, i) + recv[n - 2, i].astype(jnp.float32))
    yield copies


def block_product(h_ref, w_ref, chunk, cols, rows):
    start = pl.multiple_of(chunk * rows, 16)
    product = jnp.dot(h_ref[pl.ds(start, rows), :], w_ref[:, cols], preferred_element_type=jnp.float32)
    return product.astype(jnp.bfloat16).astype(jnp.float32)


def moe_sum_kernel(n_dp, n_t, widths, order, h_ref, w_ref, o_ref, *scratch):
    recv_sems, send_sems = scratch[-2], scratch[-1]
    bufs = scratch[:-2]
    me_dp = lax.axis_index("dp")
    me_t = lax.axis_index("tensor")
    me_e = lax.axis_index("expert")

    def dp_dev(d):
        return (lax.rem(me_dp + n_dp + d, n_dp), me_e, me_t)

    def t_dev(d):
        return (me_dp, me_e, lax.rem(me_t + n_t + d, n_t))

    barrier = pltpu.get_barrier_semaphore()
    for dev in (dp_dev(1), dp_dev(-1), t_dev(1), t_dev(-1)):
        pl.semaphore_signal(barrier, 1, device_id=dev, device_id_type=MESH_ID)
    pl.semaphore_wait(barrier, 4)

    streams = []
    sem_at = 0
    for block in range(4):
        cols = pl.ds(sum(widths[:block]), widths[block])
        direction = 1 if block % 2 == 0 else -1
        r1, s1, acc, r2, s2 = bufs[block * 5: block * 5 + 5]
        if block < 2:
            first = (n_dp, me_dp, (dp_dev(direction), direction), n_t)
            own1 = lambda c, i, cols=cols: block_product(h_ref, w_ref, c * n_t + i, cols, o_ref.shape[0])
            second = (n_t, me_t, (t_dev(direction), direction))
        else:
            first = (n_t, me_t, (t_dev(direction), direction), n_dp)
            own1 = lambda c, i, cols=cols: block_product(h_ref, w_ref, i * n_t + c, cols, o_ref.shape[0])
            second = (n_dp, me_dp, (dp_dev(direction), direction))

        def fin1(i, v, acc=acc):
            acc[i] = v

        def fin2(i, v, cols=cols):
            o_ref[:, cols] = v.astype(o_ref.dtype)

        own2 = lambda c, i, acc=acc: acc[c]

        def stream(first=first, second=second, own1=own1, own2=own2, r1=r1, s1=s1, r2=r2, s2=s2,
                   fin1=fin1, fin2=fin2, base=sem_at):
            n1, me1, to1, lead = first
            copies = []
            for copies in ring_phase(n1, me1, to1, own1, lead, r1, s1, send_sems, recv_sems, base, fin1):
                yield
            done1 = copies
            n2, me2, to2 = second
            for copies in ring_phase(n2, me2, to2, own2, 1, r2, s2, send_sems, recv_sems, base + n1 - 1,
                                     lambda i, v: fin2(i, v)):
                yield
            for copy in done1 + copies:
                copy.wait_send()

        streams.append(stream())
        sem_at += n_dp + n_t - 2

    run_in_order(streams, order)


def gather_phase(n, me, step_to, chunk, send_sems, recv_sems, first_sem):
    copies = []
    for s in range(n - 1):
        c = lax.rem(me + n * 2 - step_to[1] * s, n)
        if s > 0:
            copies[-1].wait_recv()
        copy = pltpu.make_async_remote_copy(
            src_ref=chunk(c),
            dst_ref=chunk(c),
            send_sem=send_sems.at[first_sem + s],
            recv_sem=recv_sems.at[first_sem + s],
            device_id=step_to[0],
            device_id_type=MESH_ID,
        )
        copy.start()
        copies.append(copy)
        yield copies
    copies[-1].wait_recv()
    yield copies


def row_gather_kernel(n_dp, n_t, widths, order, x_ref, o_ref, *scratch):
    recv_sems, send_sems = scratch[-2], scratch[-1]
    bufs = scratch[:-2]
    me_dp = lax.axis_index("dp")
    me_t = lax.axis_index("tensor")
    me_e = lax.axis_index("expert")
    rows = x_ref.shape[0]

    def dp_dev(d):
        return (lax.rem(me_dp + n_dp + d, n_dp), me_e, me_t)

    def t_dev(d):
        return (me_dp, me_e, lax.rem(me_t + n_t + d, n_t))

    for block in range(4):
        cols = pl.ds(sum(widths[:block]), widths[block])
        if block < 2:
            bufs[block][me_t, me_dp] = x_ref[:, cols]
        else:
            bufs[block][me_dp, me_t] = x_ref[:, cols]

    barrier = pltpu.get_barrier_semaphore()
    for dev in (dp_dev(1), dp_dev(-1), t_dev(1), t_dev(-1)):
        pl.semaphore_signal(barrier, 1, device_id=dev, device_id_type=MESH_ID)
    pl.semaphore_wait(barrier, 4)

    streams = []
    sem_at = 0
    for block in range(4):
        direction = 1 if block % 2 == 0 else -1
        g = bufs[block]
        if block < 2:
            first = (n_dp, me_dp, (dp_dev(direction), direction), lambda c, g=g: g.at[me_t, c])
            second = (n_t, me_t, (t_dev(direction), direction), lambda c, g=g: g.at[c])
        else:
            first = (n_t, me_t, (t_dev(direction), direction), lambda c, g=g: g.at[me_dp, c])
            second = (n_dp, me_dp, (dp_dev(direction), direction), lambda c, g=g: g.at[c])

        def stream(first=first, second=second, base=sem_at):
            n1, me1, to1, chunk1 = first
            copies = []
            for copies in gather_phase(n1, me1, to1, chunk1, send_sems, recv_sems, base):
                yield
            done1 = copies
            n2, me2, to2, chunk2 = second
            for copies in gather_phase(n2, me2, to2, chunk2, send_sems, recv_sems, base + n1 - 1):
                yield
            for copy in done1 + copies:
                copy.wait_send()

        streams.append(stream())
        sem_at += n_dp + n_t - 2

    run_in_order(streams, order)

    for block in range(4):
        cols = pl.ds(sum(widths[:block]), widths[block])
        for d in range(n_dp):
            for t in range(n_t):
                piece = bufs[block][t, d] if block < 2 else bufs[block][d, t]
                o_ref[pl.ds((d * n_t + t) * rows, rows), cols] = piece


def row_gather(x, n_dp, n_t):
    rows, model_width = x.shape
    widths, order = split_plan(n_dp, n_t, rows, model_width, False)
    scratch = [
        pltpu.VMEM((n_t, n_dp, rows, widths[0]), jnp.bfloat16),
        pltpu.VMEM((n_t, n_dp, rows, widths[1]), jnp.bfloat16),
        pltpu.VMEM((n_dp, n_t, rows, widths[2]), jnp.bfloat16),
        pltpu.VMEM((n_dp, n_t, rows, widths[3]), jnp.bfloat16),
    ]
    copies = 4 * (n_dp + n_t - 2)
    scratch += [pltpu.SemaphoreType.DMA((copies,)), pltpu.SemaphoreType.DMA((copies,))]
    return pl.pallas_call(
        functools.partial(row_gather_kernel, n_dp, n_t, tuple(widths), tuple(order)),
        out_shape=jax.ShapeDtypeStruct((n_dp * n_t * rows, model_width), jnp.bfloat16),
        in_specs=[pl.BlockSpec(memory_space=pltpu.VMEM)],
        out_specs=pl.BlockSpec(memory_space=pltpu.VMEM),
        scratch_shapes=scratch,
        compiler_params=pltpu.CompilerParams(
            collective_id=1, has_side_effects=True, vmem_limit_bytes=60 * 1024 * 1024
        ),
    )(x)


def head_sum_kernel(n_t, x_ref, o_ref, recv0, send0, recv1, send1, recv_sems, send_sems):
    me_dp = lax.axis_index("dp")
    me_e = lax.axis_index("expert")
    me_t = lax.axis_index("tensor")
    rows = o_ref.shape[0]
    width = o_ref.shape[1] // 2

    def t_dev(d):
        return (me_dp, me_e, lax.rem(me_t + n_t + d, n_t))

    barrier = pltpu.get_barrier_semaphore()
    for dev in (t_dev(1), t_dev(-1)):
        pl.semaphore_signal(barrier, 1, device_id=dev, device_id_type=MESH_ID)
    pl.semaphore_wait(barrier, 2)
    streams = []
    for block, (recv, send0_buf) in enumerate(((recv0, send0), (recv1, send1))):
        cols = pl.ds(block * width, width)
        direction = 1 if block == 0 else -1
        own = lambda c, i, cols=cols: x_ref[pl.ds(pl.multiple_of(c * rows, 8), rows), cols].astype(jnp.float32)

        def finish(i, v, cols=cols):
            o_ref[:, cols] = v.astype(o_ref.dtype)

        def stream(own=own, recv=recv, send0_buf=send0_buf, finish=finish, direction=direction, base=block):
            copies = []
            for copies in ring_phase(n_t, me_t, (t_dev(direction), direction), own, 1, recv, send0_buf,
                                     send_sems, recv_sems, base * (n_t - 1), finish):
                yield
            for copy in copies:
                copy.wait_send()

        streams.append(stream())
    run_in_order(streams, [0, 1] * n_t)


def head_sum(x, n_t):
    rows, model_width = x.shape[0] // n_t, x.shape[1]
    width = model_width // 2
    scratch = []
    for _ in range(2):
        scratch += [
            pltpu.VMEM((n_t - 1, 1, rows, width), jnp.bfloat16),
            pltpu.VMEM((1, rows, width), jnp.bfloat16),
        ]
    copies = 2 * (n_t - 1)
    scratch += [pltpu.SemaphoreType.DMA((copies,)), pltpu.SemaphoreType.DMA((copies,))]
    return pl.pallas_call(
        functools.partial(head_sum_kernel, n_t),
        out_shape=jax.ShapeDtypeStruct((rows, model_width), jnp.bfloat16),
        in_specs=[pl.BlockSpec(memory_space=pltpu.VMEM)],
        out_specs=pl.BlockSpec(memory_space=pltpu.VMEM),
        scratch_shapes=scratch,
        compiler_params=pltpu.CompilerParams(collective_id=2, has_side_effects=True),
    )(x)


def expert_exchange_kernel(n_e, x_ref, o_ref, recv, recv_sems, send_sems):
    me_dp = lax.axis_index("dp")
    me_e = lax.axis_index("expert")
    me_t = lax.axis_index("tensor")
    barrier = pltpu.get_barrier_semaphore()
    for k in range(1, n_e):
        pl.semaphore_signal(barrier, 1, device_id=(me_dp, lax.rem(me_e + k, n_e), me_t),
                            device_id_type=MESH_ID)
    pl.semaphore_wait(barrier, n_e - 1)
    copies = []
    for k in range(1, n_e):
        target = lax.rem(me_e + k, n_e)
        copy = pltpu.make_async_remote_copy(
            src_ref=x_ref.at[target],
            dst_ref=recv.at[me_e],
            send_sem=send_sems.at[k - 1],
            recv_sem=recv_sems.at[k - 1],
            device_id=(me_dp, target, me_t),
            device_id_type=MESH_ID,
        )
        copy.start()
        copies.append(copy)
    o_ref[me_e] = x_ref[me_e]
    for k in range(1, n_e):
        copies[k - 1].wait_recv()
        source = lax.rem(me_e + n_e - k, n_e)
        o_ref[source] = recv[source]
    for copy in copies:
        copy.wait_send()


def expert_exchange(x, collective):
    n_e = x.shape[0]
    return pl.pallas_call(
        functools.partial(expert_exchange_kernel, n_e),
        out_shape=jax.ShapeDtypeStruct(x.shape, x.dtype),
        in_specs=[pl.BlockSpec(memory_space=pltpu.VMEM)],
        out_specs=pl.BlockSpec(memory_space=pltpu.VMEM),
        scratch_shapes=[
            pltpu.VMEM(x.shape, x.dtype),
            pltpu.SemaphoreType.DMA((n_e - 1,)),
            pltpu.SemaphoreType.DMA((n_e - 1,)),
        ],
        compiler_params=pltpu.CompilerParams(collective_id=collective, has_side_effects=True),
    )(x)


def moe_sum(hidden, down, n_dp, n_t):
    rows, model_width = hidden.shape[0] // (n_dp * n_t), down.shape[1]
    widths, order = split_plan(n_dp, n_t, rows, model_width, True)
    scratch = []
    for block in range(4):
        width = widths[block]
        if block < 2:
            n1, lead, n2 = n_dp, n_t, n_t
        else:
            n1, lead, n2 = n_t, n_dp, n_dp
        scratch += [
            pltpu.VMEM((n1 - 1, lead, rows, width), jnp.bfloat16),
            pltpu.VMEM((lead, rows, width), jnp.bfloat16),
            pltpu.VMEM((lead, rows, width), jnp.float32),
            pltpu.VMEM((n2 - 1, 1, rows, width), jnp.bfloat16),
            pltpu.VMEM((1, rows, width), jnp.bfloat16),
        ]
    copies = 4 * (n_dp + n_t - 2)
    scratch += [pltpu.SemaphoreType.DMA((copies,)), pltpu.SemaphoreType.DMA((copies,))]
    return pl.pallas_call(
        functools.partial(moe_sum_kernel, n_dp, n_t, tuple(widths), tuple(order)),
        out_shape=jax.ShapeDtypeStruct((rows, model_width), jnp.bfloat16),
        in_specs=[pl.BlockSpec(memory_space=pltpu.VMEM)] * 2,
        out_specs=pl.BlockSpec(memory_space=pltpu.VMEM),
        scratch_shapes=scratch,
        compiler_params=pltpu.CompilerParams(
            collective_id=0, has_side_effects=True, vmem_limit_bytes=60 * 1024 * 1024
        ),
    )(hidden, down)


def normalize(parts):
    highest = reduce(
        jnp.maximum,
        [
            jnp.max(jnp.where(visible, scores, -jnp.inf), axis=-1, keepdims=True)
            for scores, visible in parts
        ],
    )
    portions = [jnp.where(visible, jnp.exp(scores - highest), 0.0) for scores, visible in parts]
    denominator = reduce(
        jnp.add, [jnp.sum(portion, axis=-1, keepdims=True) for portion in portions]
    )
    return [(portion / denominator).astype(jnp.bfloat16) for portion in portions]


def attend(question_vectors, new_keys, new_values, key_pages, value_pages, table, spans):
    rows_all, head_count, head_width = question_vectors.shape
    kv_heads = new_keys.shape[1]
    group_size = head_count // kv_heads
    single_count = spans.shape[0] - 1
    page_count = table.shape[1]
    page_width = key_pages.shape[2]
    context = page_count * page_width
    inverse_root = 1.0 / math.sqrt(head_width)
    page_keys = key_pages[table]
    page_values = value_pages[table]
    grouped = question_vectors.reshape(rows_all, kv_heads, group_size, head_width)
    positions = jnp.arange(context, dtype=jnp.int32)
    single_q = grouped[:single_count]
    cache_dec = (
        jnp.einsum(
            "rkgh,rmkph->rkgmp",
            single_q,
            page_keys[:single_count],
            preferred_element_type=jnp.float32,
        ).reshape(single_count, kv_heads, group_size, context)
        * inverse_root
    )
    seen_dec = (positions[None, :] < spans[:single_count, None])[:, None, None, :]
    own_dec = (
        jnp.einsum(
            "rkgh,rkh->rkg", single_q, new_keys[:single_count], preferred_element_type=jnp.float32
        )[..., None]
        * inverse_root
    )
    weight_cache, weight_own = normalize(
        [(cache_dec, seen_dec), (own_dec, jnp.full(own_dec.shape, True))]
    )
    out_dec = jnp.einsum(
        "rkgmp,rmkph->rkgh",
        weight_cache.reshape(single_count, kv_heads, group_size, page_count, page_width),
        page_values[:single_count],
        preferred_element_type=jnp.float32,
    )
    out_dec = (
        out_dec
        + weight_own.astype(jnp.float32)
        * new_values[:single_count].astype(jnp.float32)[:, :, None, :]
    )
    prompt_q = grouped[single_count:]
    prompt_rows = rows_all - single_count
    cache_pro = (
        jnp.einsum(
            "rkgh,mkph->rkgmp",
            prompt_q,
            page_keys[single_count],
            preferred_element_type=jnp.float32,
        ).reshape(prompt_rows, kv_heads, group_size, context)
        * inverse_root
    )
    seen_pro = (positions < spans[single_count])[None, None, None, :]
    new_pro = (
        jnp.einsum(
            "rkgh,mkh->rkgm", prompt_q, new_keys[single_count:], preferred_element_type=jnp.float32
        )
        * inverse_root
    )
    prompt_index = jnp.arange(prompt_rows, dtype=jnp.int32)
    causal = (prompt_index[:, None] >= prompt_index[None, :])[:, None, None, :]
    weight_cpro, weight_npro = normalize([(cache_pro, seen_pro), (new_pro, causal)])
    out_pro = jnp.einsum(
        "rkgmp,mkph->rkgh",
        weight_cpro.reshape(prompt_rows, kv_heads, group_size, page_count, page_width),
        page_values[single_count],
        preferred_element_type=jnp.float32,
    )
    out_pro = out_pro + jnp.einsum(
        "rkgm,mkh->rkgh", weight_npro, new_values[single_count:], preferred_element_type=jnp.float32
    )
    joined = jnp.concatenate([out_dec, out_pro], axis=0).astype(jnp.bfloat16)
    return joined.reshape(rows_all, head_count * head_width)


def slot_table(member, ranking, keeping, slot_count):
    slot_hit = (
        ranking[:, :, None, None] == jnp.arange(slot_count, dtype=jnp.int32)[None, None, None, :]
    )
    return ((member[..., None] > 0) & keeping[:, :, None, None] & slot_hit).astype(jnp.bfloat16)


def expert_pass(send, gating_matrices, expand_matrices, contract_matrices):
    specialist_index, slot_count, model_width = send.shape
    local_count = gating_matrices.shape[0]
    assert local_count == 1
    arrived = expert_exchange(send, 3).reshape(specialist_index * slot_count, model_width)
    row_piece = row_gather(arrived, lax.axis_size("dp"), lax.axis_size("tensor"))
    assert local_count == 1
    gate_part = lax.dot_general(
        row_piece, gating_matrices[0], (((1,), (1,)), ((), ())), preferred_element_type=jnp.float32
    )
    up_part = lax.dot_general(
        row_piece, expand_matrices[0], (((1,), (1,)), ((), ())), preferred_element_type=jnp.float32
    )
    hidden = (jax.nn.silu(gate_part) * up_part).astype(jnp.bfloat16)
    inner = hidden.shape[1]
    padded = -(-inner // 128) * 128
    hidden = jnp.pad(hidden, ((0, 0), (0, padded - inner)))
    down = jnp.pad(contract_matrices[0], ((0, padded - inner), (0, 0)))
    n_dp, n_t = lax.axis_size("dp"), lax.axis_size("tensor")
    summed = moe_sum(hidden, down, n_dp, n_t)
    return expert_exchange(summed.reshape(specialist_index, slot_count, model_width), 4)


def local(
    skip_stream_entry,
    question_vectors,
    fresh_lookup_vectors,
    fresh_content_vectors,
    stored_lookup_sheets,
    stored_content_sheets,
    sequence_sheet_map,
    stored_position_counts,
    attention_merge_matrix,
    premix_scale_factor,
    chosen_specialists,
    selection_shares,
    allowed_placements,
    favored_specialist,
    gating_matrices,
    expand_matrices,
    contract_matrices,
):
    token_count = chosen_specialists.shape[0]
    specialist_index = allowed_placements.shape[0]
    picked = (
        chosen_specialists[:, :, None]
        == jnp.arange(specialist_index, dtype=jnp.int32)[None, None, :]
    ).astype(jnp.int32)
    flat_routes = picked.reshape(token_count * 2, specialist_index)
    busiest_specialist = favored_specialist[0]
    before = (jnp.cumsum(flat_routes, axis=0) - flat_routes).reshape(
        token_count, 2, specialist_index
    )
    ranking = jnp.sum(before * picked, axis=2)
    placement_ceiling = jnp.where(
        jnp.arange(specialist_index, dtype=jnp.int32) == busiest_specialist,
        PLACEMENT_MOST,
        allowed_placements,
    )
    keeping = ranking < jnp.sum(picked * placement_ceiling[None, None, :], axis=2)
    row_total = question_vectors.shape[0]
    heads_out = attend(
        question_vectors.reshape(row_total, -1, HD),
        fresh_lookup_vectors.reshape(row_total, -1, HD),
        fresh_content_vectors.reshape(row_total, -1, HD),
        stored_lookup_sheets,
        stored_content_sheets,
        sequence_sheet_map,
        stored_position_counts,
    )
    own_attn = head_sum(
        jnp.dot(heads_out, attention_merge_matrix, preferred_element_type=jnp.float32).astype(
            jnp.bfloat16
        ),
        lax.axis_size("tensor"),
    ).astype(jnp.float32)
    stream = (skip_stream_entry.astype(jnp.float32) + own_attn).astype(jnp.bfloat16)
    wide = stream.astype(jnp.float32)
    squares = jnp.mean(wide * wide, axis=1, keepdims=True)
    normed = (wide * lax.rsqrt(squares + 1e-05) * premix_scale_factor.astype(jnp.float32)).astype(
        jnp.bfloat16
    )
    main_slots = PLACEMENT_MOST
    table_main = slot_table(picked, ranking, keeping, main_slots)
    send = jnp.einsum(
        "nkes,nd->esd", table_main, normed, preferred_element_type=jnp.float32
    ).astype(jnp.bfloat16)
    expert_out = expert_pass(send, gating_matrices, expand_matrices, contract_matrices)
    chosen = jnp.einsum("nkes,esd->nkd", table_main, expert_out, preferred_element_type=jnp.float32)
    mixed = jnp.sum(selection_shares[:, :, None] * chosen, axis=1)
    return (wide + mixed).astype(jnp.bfloat16)


def solution(mesh):
    placed = (
        P(("dp", "expert", "tensor"), None),
        P(("dp", "expert"), "tensor"),
        P(("dp", "expert"), "tensor"),
        P(("dp", "expert"), "tensor"),
        P(("dp", "expert"), "tensor", None, None),
        P(("dp", "expert"), "tensor", None, None),
        P(("dp", "expert"), None),
        P(("dp", "expert")),
        P("tensor", None),
        P(),
        P(("dp", "expert", "tensor"), None),
        P(("dp", "expert", "tensor"), None),
        P(),
        P(),
        P("expert", ("dp", "tensor"), None),
        P("expert", ("dp", "tensor"), None),
        P("expert", ("dp", "tensor"), None),
    )
    return jax.shard_map(
        local,
        mesh=mesh,
        in_specs=placed,
        out_specs=P(("dp", "expert", "tensor"), None),
        check_vma=False,
    )
```

```python
from functools import reduce
import functools
import math

import jax
import jax.numpy as jnp
from jax import lax
from jax.experimental import pallas as pl
from jax.experimental.pallas import tpu as pltpu
from jax.sharding import PartitionSpec as P

HD = 128
PLACEMENT_MOST = 6


MESH_ID = pl.DeviceIdType.MESH


def plan_order(events, rate=50000.0, latency=1.5, per_step=0.3):
    ready = [0.0] * len(events)
    at = [0] * len(events)
    free = {}
    clock = 0.0
    order = []
    while True:
        live = [i for i in range(len(events)) if at[i] < len(events[i])]
        if not live:
            return order, clock
        i = min(live, key=lambda k: (ready[k], k))
        clock = max(clock, ready[i]) + per_step
        send = events[i][at[i]]
        if send is None:
            ready[i] = clock
        else:
            link, size = send
            start = max(clock, free.get(link, 0.0))
            free[link] = start + size / rate
            ready[i] = free[link] + latency
        order.append(i)
        at[i] += 1


def ring_events(n1, n2, link1, link2, size1, size2):
    return [(link1, size1)] * (n1 - 1) + [None] + [(link2, size2)] * (n2 - 1) + [None]


def split_plan(n_dp, n_t, rows, model_width, reduce):
    best = None
    for first_dp in range(128, model_width // 2, 128):
        widths = [first_dp, first_dp, model_width // 2 - first_dp, model_width // 2 - first_dp]
        events = []
        for block, width in enumerate(widths):
            unit = rows * width * 2
            sign = "+" if block % 2 == 0 else "-"
            if block < 2:
                big1, big2 = (n_t * unit, unit) if reduce else (unit, n_dp * unit)
                events.append(ring_events(n_dp, n_t, "z" + sign, "y" + sign, big1, big2))
            else:
                big1, big2 = (n_dp * unit, unit) if reduce else (unit, n_t * unit)
                events.append(ring_events(n_t, n_dp, "y" + sign, "z" + sign, big1, big2))
        order, finish = plan_order(events)
        if best is None or finish < best[0]:
            best = (finish, widths, order)
    return best[1], best[2]


def run_in_order(streams, order):
    for i in order:
        next(streams[i])
    for st in streams:
        for _ in st:
            pass


def ring_phase(n, me, step_to, own, chunk_lead, recv, send0, send_sems, recv_sems, first_sem, finish):
    copies = []
    for s in range(n - 1):
        c = lax.rem(me + n * 2 - step_to[1] * (s + 1), n)
        if s == 0:
            for i in range(chunk_lead):
                send0[i] = own(c, i).astype(send0.dtype)
            src = send0
        else:
            copies[-1].wait_recv()
            for i in range(chunk_lead):
                recv[s - 1, i] = (own(c, i) + recv[s - 1, i].astype(jnp.float32)).astype(recv.dtype)
            src = recv.at[s - 1]
        copy = pltpu.make_async_remote_copy(
            src_ref=src,
            dst_ref=recv.at[s],
            send_sem=send_sems.at[first_sem + s],
            recv_sem=recv_sems.at[first_sem + s],
            device_id=step_to[0],
            device_id_type=MESH_ID,
        )
        copy.start()
        copies.append(copy)
        yield copies
    copies[-1].wait_recv()
    for i in range(chunk_lead):
        finish(i, own(me, i) + recv[n - 2, i].astype(jnp.float32))
    yield copies


def block_product(h_ref, w_ref, chunk, cols, rows):
    start = pl.multiple_of(chunk * rows, 16)
    product = jnp.dot(h_ref[pl.ds(start, rows), :], w_ref[:, cols], preferred_element_type=jnp.float32)
    return product.astype(jnp.bfloat16).astype(jnp.float32)


def moe_sum_kernel(n_dp, n_t, widths, order, h_ref, w_ref, o_ref, *scratch):
    recv_sems, send_sems = scratch[-2], scratch[-1]
    bufs = scratch[:-2]
    me_dp = lax.axis_index("dp")
    me_t = lax.axis_index("tensor")
    me_e = lax.axis_index("expert")

    def dp_dev(d):
        return (lax.rem(me_dp + n_dp + d, n_dp), me_e, me_t)

    def t_dev(d):
        return (me_dp, me_e, lax.rem(me_t + n_t + d, n_t))

    barrier = pltpu.get_barrier_semaphore()
    for dev in (dp_dev(1), dp_dev(-1), t_dev(1), t_dev(-1)):
        pl.semaphore_signal(barrier, 1, device_id=dev, device_id_type=MESH_ID)
    pl.semaphore_wait(barrier, 4)

    streams = []
    sem_at = 0
    for block in range(4):
        cols = pl.ds(sum(widths[:block]), widths[block])
        direction = 1 if block % 2 == 0 else -1
        r1, s1, acc, r2, s2 = bufs[block * 5: block * 5 + 5]
        if block < 2:
            first = (n_dp, me_dp, (dp_dev(direction), direction), n_t)
            own1 = lambda c, i, cols=cols: block_product(h_ref, w_ref, c * n_t + i, cols, o_ref.shape[0])
            second = (n_t, me_t, (t_dev(direction), direction))
        else:
            first = (n_t, me_t, (t_dev(direction), direction), n_dp)
            own1 = lambda c, i, cols=cols: block_product(h_ref, w_ref, i * n_t + c, cols, o_ref.shape[0])
            second = (n_dp, me_dp, (dp_dev(direction), direction))

        def fin1(i, v, acc=acc):
            acc[i] = v

        def fin2(i, v, cols=cols):
            o_ref[:, cols] = v.astype(o_ref.dtype)

        own2 = lambda c, i, acc=acc: acc[c]

        def stream(first=first, second=second, own1=own1, own2=own2, r1=r1, s1=s1, r2=r2, s2=s2,
                   fin1=fin1, fin2=fin2, base=sem_at):
            n1, me1, to1, lead = first
            copies = []
            for copies in ring_phase(n1, me1, to1, own1, lead, r1, s1, send_sems, recv_sems, base, fin1):
                yield
            done1 = copies
            n2, me2, to2 = second
            for copies in ring_phase(n2, me2, to2, own2, 1, r2, s2, send_sems, recv_sems, base + n1 - 1,
                                     lambda i, v: fin2(i, v)):
                yield
            for copy in done1 + copies:
                copy.wait_send()

        streams.append(stream())
        sem_at += n_dp + n_t - 2

    run_in_order(streams, order)


def gather_phase(n, me, step_to, chunk, send_sems, recv_sems, first_sem):
    copies = []
    for s in range(n - 1):
        c = lax.rem(me + n * 2 - step_to[1] * s, n)
        if s > 0:
            copies[-1].wait_recv()
        copy = pltpu.make_async_remote_copy(
            src_ref=chunk(c),
            dst_ref=chunk(c),
            send_sem=send_sems.at[first_sem + s],
            recv_sem=recv_sems.at[first_sem + s],
            device_id=step_to[0],
            device_id_type=MESH_ID,
        )
        copy.start()
        copies.append(copy)
        yield copies
    copies[-1].wait_recv()
    yield copies


def row_gather_kernel(n_dp, n_t, widths, order, x_ref, o_ref, *scratch):
    recv_sems, send_sems = scratch[-2], scratch[-1]
    bufs = scratch[:-2]
    me_dp = lax.axis_index("dp")
    me_t = lax.axis_index("tensor")
    me_e = lax.axis_index("expert")
    rows = x_ref.shape[0]

    def dp_dev(d):
        return (lax.rem(me_dp + n_dp + d, n_dp), me_e, me_t)

    def t_dev(d):
        return (me_dp, me_e, lax.rem(me_t + n_t + d, n_t))

    for block in range(4):
        cols = pl.ds(sum(widths[:block]), widths[block])
        if block < 2:
            bufs[block][me_t, me_dp] = x_ref[:, cols]
        else:
            bufs[block][me_dp, me_t] = x_ref[:, cols]

    barrier = pltpu.get_barrier_semaphore()
    for dev in (dp_dev(1), dp_dev(-1), t_dev(1), t_dev(-1)):
        pl.semaphore_signal(barrier, 1, device_id=dev, device_id_type=MESH_ID)
    pl.semaphore_wait(barrier, 4)

    streams = []
    sem_at = 0
    for block in range(4):
        direction = 1 if block % 2 == 0 else -1
        g = bufs[block]
        if block < 2:
            first = (n_dp, me_dp, (dp_dev(direction), direction), lambda c, g=g: g.at[me_t, c])
            second = (n_t, me_t, (t_dev(direction), direction), lambda c, g=g: g.at[c])
        else:
            first = (n_t, me_t, (t_dev(direction), direction), lambda c, g=g: g.at[me_dp, c])
            second = (n_dp, me_dp, (dp_dev(direction), direction), lambda c, g=g: g.at[c])

        def stream(first=first, second=second, base=sem_at):
            n1, me1, to1, chunk1 = first
            copies = []
            for copies in gather_phase(n1, me1, to1, chunk1, send_sems, recv_sems, base):
                yield
            done1 = copies
            n2, me2, to2, chunk2 = second
            for copies in gather_phase(n2, me2, to2, chunk2, send_sems, recv_sems, base + n1 - 1):
                yield
            for copy in done1 + copies:
                copy.wait_send()

        streams.append(stream())
        sem_at += n_dp + n_t - 2

    run_in_order(streams, order)

    for block in range(4):
        cols = pl.ds(sum(widths[:block]), widths[block])
        for d in range(n_dp):
            for t in range(n_t):
                piece = bufs[block][t, d] if block < 2 else bufs[block][d, t]
                o_ref[pl.ds((d * n_t + t) * rows, rows), cols] = piece


def row_gather(x, n_dp, n_t):
    rows, model_width = x.shape
    widths, order = split_plan(n_dp, n_t, rows, model_width, False)
    scratch = [
        pltpu.VMEM((n_t, n_dp, rows, widths[0]), jnp.bfloat16),
        pltpu.VMEM((n_t, n_dp, rows, widths[1]), jnp.bfloat16),
        pltpu.VMEM((n_dp, n_t, rows, widths[2]), jnp.bfloat16),
        pltpu.VMEM((n_dp, n_t, rows, widths[3]), jnp.bfloat16),
    ]
    copies = 4 * (n_dp + n_t - 2)
    scratch += [pltpu.SemaphoreType.DMA((copies,)), pltpu.SemaphoreType.DMA((copies,))]
    return pl.pallas_call(
        functools.partial(row_gather_kernel, n_dp, n_t, tuple(widths), tuple(order)),
        out_shape=jax.ShapeDtypeStruct((n_dp * n_t * rows, model_width), jnp.bfloat16),
        in_specs=[pl.BlockSpec(memory_space=pltpu.VMEM)],
        out_specs=pl.BlockSpec(memory_space=pltpu.VMEM),
        scratch_shapes=scratch,
        compiler_params=pltpu.CompilerParams(
            collective_id=1, has_side_effects=True, vmem_limit_bytes=60 * 1024 * 1024
        ),
    )(x)


def head_sum_kernel(n_t, x_ref, o_ref, recv0, send0, recv1, send1, recv_sems, send_sems):
    me_dp = lax.axis_index("dp")
    me_e = lax.axis_index("expert")
    me_t = lax.axis_index("tensor")
    rows = o_ref.shape[0]
    width = o_ref.shape[1] // 2

    def t_dev(d):
        return (me_dp, me_e, lax.rem(me_t + n_t + d, n_t))

    barrier = pltpu.get_barrier_semaphore()
    for dev in (t_dev(1), t_dev(-1)):
        pl.semaphore_signal(barrier, 1, device_id=dev, device_id_type=MESH_ID)
    pl.semaphore_wait(barrier, 2)
    streams = []
    for block, (recv, send0_buf) in enumerate(((recv0, send0), (recv1, send1))):
        cols = pl.ds(block * width, width)
        direction = 1 if block == 0 else -1
        own = lambda c, i, cols=cols: x_ref[pl.ds(pl.multiple_of(c * rows, 8), rows), cols].astype(jnp.float32)

        def finish(i, v, cols=cols):
            o_ref[:, cols] = v.astype(o_ref.dtype)

        def stream(own=own, recv=recv, send0_buf=send0_buf, finish=finish, direction=direction, base=block):
            copies = []
            for copies in ring_phase(n_t, me_t, (t_dev(direction), direction), own, 1, recv, send0_buf,
                                     send_sems, recv_sems, base * (n_t - 1), finish):
                yield
            for copy in copies:
                copy.wait_send()

        streams.append(stream())
    run_in_order(streams, [0, 1] * n_t)


def head_sum(x, n_t):
    rows, model_width = x.shape[0] // n_t, x.shape[1]
    width = model_width // 2
    scratch = []
    for _ in range(2):
        scratch += [
            pltpu.VMEM((n_t - 1, 1, rows, width), jnp.bfloat16),
            pltpu.VMEM((1, rows, width), jnp.bfloat16),
        ]
    copies = 2 * (n_t - 1)
    scratch += [pltpu.SemaphoreType.DMA((copies,)), pltpu.SemaphoreType.DMA((copies,))]
    return pl.pallas_call(
        functools.partial(head_sum_kernel, n_t),
        out_shape=jax.ShapeDtypeStruct((rows, model_width), jnp.bfloat16),
        in_specs=[pl.BlockSpec(memory_space=pltpu.VMEM)],
        out_specs=pl.BlockSpec(memory_space=pltpu.VMEM),
        scratch_shapes=scratch,
        compiler_params=pltpu.CompilerParams(collective_id=2, has_side_effects=True),
    )(x)


def expert_exchange_kernel(n_e, x_ref, o_ref, recv, recv_sems, send_sems):
    me_dp = lax.axis_index("dp")
    me_e = lax.axis_index("expert")
    me_t = lax.axis_index("tensor")
    barrier = pltpu.get_barrier_semaphore()
    for k in range(1, n_e):
        pl.semaphore_signal(barrier, 1, device_id=(me_dp, lax.rem(me_e + k, n_e), me_t),
                            device_id_type=MESH_ID)
    pl.semaphore_wait(barrier, n_e - 1)
    copies = []
    for k in range(1, n_e):
        target = lax.rem(me_e + k, n_e)
        copy = pltpu.make_async_remote_copy(
            src_ref=x_ref.at[target],
            dst_ref=recv.at[me_e],
            send_sem=send_sems.at[k - 1],
            recv_sem=recv_sems.at[k - 1],
            device_id=(me_dp, target, me_t),
            device_id_type=MESH_ID,
        )
        copy.start()
        copies.append(copy)
    o_ref[me_e] = x_ref[me_e]
    for k in range(1, n_e):
        copies[k - 1].wait_recv()
        source = lax.rem(me_e + n_e - k, n_e)
        o_ref[source] = recv[source]
    for copy in copies:
        copy.wait_send()


def expert_exchange(x, collective):
    n_e = x.shape[0]
    return pl.pallas_call(
        functools.partial(expert_exchange_kernel, n_e),
        out_shape=jax.ShapeDtypeStruct(x.shape, x.dtype),
        in_specs=[pl.BlockSpec(memory_space=pltpu.VMEM)],
        out_specs=pl.BlockSpec(memory_space=pltpu.VMEM),
        scratch_shapes=[
            pltpu.VMEM(x.shape, x.dtype),
            pltpu.SemaphoreType.DMA((n_e - 1,)),
            pltpu.SemaphoreType.DMA((n_e - 1,)),
        ],
        compiler_params=pltpu.CompilerParams(collective_id=collective, has_side_effects=True),
    )(x)


def gather_feed_phase(n, me, step_to, chunk, send_sems, recv_sems, first_sem, process, own_too):
    copies = []
    for s in range(n - 1):
        c = lax.rem(me + n * 2 - step_to[1] * s, n)
        if s > 0:
            copies[-1].wait_recv()
        copy = pltpu.make_async_remote_copy(
            src_ref=chunk(c),
            dst_ref=chunk(c),
            send_sem=send_sems.at[first_sem + s],
            recv_sem=recv_sems.at[first_sem + s],
            device_id=step_to[0],
            device_id_type=MESH_ID,
        )
        copy.start()
        copies.append(copy)
        if s > 0 or own_too:
            process(c)
        yield copies
    copies[-1].wait_recv()
    process(lax.rem(me + n * 2 - step_to[1] * (n - 1), n))
    yield copies


def expert_front_kernel(n_dp, n_t, widths, order, x_ref, wg_ref, wu_ref, o_ref, *scratch):
    recv_sems, send_sems = scratch[-2], scratch[-1]
    gate_acc, up_acc = scratch[-4], scratch[-3]
    bufs = scratch[:-4]
    me_dp = lax.axis_index("dp")
    me_t = lax.axis_index("tensor")
    me_e = lax.axis_index("expert")
    rows = x_ref.shape[0]

    def dp_dev(d):
        return (lax.rem(me_dp + n_dp + d, n_dp), me_e, me_t)

    def t_dev(d):
        return (me_dp, me_e, lax.rem(me_t + n_t + d, n_t))

    gate_acc[...] = jnp.zeros_like(gate_acc)
    up_acc[...] = jnp.zeros_like(up_acc)
    for block in range(4):
        cols = pl.ds(sum(widths[:block]), widths[block])
        if block < 2:
            bufs[block][me_t, me_dp] = x_ref[:, cols]
        else:
            bufs[block][me_dp, me_t] = x_ref[:, cols]

    barrier = pltpu.get_barrier_semaphore()
    for dev in (dp_dev(1), dp_dev(-1), t_dev(1), t_dev(-1)):
        pl.semaphore_signal(barrier, 1, device_id=dev, device_id_type=MESH_ID)
    pl.semaphore_wait(barrier, 4)

    def feed(piece, row_chunk, cols):
        start = pl.multiple_of(row_chunk * rows, 16)
        v = piece[...]
        dims = (((1,), (1,)), ((), ()))
        gate_acc[pl.ds(start, rows), :] += lax.dot_general(
            v, wg_ref[:, cols], dims, preferred_element_type=jnp.float32)
        up_acc[pl.ds(start, rows), :] += lax.dot_general(
            v, wu_ref[:, cols], dims, preferred_element_type=jnp.float32)

    streams = []
    sem_at = 0
    for block in range(4):
        direction = 1 if block % 2 == 0 else -1
        g = bufs[block]
        cols = pl.ds(sum(widths[:block]), widths[block])
        if block < 2:
            def p1(c, g=g, cols=cols):
                feed(g.at[me_t, c], c * n_t + me_t, cols)

            def p2(c, g=g, cols=cols):
                def body(d, carry):
                    feed(g.at[c, d], d * n_t + c, cols)
                    return carry
                lax.fori_loop(0, n_dp, body, 0)
            first = (n_dp, me_dp, (dp_dev(direction), direction), lambda c, g=g: g.at[me_t, c], p1)
            second = (n_t, me_t, (t_dev(direction), direction), lambda c, g=g: g.at[c], p2)
        else:
            def p1(c, g=g, cols=cols):
                feed(g.at[me_dp, c], me_dp * n_t + c, cols)

            def p2(c, g=g, cols=cols):
                def body(t, carry):
                    feed(g.at[c, t], c * n_t + t, cols)
                    return carry
                lax.fori_loop(0, n_t, body, 0)
            first = (n_t, me_t, (t_dev(direction), direction), lambda c, g=g: g.at[me_dp, c], p1)
            second = (n_dp, me_dp, (dp_dev(direction), direction), lambda c, g=g: g.at[c], p2)

        def stream(first=first, second=second, base=sem_at):
            n1, me1, to1, chunk1, proc1 = first
            copies = []
            for copies in gather_feed_phase(n1, me1, to1, chunk1, send_sems, recv_sems, base, proc1, True):
                yield
            done1 = copies
            n2, me2, to2, chunk2, proc2 = second
            for copies in gather_feed_phase(n2, me2, to2, chunk2, send_sems, recv_sems, base + n1 - 1,
                                            proc2, False):
                yield
            for copy in done1 + copies:
                copy.wait_send()

        streams.append(stream())
        sem_at += n_dp + n_t - 2

    run_in_order(streams, order)

    tile = 128

    def finish(i, carry):
        at = pl.ds(pl.multiple_of(i * tile, tile), tile)
        gate = gate_acc[at, :]
        o_ref[at, :] = (gate / (1.0 + jnp.exp(-gate)) * up_acc[at, :]).astype(o_ref.dtype)
        return carry

    lax.fori_loop(0, o_ref.shape[0] // tile, finish, 0)


def expert_front(x, gate_w, up_w, n_dp, n_t):
    rows, model_width = x.shape
    inner = gate_w.shape[0]
    widths, order = split_plan(n_dp, n_t, rows, model_width, False)
    scratch = [
        pltpu.VMEM((n_t, n_dp, rows, widths[0]), jnp.bfloat16),
        pltpu.VMEM((n_t, n_dp, rows, widths[1]), jnp.bfloat16),
        pltpu.VMEM((n_dp, n_t, rows, widths[2]), jnp.bfloat16),
        pltpu.VMEM((n_dp, n_t, rows, widths[3]), jnp.bfloat16),
        pltpu.VMEM((n_dp * n_t * rows, inner), jnp.float32),
        pltpu.VMEM((n_dp * n_t * rows, inner), jnp.float32),
    ]
    copies = 4 * (n_dp + n_t - 2)
    scratch += [pltpu.SemaphoreType.DMA((copies,)), pltpu.SemaphoreType.DMA((copies,))]
    return pl.pallas_call(
        functools.partial(expert_front_kernel, n_dp, n_t, tuple(widths), tuple(order)),
        out_shape=jax.ShapeDtypeStruct((n_dp * n_t * rows, inner), jnp.bfloat16),
        in_specs=[pl.BlockSpec(memory_space=pltpu.VMEM)] * 3,
        out_specs=pl.BlockSpec(memory_space=pltpu.VMEM),
        scratch_shapes=scratch,
        compiler_params=pltpu.CompilerParams(
            collective_id=1, has_side_effects=True, vmem_limit_bytes=60 * 1024 * 1024
        ),
    )(x, gate_w, up_w)


def moe_sum(hidden, down, n_dp, n_t):
    rows, model_width = hidden.shape[0] // (n_dp * n_t), down.shape[1]
    widths, order = split_plan(n_dp, n_t, rows, model_width, True)
    scratch = []
    for block in range(4):
        width = widths[block]
        if block < 2:
            n1, lead, n2 = n_dp, n_t, n_t
        else:
            n1, lead, n2 = n_t, n_dp, n_dp
        scratch += [
            pltpu.VMEM((n1 - 1, lead, rows, width), jnp.bfloat16),
            pltpu.VMEM((lead, rows, width), jnp.bfloat16),
            pltpu.VMEM((lead, rows, width), jnp.float32),
            pltpu.VMEM((n2 - 1, 1, rows, width), jnp.bfloat16),
            pltpu.VMEM((1, rows, width), jnp.bfloat16),
        ]
    copies = 4 * (n_dp + n_t - 2)
    scratch += [pltpu.SemaphoreType.DMA((copies,)), pltpu.SemaphoreType.DMA((copies,))]
    return pl.pallas_call(
        functools.partial(moe_sum_kernel, n_dp, n_t, tuple(widths), tuple(order)),
        out_shape=jax.ShapeDtypeStruct((rows, model_width), jnp.bfloat16),
        in_specs=[pl.BlockSpec(memory_space=pltpu.VMEM)] * 2,
        out_specs=pl.BlockSpec(memory_space=pltpu.VMEM),
        scratch_shapes=scratch,
        compiler_params=pltpu.CompilerParams(
            collective_id=0, has_side_effects=True, vmem_limit_bytes=60 * 1024 * 1024
        ),
    )(hidden, down)


def normalize(parts):
    highest = reduce(
        jnp.maximum,
        [
            jnp.max(jnp.where(visible, scores, -jnp.inf), axis=-1, keepdims=True)
            for scores, visible in parts
        ],
    )
    portions = [jnp.where(visible, jnp.exp(scores - highest), 0.0) for scores, visible in parts]
    denominator = reduce(
        jnp.add, [jnp.sum(portion, axis=-1, keepdims=True) for portion in portions]
    )
    return [(portion / denominator).astype(jnp.bfloat16) for portion in portions]


def attend(question_vectors, new_keys, new_values, key_pages, value_pages, table, spans):
    rows_all, head_count, head_width = question_vectors.shape
    kv_heads = new_keys.shape[1]
    group_size = head_count // kv_heads
    single_count = spans.shape[0] - 1
    page_count = table.shape[1]
    page_width = key_pages.shape[2]
    context = page_count * page_width
    inverse_root = 1.0 / math.sqrt(head_width)
    page_keys = key_pages[table]
    page_values = value_pages[table]
    grouped = question_vectors.reshape(rows_all, kv_heads, group_size, head_width)
    positions = jnp.arange(context, dtype=jnp.int32)
    single_q = grouped[:single_count]
    cache_dec = (
        jnp.einsum(
            "rkgh,rmkph->rkgmp",
            single_q,
            page_keys[:single_count],
            preferred_element_type=jnp.float32,
        ).reshape(single_count, kv_heads, group_size, context)
        * inverse_root
    )
    seen_dec = (positions[None, :] < spans[:single_count, None])[:, None, None, :]
    own_dec = (
        jnp.einsum(
            "rkgh,rkh->rkg", single_q, new_keys[:single_count], preferred_element_type=jnp.float32
        )[..., None]
        * inverse_root
    )
    weight_cache, weight_own = normalize(
        [(cache_dec, seen_dec), (own_dec, jnp.full(own_dec.shape, True))]
    )
    out_dec = jnp.einsum(
        "rkgmp,rmkph->rkgh",
        weight_cache.reshape(single_count, kv_heads, group_size, page_count, page_width),
        page_values[:single_count],
        preferred_element_type=jnp.float32,
    )
    out_dec = (
        out_dec
        + weight_own.astype(jnp.float32)
        * new_values[:single_count].astype(jnp.float32)[:, :, None, :]
    )
    prompt_q = grouped[single_count:]
    prompt_rows = rows_all - single_count
    cache_pro = (
        jnp.einsum(
            "rkgh,mkph->rkgmp",
            prompt_q,
            page_keys[single_count],
            preferred_element_type=jnp.float32,
        ).reshape(prompt_rows, kv_heads, group_size, context)
        * inverse_root
    )
    seen_pro = (positions < spans[single_count])[None, None, None, :]
    new_pro = (
        jnp.einsum(
            "rkgh,mkh->rkgm", prompt_q, new_keys[single_count:], preferred_element_type=jnp.float32
        )
        * inverse_root
    )
    prompt_index = jnp.arange(prompt_rows, dtype=jnp.int32)
    causal = (prompt_index[:, None] >= prompt_index[None, :])[:, None, None, :]
    weight_cpro, weight_npro = normalize([(cache_pro, seen_pro), (new_pro, causal)])
    out_pro = jnp.einsum(
        "rkgmp,mkph->rkgh",
        weight_cpro.reshape(prompt_rows, kv_heads, group_size, page_count, page_width),
        page_values[single_count],
        preferred_element_type=jnp.float32,
    )
    out_pro = out_pro + jnp.einsum(
        "rkgm,mkh->rkgh", weight_npro, new_values[single_count:], preferred_element_type=jnp.float32
    )
    joined = jnp.concatenate([out_dec, out_pro], axis=0).astype(jnp.bfloat16)
    return joined.reshape(rows_all, head_count * head_width)


def slot_table(member, ranking, keeping, slot_count):
    slot_hit = (
        ranking[:, :, None, None] == jnp.arange(slot_count, dtype=jnp.int32)[None, None, None, :]
    )
    return ((member[..., None] > 0) & keeping[:, :, None, None] & slot_hit).astype(jnp.bfloat16)


def expert_pass(send, gating_matrices, expand_matrices, contract_matrices):
    specialist_index, slot_count, model_width = send.shape
    local_count = gating_matrices.shape[0]
    assert local_count == 1
    arrived = expert_exchange(send, 3).reshape(specialist_index * slot_count, model_width)
    inner = gating_matrices.shape[1]
    padded = -(-inner // 128) * 128
    widen = ((0, padded - inner), (0, 0))
    hidden = expert_front(
        arrived,
        jnp.pad(gating_matrices[0], widen),
        jnp.pad(expand_matrices[0], widen),
        lax.axis_size("dp"),
        lax.axis_size("tensor"),
    )
    down = jnp.pad(contract_matrices[0], widen)
    n_dp, n_t = lax.axis_size("dp"), lax.axis_size("tensor")
    summed = moe_sum(hidden, down, n_dp, n_t)
    return expert_exchange(summed.reshape(specialist_index, slot_count, model_width), 4)


def local(
    skip_stream_entry,
    question_vectors,
    fresh_lookup_vectors,
    fresh_content_vectors,
    stored_lookup_sheets,
    stored_content_sheets,
    sequence_sheet_map,
    stored_position_counts,
    attention_merge_matrix,
    premix_scale_factor,
    chosen_specialists,
    selection_shares,
    allowed_placements,
    favored_specialist,
    gating_matrices,
    expand_matrices,
    contract_matrices,
):
    token_count = chosen_specialists.shape[0]
    specialist_index = allowed_placements.shape[0]
    picked = (
        chosen_specialists[:, :, None]
        == jnp.arange(specialist_index, dtype=jnp.int32)[None, None, :]
    ).astype(jnp.int32)
    flat_routes = picked.reshape(token_count * 2, specialist_index)
    busiest_specialist = favored_specialist[0]
    before = (jnp.cumsum(flat_routes, axis=0) - flat_routes).reshape(
        token_count, 2, specialist_index
    )
    ranking = jnp.sum(before * picked, axis=2)
    placement_ceiling = jnp.where(
        jnp.arange(specialist_index, dtype=jnp.int32) == busiest_specialist,
        PLACEMENT_MOST,
        allowed_placements,
    )
    keeping = ranking < jnp.sum(picked * placement_ceiling[None, None, :], axis=2)
    row_total = question_vectors.shape[0]
    heads_out = attend(
        question_vectors.reshape(row_total, -1, HD),
        fresh_lookup_vectors.reshape(row_total, -1, HD),
        fresh_content_vectors.reshape(row_total, -1, HD),
        stored_lookup_sheets,
        stored_content_sheets,
        sequence_sheet_map,
        stored_position_counts,
    )
    own_attn = head_sum(
        jnp.dot(heads_out, attention_merge_matrix, preferred_element_type=jnp.float32).astype(
            jnp.bfloat16
        ),
        lax.axis_size("tensor"),
    ).astype(jnp.float32)
    stream = (skip_stream_entry.astype(jnp.float32) + own_attn).astype(jnp.bfloat16)
    wide = stream.astype(jnp.float32)
    squares = jnp.mean(wide * wide, axis=1, keepdims=True)
    normed = (wide * lax.rsqrt(squares + 1e-05) * premix_scale_factor.astype(jnp.float32)).astype(
        jnp.bfloat16
    )
    main_slots = PLACEMENT_MOST
    table_main = slot_table(picked, ranking, keeping, main_slots)
    send = jnp.einsum(
        "nkes,nd->esd", table_main, normed, preferred_element_type=jnp.float32
    ).astype(jnp.bfloat16)
    expert_out = expert_pass(send, gating_matrices, expand_matrices, contract_matrices)
    chosen = jnp.einsum("nkes,esd->nkd", table_main, expert_out, preferred_element_type=jnp.float32)
    mixed = jnp.sum(selection_shares[:, :, None] * chosen, axis=1)
    return (wide + mixed).astype(jnp.bfloat16)


def solution(mesh):
    placed = (
        P(("dp", "expert", "tensor"), None),
        P(("dp", "expert"), "tensor"),
        P(("dp", "expert"), "tensor"),
        P(("dp", "expert"), "tensor"),
        P(("dp", "expert"), "tensor", None, None),
        P(("dp", "expert"), "tensor", None, None),
        P(("dp", "expert"), None),
        P(("dp", "expert")),
        P("tensor", None),
        P(),
        P(("dp", "expert", "tensor"), None),
        P(("dp", "expert", "tensor"), None),
        P(),
        P(),
        P("expert", ("dp", "tensor"), None),
        P("expert", ("dp", "tensor"), None),
        P("expert", ("dp", "tensor"), None),
    )
    return jax.shard_map(
        local,
        mesh=mesh,
        in_specs=placed,
        out_specs=P(("dp", "expert", "tensor"), None),
        check_vma=False,
    )
```

```python
from functools import reduce
import functools
import math

import jax
import jax.numpy as jnp
from jax import lax
from jax.experimental import pallas as pl
from jax.experimental.pallas import tpu as pltpu
from jax.sharding import PartitionSpec as P

HD = 128
PLACEMENT_MOST = 6


MESH_ID = pl.DeviceIdType.MESH


def plan_order(events, rate=50000.0, latency=1.5, per_step=0.3):
    ready = [0.0] * len(events)
    at = [0] * len(events)
    free = {}
    clock = 0.0
    order = []
    while True:
        live = [i for i in range(len(events)) if at[i] < len(events[i])]
        if not live:
            return order, clock
        i = min(live, key=lambda k: (ready[k], k))
        clock = max(clock, ready[i]) + per_step
        send = events[i][at[i]]
        if send is None:
            ready[i] = clock
        else:
            link, size = send
            start = max(clock, free.get(link, 0.0))
            free[link] = start + size / rate
            ready[i] = free[link] + latency
        order.append(i)
        at[i] += 1


def ring_events(n1, n2, link1, link2, size1, size2):
    return [(link1, size1)] * (n1 - 1) + [None] + [(link2, size2)] * (n2 - 1) + [None]


def split_plan(n_dp, n_t, rows, model_width, reduce):
    best = None
    for first_dp in range(128, model_width // 2, 128):
        widths = [first_dp, first_dp, model_width // 2 - first_dp, model_width // 2 - first_dp]
        events = []
        for block, width in enumerate(widths):
            unit = rows * width * 2
            sign = "+" if block % 2 == 0 else "-"
            if block < 2:
                big1, big2 = (n_t * unit, unit) if reduce else (unit, n_dp * unit)
                events.append(ring_events(n_dp, n_t, "z" + sign, "y" + sign, big1, big2))
            else:
                big1, big2 = (n_dp * unit, unit) if reduce else (unit, n_t * unit)
                events.append(ring_events(n_t, n_dp, "y" + sign, "z" + sign, big1, big2))
        order, finish = plan_order(events)
        if best is None or finish < best[0]:
            best = (finish, widths, order)
    return best[1], best[2]


def run_in_order(streams, order):
    for i in order:
        next(streams[i])
    for st in streams:
        for _ in st:
            pass


def ring_phase(n, me, step_to, own, chunk_lead, recv, send0, send_sems, recv_sems, first_sem, finish):
    copies = []
    for s in range(n - 1):
        c = lax.rem(me + n * 2 - step_to[1] * (s + 1), n)
        if s == 0:
            for i in range(chunk_lead):
                send0[i] = own(c, i).astype(send0.dtype)
            src = send0
        else:
            copies[-1].wait_recv()
            for i in range(chunk_lead):
                recv[s - 1, i] = (own(c, i) + recv[s - 1, i].astype(jnp.float32)).astype(recv.dtype)
            src = recv.at[s - 1]
        copy = pltpu.make_async_remote_copy(
            src_ref=src,
            dst_ref=recv.at[s],
            send_sem=send_sems.at[first_sem + s],
            recv_sem=recv_sems.at[first_sem + s],
            device_id=step_to[0],
            device_id_type=MESH_ID,
        )
        copy.start()
        copies.append(copy)
        yield copies
    copies[-1].wait_recv()
    for i in range(chunk_lead):
        finish(i, own(me, i) + recv[n - 2, i].astype(jnp.float32))
    yield copies


def block_product(h_ref, w_ref, chunk, cols, rows):
    start = pl.multiple_of(chunk * rows, 16)
    product = jnp.dot(h_ref[pl.ds(start, rows), :], w_ref[:, cols], preferred_element_type=jnp.float32)
    return product.astype(jnp.bfloat16).astype(jnp.float32)


def moe_sum_kernel(n_dp, n_t, widths, order, h_ref, w_ref, o_ref, *scratch):
    recv_sems, send_sems = scratch[-2], scratch[-1]
    bufs = scratch[:-2]
    me_dp = lax.axis_index("dp")
    me_t = lax.axis_index("tensor")
    me_e = lax.axis_index("expert")

    def dp_dev(d):
        return (lax.rem(me_dp + n_dp + d, n_dp), me_e, me_t)

    def t_dev(d):
        return (me_dp, me_e, lax.rem(me_t + n_t + d, n_t))

    barrier = pltpu.get_barrier_semaphore()
    for dev in (dp_dev(1), dp_dev(-1), t_dev(1), t_dev(-1)):
        pl.semaphore_signal(barrier, 1, device_id=dev, device_id_type=MESH_ID)
    pl.semaphore_wait(barrier, 4)

    streams = []
    sem_at = 0
    for block in range(4):
        cols = pl.ds(sum(widths[:block]), widths[block])
        direction = 1 if block % 2 == 0 else -1
        r1, s1, acc, r2, s2 = bufs[block * 5: block * 5 + 5]
        if block < 2:
            first = (n_dp, me_dp, (dp_dev(direction), direction), n_t)
            own1 = lambda c, i, cols=cols: block_product(h_ref, w_ref, c * n_t + i, cols, o_ref.shape[0])
            second = (n_t, me_t, (t_dev(direction), direction))
        else:
            first = (n_t, me_t, (t_dev(direction), direction), n_dp)
            own1 = lambda c, i, cols=cols: block_product(h_ref, w_ref, i * n_t + c, cols, o_ref.shape[0])
            second = (n_dp, me_dp, (dp_dev(direction), direction))

        def fin1(i, v, acc=acc):
            acc[i] = v

        def fin2(i, v, cols=cols):
            o_ref[:, cols] = v.astype(o_ref.dtype)

        own2 = lambda c, i, acc=acc: acc[c]

        def stream(first=first, second=second, own1=own1, own2=own2, r1=r1, s1=s1, r2=r2, s2=s2,
                   fin1=fin1, fin2=fin2, base=sem_at):
            n1, me1, to1, lead = first
            copies = []
            for copies in ring_phase(n1, me1, to1, own1, lead, r1, s1, send_sems, recv_sems, base, fin1):
                yield
            done1 = copies
            n2, me2, to2 = second
            for copies in ring_phase(n2, me2, to2, own2, 1, r2, s2, send_sems, recv_sems, base + n1 - 1,
                                     lambda i, v: fin2(i, v)):
                yield
            for copy in done1 + copies:
                copy.wait_send()

        streams.append(stream())
        sem_at += n_dp + n_t - 2

    run_in_order(streams, order)


def gather_phase(n, me, step_to, chunk, send_sems, recv_sems, first_sem):
    copies = []
    for s in range(n - 1):
        c = lax.rem(me + n * 2 - step_to[1] * s, n)
        if s > 0:
            copies[-1].wait_recv()
        copy = pltpu.make_async_remote_copy(
            src_ref=chunk(c),
            dst_ref=chunk(c),
            send_sem=send_sems.at[first_sem + s],
            recv_sem=recv_sems.at[first_sem + s],
            device_id=step_to[0],
            device_id_type=MESH_ID,
        )
        copy.start()
        copies.append(copy)
        yield copies
    copies[-1].wait_recv()
    yield copies


def row_gather_kernel(n_dp, n_t, widths, order, x_ref, o_ref, *scratch):
    recv_sems, send_sems = scratch[-2], scratch[-1]
    bufs = scratch[:-2]
    me_dp = lax.axis_index("dp")
    me_t = lax.axis_index("tensor")
    me_e = lax.axis_index("expert")
    rows = x_ref.shape[0]

    def dp_dev(d):
        return (lax.rem(me_dp + n_dp + d, n_dp), me_e, me_t)

    def t_dev(d):
        return (me_dp, me_e, lax.rem(me_t + n_t + d, n_t))

    for block in range(4):
        cols = pl.ds(sum(widths[:block]), widths[block])
        if block < 2:
            bufs[block][me_t, me_dp] = x_ref[:, cols]
        else:
            bufs[block][me_dp, me_t] = x_ref[:, cols]

    barrier = pltpu.get_barrier_semaphore()
    for dev in (dp_dev(1), dp_dev(-1), t_dev(1), t_dev(-1)):
        pl.semaphore_signal(barrier, 1, device_id=dev, device_id_type=MESH_ID)
    pl.semaphore_wait(barrier, 4)

    streams = []
    sem_at = 0
    for block in range(4):
        direction = 1 if block % 2 == 0 else -1
        g = bufs[block]
        if block < 2:
            first = (n_dp, me_dp, (dp_dev(direction), direction), lambda c, g=g: g.at[me_t, c])
            second = (n_t, me_t, (t_dev(direction), direction), lambda c, g=g: g.at[c])
        else:
            first = (n_t, me_t, (t_dev(direction), direction), lambda c, g=g: g.at[me_dp, c])
            second = (n_dp, me_dp, (dp_dev(direction), direction), lambda c, g=g: g.at[c])

        def stream(first=first, second=second, base=sem_at):
            n1, me1, to1, chunk1 = first
            copies = []
            for copies in gather_phase(n1, me1, to1, chunk1, send_sems, recv_sems, base):
                yield
            done1 = copies
            n2, me2, to2, chunk2 = second
            for copies in gather_phase(n2, me2, to2, chunk2, send_sems, recv_sems, base + n1 - 1):
                yield
            for copy in done1 + copies:
                copy.wait_send()

        streams.append(stream())
        sem_at += n_dp + n_t - 2

    run_in_order(streams, order)

    for block in range(4):
        cols = pl.ds(sum(widths[:block]), widths[block])
        for d in range(n_dp):
            for t in range(n_t):
                piece = bufs[block][t, d] if block < 2 else bufs[block][d, t]
                o_ref[pl.ds((d * n_t + t) * rows, rows), cols] = piece


def row_gather(x, n_dp, n_t):
    rows, model_width = x.shape
    widths, order = split_plan(n_dp, n_t, rows, model_width, False)
    scratch = [
        pltpu.VMEM((n_t, n_dp, rows, widths[0]), jnp.bfloat16),
        pltpu.VMEM((n_t, n_dp, rows, widths[1]), jnp.bfloat16),
        pltpu.VMEM((n_dp, n_t, rows, widths[2]), jnp.bfloat16),
        pltpu.VMEM((n_dp, n_t, rows, widths[3]), jnp.bfloat16),
    ]
    copies = 4 * (n_dp + n_t - 2)
    scratch += [pltpu.SemaphoreType.DMA((copies,)), pltpu.SemaphoreType.DMA((copies,))]
    return pl.pallas_call(
        functools.partial(row_gather_kernel, n_dp, n_t, tuple(widths), tuple(order)),
        out_shape=jax.ShapeDtypeStruct((n_dp * n_t * rows, model_width), jnp.bfloat16),
        in_specs=[pl.BlockSpec(memory_space=pltpu.VMEM)],
        out_specs=pl.BlockSpec(memory_space=pltpu.VMEM),
        scratch_shapes=scratch,
        compiler_params=pltpu.CompilerParams(
            collective_id=1, has_side_effects=True, vmem_limit_bytes=60 * 1024 * 1024
        ),
    )(x)


def head_sum_kernel(n_t, x_ref, o_ref, recv0, send0, recv1, send1, recv_sems, send_sems):
    me_dp = lax.axis_index("dp")
    me_e = lax.axis_index("expert")
    me_t = lax.axis_index("tensor")
    rows = o_ref.shape[0]
    width = o_ref.shape[1] // 2

    def t_dev(d):
        return (me_dp, me_e, lax.rem(me_t + n_t + d, n_t))

    barrier = pltpu.get_barrier_semaphore()
    for dev in (t_dev(1), t_dev(-1)):
        pl.semaphore_signal(barrier, 1, device_id=dev, device_id_type=MESH_ID)
    pl.semaphore_wait(barrier, 2)
    streams = []
    for block, (recv, send0_buf) in enumerate(((recv0, send0), (recv1, send1))):
        cols = pl.ds(block * width, width)
        direction = 1 if block == 0 else -1
        own = lambda c, i, cols=cols: x_ref[pl.ds(pl.multiple_of(c * rows, 8), rows), cols].astype(jnp.float32)

        def finish(i, v, cols=cols):
            o_ref[:, cols] = v.astype(o_ref.dtype)

        def stream(own=own, recv=recv, send0_buf=send0_buf, finish=finish, direction=direction, base=block):
            copies = []
            for copies in ring_phase(n_t, me_t, (t_dev(direction), direction), own, 1, recv, send0_buf,
                                     send_sems, recv_sems, base * (n_t - 1), finish):
                yield
            for copy in copies:
                copy.wait_send()

        streams.append(stream())
    run_in_order(streams, [0, 1] * n_t)


def head_sum(x, n_t):
    rows, model_width = x.shape[0] // n_t, x.shape[1]
    width = model_width // 2
    scratch = []
    for _ in range(2):
        scratch += [
            pltpu.VMEM((n_t - 1, 1, rows, width), jnp.bfloat16),
            pltpu.VMEM((1, rows, width), jnp.bfloat16),
        ]
    copies = 2 * (n_t - 1)
    scratch += [pltpu.SemaphoreType.DMA((copies,)), pltpu.SemaphoreType.DMA((copies,))]
    return pl.pallas_call(
        functools.partial(head_sum_kernel, n_t),
        out_shape=jax.ShapeDtypeStruct((rows, model_width), jnp.bfloat16),
        in_specs=[pl.BlockSpec(memory_space=pltpu.VMEM)],
        out_specs=pl.BlockSpec(memory_space=pltpu.VMEM),
        scratch_shapes=scratch,
        compiler_params=pltpu.CompilerParams(collective_id=2, has_side_effects=True),
    )(x)


def expert_exchange_kernel(n_e, x_ref, o_ref, recv, recv_sems, send_sems):
    me_dp = lax.axis_index("dp")
    me_e = lax.axis_index("expert")
    me_t = lax.axis_index("tensor")
    barrier = pltpu.get_barrier_semaphore()
    for k in range(1, n_e):
        pl.semaphore_signal(barrier, 1, device_id=(me_dp, lax.rem(me_e + k, n_e), me_t),
                            device_id_type=MESH_ID)
    pl.semaphore_wait(barrier, n_e - 1)
    copies = []
    for k in range(1, n_e):
        target = lax.rem(me_e + k, n_e)
        copy = pltpu.make_async_remote_copy(
            src_ref=x_ref.at[target],
            dst_ref=recv.at[me_e],
            send_sem=send_sems.at[k - 1],
            recv_sem=recv_sems.at[k - 1],
            device_id=(me_dp, target, me_t),
            device_id_type=MESH_ID,
        )
        copy.start()
        copies.append(copy)
    o_ref[me_e] = x_ref[me_e]
    for k in range(1, n_e):
        copies[k - 1].wait_recv()
        source = lax.rem(me_e + n_e - k, n_e)
        o_ref[source] = recv[source]
    for copy in copies:
        copy.wait_send()


def expert_exchange(x, collective):
    n_e = x.shape[0]
    return pl.pallas_call(
        functools.partial(expert_exchange_kernel, n_e),
        out_shape=jax.ShapeDtypeStruct(x.shape, x.dtype),
        in_specs=[pl.BlockSpec(memory_space=pltpu.VMEM)],
        out_specs=pl.BlockSpec(memory_space=pltpu.VMEM),
        scratch_shapes=[
            pltpu.VMEM(x.shape, x.dtype),
            pltpu.SemaphoreType.DMA((n_e - 1,)),
            pltpu.SemaphoreType.DMA((n_e - 1,)),
        ],
        compiler_params=pltpu.CompilerParams(collective_id=collective, has_side_effects=True),
    )(x)


def gather_feed_phase(n, me, step_to, chunk, send_sems, recv_sems, first_sem, process, own_too):
    copies = []
    for s in range(n - 1):
        c = lax.rem(me + n * 2 - step_to[1] * s, n)
        if s > 0:
            copies[-1].wait_recv()
        copy = pltpu.make_async_remote_copy(
            src_ref=chunk(c),
            dst_ref=chunk(c),
            send_sem=send_sems.at[first_sem + s],
            recv_sem=recv_sems.at[first_sem + s],
            device_id=step_to[0],
            device_id_type=MESH_ID,
        )
        copy.start()
        copies.append(copy)
        if s > 0 or own_too:
            process(c)
        yield copies
    copies[-1].wait_recv()
    process(lax.rem(me + n * 2 - step_to[1] * (n - 1), n))
    yield copies


def expert_front_kernel(n_dp, n_t, widths, order, x_ref, wg_ref, wu_ref, o_ref, *scratch):
    recv_sems, send_sems = scratch[-2], scratch[-1]
    gate_acc, up_acc = scratch[-4], scratch[-3]
    bufs = scratch[:-4]
    me_dp = lax.axis_index("dp")
    me_t = lax.axis_index("tensor")
    me_e = lax.axis_index("expert")
    rows = x_ref.shape[0]

    def dp_dev(d):
        return (lax.rem(me_dp + n_dp + d, n_dp), me_e, me_t)

    def t_dev(d):
        return (me_dp, me_e, lax.rem(me_t + n_t + d, n_t))

    gate_acc[...] = jnp.zeros_like(gate_acc)
    up_acc[...] = jnp.zeros_like(up_acc)
    for block in range(4):
        cols = pl.ds(sum(widths[:block]), widths[block])
        if block < 2:
            bufs[block][me_t, me_dp] = x_ref[:, cols]
        else:
            bufs[block][me_dp, me_t] = x_ref[:, cols]

    barrier = pltpu.get_barrier_semaphore()
    for dev in (dp_dev(1), dp_dev(-1), t_dev(1), t_dev(-1)):
        pl.semaphore_signal(barrier, 1, device_id=dev, device_id_type=MESH_ID)
    pl.semaphore_wait(barrier, 4)

    def feed(piece, row_chunk, cols):
        start = pl.multiple_of(row_chunk * rows, 16)
        v = piece[...]
        gate_acc[pl.ds(start, rows), :] += jnp.dot(v, wg_ref[cols, :], preferred_element_type=jnp.float32)
        up_acc[pl.ds(start, rows), :] += jnp.dot(v, wu_ref[cols, :], preferred_element_type=jnp.float32)

    streams = []
    sem_at = 0
    for block in range(4):
        direction = 1 if block % 2 == 0 else -1
        g = bufs[block]
        cols = pl.ds(sum(widths[:block]), widths[block])
        if block < 2:
            def p1(c, g=g, cols=cols):
                feed(g.at[me_t, c], c * n_t + me_t, cols)

            def p2(c, g=g, cols=cols):
                def body(d, carry):
                    feed(g.at[c, d], d * n_t + c, cols)
                    return carry
                lax.fori_loop(0, n_dp, body, 0)
            first = (n_dp, me_dp, (dp_dev(direction), direction), lambda c, g=g: g.at[me_t, c], p1)
            second = (n_t, me_t, (t_dev(direction), direction), lambda c, g=g: g.at[c], p2)
        else:
            def p1(c, g=g, cols=cols):
                feed(g.at[me_dp, c], me_dp * n_t + c, cols)

            def p2(c, g=g, cols=cols):
                def body(t, carry):
                    feed(g.at[c, t], c * n_t + t, cols)
                    return carry
                lax.fori_loop(0, n_t, body, 0)
            first = (n_t, me_t, (t_dev(direction), direction), lambda c, g=g: g.at[me_dp, c], p1)
            second = (n_dp, me_dp, (dp_dev(direction), direction), lambda c, g=g: g.at[c], p2)

        def stream(first=first, second=second, base=sem_at):
            n1, me1, to1, chunk1, proc1 = first
            copies = []
            for copies in gather_feed_phase(n1, me1, to1, chunk1, send_sems, recv_sems, base, proc1, True):
                yield
            done1 = copies
            n2, me2, to2, chunk2, proc2 = second
            for copies in gather_feed_phase(n2, me2, to2, chunk2, send_sems, recv_sems, base + n1 - 1,
                                            proc2, False):
                yield
            for copy in done1 + copies:
                copy.wait_send()

        streams.append(stream())
        sem_at += n_dp + n_t - 2

    run_in_order(streams, order)

    tile = 128

    def finish(i, carry):
        at = pl.ds(pl.multiple_of(i * tile, tile), tile)
        gate = gate_acc[at, :]
        o_ref[at, :] = (gate / (1.0 + jnp.exp(-gate)) * up_acc[at, :]).astype(o_ref.dtype)
        return carry

    lax.fori_loop(0, o_ref.shape[0] // tile, finish, 0)


def expert_front(x, gate_w, up_w, n_dp, n_t):
    rows, model_width = x.shape
    inner = gate_w.shape[1]
    widths, order = split_plan(n_dp, n_t, rows, model_width, False)
    scratch = [
        pltpu.VMEM((n_t, n_dp, rows, widths[0]), jnp.bfloat16),
        pltpu.VMEM((n_t, n_dp, rows, widths[1]), jnp.bfloat16),
        pltpu.VMEM((n_dp, n_t, rows, widths[2]), jnp.bfloat16),
        pltpu.VMEM((n_dp, n_t, rows, widths[3]), jnp.bfloat16),
        pltpu.VMEM((n_dp * n_t * rows, inner), jnp.float32),
        pltpu.VMEM((n_dp * n_t * rows, inner), jnp.float32),
    ]
    copies = 4 * (n_dp + n_t - 2)
    scratch += [pltpu.SemaphoreType.DMA((copies,)), pltpu.SemaphoreType.DMA((copies,))]
    return pl.pallas_call(
        functools.partial(expert_front_kernel, n_dp, n_t, tuple(widths), tuple(order)),
        out_shape=jax.ShapeDtypeStruct((n_dp * n_t * rows, inner), jnp.bfloat16),
        in_specs=[pl.BlockSpec(memory_space=pltpu.VMEM)] * 3,
        out_specs=pl.BlockSpec(memory_space=pltpu.VMEM),
        scratch_shapes=scratch,
        compiler_params=pltpu.CompilerParams(
            collective_id=1, has_side_effects=True, vmem_limit_bytes=60 * 1024 * 1024
        ),
    )(x, gate_w, up_w)


def moe_sum(hidden, down, n_dp, n_t):
    rows, model_width = hidden.shape[0] // (n_dp * n_t), down.shape[1]
    widths, order = split_plan(n_dp, n_t, rows, model_width, True)
    scratch = []
    for block in range(4):
        width = widths[block]
        if block < 2:
            n1, lead, n2 = n_dp, n_t, n_t
        else:
            n1, lead, n2 = n_t, n_dp, n_dp
        scratch += [
            pltpu.VMEM((n1 - 1, lead, rows, width), jnp.bfloat16),
            pltpu.VMEM((lead, rows, width), jnp.bfloat16),
            pltpu.VMEM((lead, rows, width), jnp.float32),
            pltpu.VMEM((n2 - 1, 1, rows, width), jnp.bfloat16),
            pltpu.VMEM((1, rows, width), jnp.bfloat16),
        ]
    copies = 4 * (n_dp + n_t - 2)
    scratch += [pltpu.SemaphoreType.DMA((copies,)), pltpu.SemaphoreType.DMA((copies,))]
    return pl.pallas_call(
        functools.partial(moe_sum_kernel, n_dp, n_t, tuple(widths), tuple(order)),
        out_shape=jax.ShapeDtypeStruct((rows, model_width), jnp.bfloat16),
        in_specs=[pl.BlockSpec(memory_space=pltpu.VMEM)] * 2,
        out_specs=pl.BlockSpec(memory_space=pltpu.VMEM),
        scratch_shapes=scratch,
        compiler_params=pltpu.CompilerParams(
            collective_id=0, has_side_effects=True, vmem_limit_bytes=60 * 1024 * 1024
        ),
    )(hidden, down)


def normalize(parts):
    highest = reduce(
        jnp.maximum,
        [
            jnp.max(jnp.where(visible, scores, -jnp.inf), axis=-1, keepdims=True)
            for scores, visible in parts
        ],
    )
    portions = [jnp.where(visible, jnp.exp(scores - highest), 0.0) for scores, visible in parts]
    denominator = reduce(
        jnp.add, [jnp.sum(portion, axis=-1, keepdims=True) for portion in portions]
    )
    return [(portion / denominator).astype(jnp.bfloat16) for portion in portions]


def attend(question_vectors, new_keys, new_values, key_pages, value_pages, table, spans):
    rows_all, head_count, head_width = question_vectors.shape
    kv_heads = new_keys.shape[1]
    group_size = head_count // kv_heads
    single_count = spans.shape[0] - 1
    page_count = table.shape[1]
    page_width = key_pages.shape[2]
    context = page_count * page_width
    inverse_root = 1.0 / math.sqrt(head_width)
    page_keys = key_pages[table]
    page_values = value_pages[table]
    grouped = question_vectors.reshape(rows_all, kv_heads, group_size, head_width)
    positions = jnp.arange(context, dtype=jnp.int32)
    single_q = grouped[:single_count]
    cache_dec = (
        jnp.einsum(
            "rkgh,rmkph->rkgmp",
            single_q,
            page_keys[:single_count],
            preferred_element_type=jnp.float32,
        ).reshape(single_count, kv_heads, group_size, context)
        * inverse_root
    )
    seen_dec = (positions[None, :] < spans[:single_count, None])[:, None, None, :]
    own_dec = (
        jnp.einsum(
            "rkgh,rkh->rkg", single_q, new_keys[:single_count], preferred_element_type=jnp.float32
        )[..., None]
        * inverse_root
    )
    weight_cache, weight_own = normalize(
        [(cache_dec, seen_dec), (own_dec, jnp.full(own_dec.shape, True))]
    )
    out_dec = jnp.einsum(
        "rkgmp,rmkph->rkgh",
        weight_cache.reshape(single_count, kv_heads, group_size, page_count, page_width),
        page_values[:single_count],
        preferred_element_type=jnp.float32,
    )
    out_dec = (
        out_dec
        + weight_own.astype(jnp.float32)
        * new_values[:single_count].astype(jnp.float32)[:, :, None, :]
    )
    prompt_q = grouped[single_count:]
    prompt_rows = rows_all - single_count
    cache_pro = (
        jnp.einsum(
            "rkgh,mkph->rkgmp",
            prompt_q,
            page_keys[single_count],
            preferred_element_type=jnp.float32,
        ).reshape(prompt_rows, kv_heads, group_size, context)
        * inverse_root
    )
    seen_pro = (positions < spans[single_count])[None, None, None, :]
    new_pro = (
        jnp.einsum(
            "rkgh,mkh->rkgm", prompt_q, new_keys[single_count:], preferred_element_type=jnp.float32
        )
        * inverse_root
    )
    prompt_index = jnp.arange(prompt_rows, dtype=jnp.int32)
    causal = (prompt_index[:, None] >= prompt_index[None, :])[:, None, None, :]
    weight_cpro, weight_npro = normalize([(cache_pro, seen_pro), (new_pro, causal)])
    out_pro = jnp.einsum(
        "rkgmp,mkph->rkgh",
        weight_cpro.reshape(prompt_rows, kv_heads, group_size, page_count, page_width),
        page_values[single_count],
        preferred_element_type=jnp.float32,
    )
    out_pro = out_pro + jnp.einsum(
        "rkgm,mkh->rkgh", weight_npro, new_values[single_count:], preferred_element_type=jnp.float32
    )
    joined = jnp.concatenate([out_dec, out_pro], axis=0).astype(jnp.bfloat16)
    return joined.reshape(rows_all, head_count * head_width)


def slot_table(member, ranking, keeping, slot_count):
    slot_hit = (
        ranking[:, :, None, None] == jnp.arange(slot_count, dtype=jnp.int32)[None, None, None, :]
    )
    return ((member[..., None] > 0) & keeping[:, :, None, None] & slot_hit).astype(jnp.bfloat16)


def expert_pass(send, gating_matrices, expand_matrices, contract_matrices):
    specialist_index, slot_count, model_width = send.shape
    local_count = gating_matrices.shape[0]
    assert local_count == 1
    arrived = expert_exchange(send, 3).reshape(specialist_index * slot_count, model_width)
    inner = gating_matrices.shape[1]
    padded = -(-inner // 128) * 128
    widen = ((0, padded - inner), (0, 0))
    hidden = expert_front(
        arrived,
        jnp.pad(gating_matrices[0], widen).T,
        jnp.pad(expand_matrices[0], widen).T,
        lax.axis_size("dp"),
        lax.axis_size("tensor"),
    )
    down = jnp.pad(contract_matrices[0], widen)
    n_dp, n_t = lax.axis_size("dp"), lax.axis_size("tensor")
    summed = moe_sum(hidden, down, n_dp, n_t)
    return expert_exchange(summed.reshape(specialist_index, slot_count, model_width), 4)


def local(
    skip_stream_entry,
    question_vectors,
    fresh_lookup_vectors,
    fresh_content_vectors,
    stored_lookup_sheets,
    stored_content_sheets,
    sequence_sheet_map,
    stored_position_counts,
    attention_merge_matrix,
    premix_scale_factor,
    chosen_specialists,
    selection_shares,
    allowed_placements,
    favored_specialist,
    gating_matrices,
    expand_matrices,
    contract_matrices,
):
    token_count = chosen_specialists.shape[0]
    specialist_index = allowed_placements.shape[0]
    picked = (
        chosen_specialists[:, :, None]
        == jnp.arange(specialist_index, dtype=jnp.int32)[None, None, :]
    ).astype(jnp.int32)
    flat_routes = picked.reshape(token_count * 2, specialist_index)
    busiest_specialist = favored_specialist[0]
    before = (jnp.cumsum(flat_routes, axis=0) - flat_routes).reshape(
        token_count, 2, specialist_index
    )
    ranking = jnp.sum(before * picked, axis=2)
    placement_ceiling = jnp.where(
        jnp.arange(specialist_index, dtype=jnp.int32) == busiest_specialist,
        PLACEMENT_MOST,
        allowed_placements,
    )
    keeping = ranking < jnp.sum(picked * placement_ceiling[None, None, :], axis=2)
    row_total = question_vectors.shape[0]
    heads_out = attend(
        question_vectors.reshape(row_total, -1, HD),
        fresh_lookup_vectors.reshape(row_total, -1, HD),
        fresh_content_vectors.reshape(row_total, -1, HD),
        stored_lookup_sheets,
        stored_content_sheets,
        sequence_sheet_map,
        stored_position_counts,
    )
    own_attn = head_sum(
        jnp.dot(heads_out, attention_merge_matrix, preferred_element_type=jnp.float32).astype(
            jnp.bfloat16
        ),
        lax.axis_size("tensor"),
    ).astype(jnp.float32)
    stream = (skip_stream_entry.astype(jnp.float32) + own_attn).astype(jnp.bfloat16)
    wide = stream.astype(jnp.float32)
    squares = jnp.mean(wide * wide, axis=1, keepdims=True)
    normed = (wide * lax.rsqrt(squares + 1e-05) * premix_scale_factor.astype(jnp.float32)).astype(
        jnp.bfloat16
    )
    main_slots = PLACEMENT_MOST
    table_main = slot_table(picked, ranking, keeping, main_slots)
    send = jnp.einsum(
        "nkes,nd->esd", table_main, normed, preferred_element_type=jnp.float32
    ).astype(jnp.bfloat16)
    expert_out = expert_pass(send, gating_matrices, expand_matrices, contract_matrices)
    chosen = jnp.einsum("nkes,esd->nkd", table_main, expert_out, preferred_element_type=jnp.float32)
    mixed = jnp.sum(selection_shares[:, :, None] * chosen, axis=1)
    return (wide + mixed).astype(jnp.bfloat16)


def solution(mesh):
    placed = (
        P(("dp", "expert", "tensor"), None),
        P(("dp", "expert"), "tensor"),
        P(("dp", "expert"), "tensor"),
        P(("dp", "expert"), "tensor"),
        P(("dp", "expert"), "tensor", None, None),
        P(("dp", "expert"), "tensor", None, None),
        P(("dp", "expert"), None),
        P(("dp", "expert")),
        P("tensor", None),
        P(),
        P(("dp", "expert", "tensor"), None),
        P(("dp", "expert", "tensor"), None),
        P(),
        P(),
        P("expert", ("dp", "tensor"), None),
        P("expert", ("dp", "tensor"), None),
        P("expert", ("dp", "tensor"), None),
    )
    return jax.shard_map(
        local,
        mesh=mesh,
        in_specs=placed,
        out_specs=P(("dp", "expert", "tensor"), None),
        check_vma=False,
    )
```

```python
from functools import reduce
import functools
import math

import jax
import jax.numpy as jnp
from jax import lax
from jax.experimental import pallas as pl
from jax.experimental.pallas import tpu as pltpu
from jax.sharding import PartitionSpec as P

HD = 128
PLACEMENT_MOST = 6


MESH_ID = pl.DeviceIdType.MESH


def plan_order(events, rate=50000.0, latency=1.5, per_step=0.3):
    ready = [0.0] * len(events)
    at = [0] * len(events)
    free = {}
    clock = 0.0
    order = []
    while True:
        live = [i for i in range(len(events)) if at[i] < len(events[i])]
        if not live:
            return order, clock
        i = min(live, key=lambda k: (ready[k], k))
        clock = max(clock, ready[i]) + per_step
        send = events[i][at[i]]
        if send is None:
            ready[i] = clock
        else:
            link, size = send
            start = max(clock, free.get(link, 0.0))
            free[link] = start + size / rate
            ready[i] = free[link] + latency
        order.append(i)
        at[i] += 1


def ring_events(n1, n2, link1, link2, size1, size2):
    return [(link1, size1)] * (n1 - 1) + [None] + [(link2, size2)] * (n2 - 1) + [None]


def split_plan(n_dp, n_t, rows, model_width, reduce):
    best = None
    for first_dp in range(128, model_width // 2, 128):
        widths = [first_dp, first_dp, model_width // 2 - first_dp, model_width // 2 - first_dp]
        events = []
        for block, width in enumerate(widths):
            unit = rows * width * 2
            sign = "+" if block % 2 == 0 else "-"
            if block < 2:
                big1, big2 = (n_t * unit, unit) if reduce else (unit, n_dp * unit)
                events.append(ring_events(n_dp, n_t, "z" + sign, "y" + sign, big1, big2))
            else:
                big1, big2 = (n_dp * unit, unit) if reduce else (unit, n_t * unit)
                events.append(ring_events(n_t, n_dp, "y" + sign, "z" + sign, big1, big2))
        order, finish = plan_order(events)
        if best is None or finish < best[0]:
            best = (finish, widths, order)
    return best[1], best[2]


def run_in_order(streams, order):
    for i in order:
        next(streams[i])
    for st in streams:
        for _ in st:
            pass


def ring_phase(n, me, step_to, own, chunk_lead, recv, send0, send_sems, recv_sems, first_sem, finish):
    copies = []
    for s in range(n - 1):
        c = lax.rem(me + n * 2 - step_to[1] * (s + 1), n)
        if s == 0:
            for i in range(chunk_lead):
                send0[i] = own(c, i).astype(send0.dtype)
            src = send0
        else:
            copies[-1].wait_recv()
            for i in range(chunk_lead):
                recv[s - 1, i] = (own(c, i) + recv[s - 1, i].astype(jnp.float32)).astype(recv.dtype)
            src = recv.at[s - 1]
        copy = pltpu.make_async_remote_copy(
            src_ref=src,
            dst_ref=recv.at[s],
            send_sem=send_sems.at[first_sem + s],
            recv_sem=recv_sems.at[first_sem + s],
            device_id=step_to[0],
            device_id_type=MESH_ID,
        )
        copy.start()
        copies.append(copy)
        yield copies
    copies[-1].wait_recv()
    for i in range(chunk_lead):
        finish(i, own(me, i) + recv[n - 2, i].astype(jnp.float32))
    yield copies


def block_product(h_ref, w_ref, chunk, cols, rows):
    start = pl.multiple_of(chunk * rows, 16)
    product = jnp.dot(h_ref[pl.ds(start, rows), :], w_ref[:, cols], preferred_element_type=jnp.float32)
    return product.astype(jnp.bfloat16).astype(jnp.float32)


def moe_sum_kernel(n_dp, n_t, widths, order, h_ref, w_ref, o_ref, *scratch):
    recv_sems, send_sems = scratch[-2], scratch[-1]
    bufs = scratch[:-2]
    me_dp = lax.axis_index("dp")
    me_t = lax.axis_index("tensor")
    me_e = lax.axis_index("expert")

    def dp_dev(d):
        return (lax.rem(me_dp + n_dp + d, n_dp), me_e, me_t)

    def t_dev(d):
        return (me_dp, me_e, lax.rem(me_t + n_t + d, n_t))

    barrier = pltpu.get_barrier_semaphore()
    for dev in (dp_dev(1), dp_dev(-1), t_dev(1), t_dev(-1)):
        pl.semaphore_signal(barrier, 1, device_id=dev, device_id_type=MESH_ID)
    pl.semaphore_wait(barrier, 4)

    streams = []
    sem_at = 0
    for block in range(4):
        cols = pl.ds(sum(widths[:block]), widths[block])
        direction = 1 if block % 2 == 0 else -1
        r1, s1, acc, r2, s2 = bufs[block * 5: block * 5 + 5]
        if block < 2:
            first = (n_dp, me_dp, (dp_dev(direction), direction), n_t)
            own1 = lambda c, i, cols=cols: block_product(h_ref, w_ref, c * n_t + i, cols, o_ref.shape[0])
            second = (n_t, me_t, (t_dev(direction), direction))
        else:
            first = (n_t, me_t, (t_dev(direction), direction), n_dp)
            own1 = lambda c, i, cols=cols: block_product(h_ref, w_ref, i * n_t + c, cols, o_ref.shape[0])
            second = (n_dp, me_dp, (dp_dev(direction), direction))

        def fin1(i, v, acc=acc):
            acc[i] = v

        def fin2(i, v, cols=cols):
            o_ref[:, cols] = v.astype(o_ref.dtype)

        own2 = lambda c, i, acc=acc: acc[c]

        def stream(first=first, second=second, own1=own1, own2=own2, r1=r1, s1=s1, r2=r2, s2=s2,
                   fin1=fin1, fin2=fin2, base=sem_at):
            n1, me1, to1, lead = first
            copies = []
            for copies in ring_phase(n1, me1, to1, own1, lead, r1, s1, send_sems, recv_sems, base, fin1):
                yield
            done1 = copies
            n2, me2, to2 = second
            for copies in ring_phase(n2, me2, to2, own2, 1, r2, s2, send_sems, recv_sems, base + n1 - 1,
                                     lambda i, v: fin2(i, v)):
                yield
            for copy in done1 + copies:
                copy.wait_send()

        streams.append(stream())
        sem_at += n_dp + n_t - 2

    run_in_order(streams, order)


def gather_phase(n, me, step_to, chunk, send_sems, recv_sems, first_sem):
    copies = []
    for s in range(n - 1):
        c = lax.rem(me + n * 2 - step_to[1] * s, n)
        if s > 0:
            copies[-1].wait_recv()
        copy = pltpu.make_async_remote_copy(
            src_ref=chunk(c),
            dst_ref=chunk(c),
            send_sem=send_sems.at[first_sem + s],
            recv_sem=recv_sems.at[first_sem + s],
            device_id=step_to[0],
            device_id_type=MESH_ID,
        )
        copy.start()
        copies.append(copy)
        yield copies
    copies[-1].wait_recv()
    yield copies


def row_gather_kernel(n_dp, n_t, widths, order, x_ref, o_ref, *scratch):
    recv_sems, send_sems = scratch[-2], scratch[-1]
    bufs = scratch[:-2]
    me_dp = lax.axis_index("dp")
    me_t = lax.axis_index("tensor")
    me_e = lax.axis_index("expert")
    rows = x_ref.shape[0]

    def dp_dev(d):
        return (lax.rem(me_dp + n_dp + d, n_dp), me_e, me_t)

    def t_dev(d):
        return (me_dp, me_e, lax.rem(me_t + n_t + d, n_t))

    for block in range(4):
        cols = pl.ds(sum(widths[:block]), widths[block])
        if block < 2:
            bufs[block][me_t, me_dp] = x_ref[:, cols]
        else:
            bufs[block][me_dp, me_t] = x_ref[:, cols]

    barrier = pltpu.get_barrier_semaphore()
    for dev in (dp_dev(1), dp_dev(-1), t_dev(1), t_dev(-1)):
        pl.semaphore_signal(barrier, 1, device_id=dev, device_id_type=MESH_ID)
    pl.semaphore_wait(barrier, 4)

    streams = []
    sem_at = 0
    for block in range(4):
        direction = 1 if block % 2 == 0 else -1
        g = bufs[block]
        if block < 2:
            first = (n_dp, me_dp, (dp_dev(direction), direction), lambda c, g=g: g.at[me_t, c])
            second = (n_t, me_t, (t_dev(direction), direction), lambda c, g=g: g.at[c])
        else:
            first = (n_t, me_t, (t_dev(direction), direction), lambda c, g=g: g.at[me_dp, c])
            second = (n_dp, me_dp, (dp_dev(direction), direction), lambda c, g=g: g.at[c])

        def stream(first=first, second=second, base=sem_at):
            n1, me1, to1, chunk1 = first
            copies = []
            for copies in gather_phase(n1, me1, to1, chunk1, send_sems, recv_sems, base):
                yield
            done1 = copies
            n2, me2, to2, chunk2 = second
            for copies in gather_phase(n2, me2, to2, chunk2, send_sems, recv_sems, base + n1 - 1):
                yield
            for copy in done1 + copies:
                copy.wait_send()

        streams.append(stream())
        sem_at += n_dp + n_t - 2

    run_in_order(streams, order)

    for block in range(4):
        cols = pl.ds(sum(widths[:block]), widths[block])
        for d in range(n_dp):
            for t in range(n_t):
                piece = bufs[block][t, d] if block < 2 else bufs[block][d, t]
                o_ref[pl.ds((d * n_t + t) * rows, rows), cols] = piece


def row_gather(x, n_dp, n_t):
    rows, model_width = x.shape
    widths, order = split_plan(n_dp, n_t, rows, model_width, False)
    scratch = [
        pltpu.VMEM((n_t, n_dp, rows, widths[0]), jnp.bfloat16),
        pltpu.VMEM((n_t, n_dp, rows, widths[1]), jnp.bfloat16),
        pltpu.VMEM((n_dp, n_t, rows, widths[2]), jnp.bfloat16),
        pltpu.VMEM((n_dp, n_t, rows, widths[3]), jnp.bfloat16),
    ]
    copies = 4 * (n_dp + n_t - 2)
    scratch += [pltpu.SemaphoreType.DMA((copies,)), pltpu.SemaphoreType.DMA((copies,))]
    return pl.pallas_call(
        functools.partial(row_gather_kernel, n_dp, n_t, tuple(widths), tuple(order)),
        out_shape=jax.ShapeDtypeStruct((n_dp * n_t * rows, model_width), jnp.bfloat16),
        in_specs=[pl.BlockSpec(memory_space=pltpu.VMEM)],
        out_specs=pl.BlockSpec(memory_space=pltpu.VMEM),
        scratch_shapes=scratch,
        compiler_params=pltpu.CompilerParams(
            collective_id=1, has_side_effects=True, vmem_limit_bytes=60 * 1024 * 1024
        ),
    )(x)


def head_sum_kernel(n_t, x_ref, o_ref, recv0, send0, recv1, send1, recv_sems, send_sems):
    me_dp = lax.axis_index("dp")
    me_e = lax.axis_index("expert")
    me_t = lax.axis_index("tensor")
    rows = o_ref.shape[0]
    width = o_ref.shape[1] // 2

    def t_dev(d):
        return (me_dp, me_e, lax.rem(me_t + n_t + d, n_t))

    barrier = pltpu.get_barrier_semaphore()
    for dev in (t_dev(1), t_dev(-1)):
        pl.semaphore_signal(barrier, 1, device_id=dev, device_id_type=MESH_ID)
    pl.semaphore_wait(barrier, 2)
    streams = []
    for block, (recv, send0_buf) in enumerate(((recv0, send0), (recv1, send1))):
        cols = pl.ds(block * width, width)
        direction = 1 if block == 0 else -1
        own = lambda c, i, cols=cols: x_ref[pl.ds(pl.multiple_of(c * rows, 8), rows), cols].astype(jnp.float32)

        def finish(i, v, cols=cols):
            o_ref[:, cols] = v.astype(o_ref.dtype)

        def stream(own=own, recv=recv, send0_buf=send0_buf, finish=finish, direction=direction, base=block):
            copies = []
            for copies in ring_phase(n_t, me_t, (t_dev(direction), direction), own, 1, recv, send0_buf,
                                     send_sems, recv_sems, base * (n_t - 1), finish):
                yield
            for copy in copies:
                copy.wait_send()

        streams.append(stream())
    run_in_order(streams, [0, 1] * n_t)


def head_sum(x, n_t):
    rows, model_width = x.shape[0] // n_t, x.shape[1]
    width = model_width // 2
    scratch = []
    for _ in range(2):
        scratch += [
            pltpu.VMEM((n_t - 1, 1, rows, width), jnp.bfloat16),
            pltpu.VMEM((1, rows, width), jnp.bfloat16),
        ]
    copies = 2 * (n_t - 1)
    scratch += [pltpu.SemaphoreType.DMA((copies,)), pltpu.SemaphoreType.DMA((copies,))]
    return pl.pallas_call(
        functools.partial(head_sum_kernel, n_t),
        out_shape=jax.ShapeDtypeStruct((rows, model_width), jnp.bfloat16),
        in_specs=[pl.BlockSpec(memory_space=pltpu.VMEM)],
        out_specs=pl.BlockSpec(memory_space=pltpu.VMEM),
        scratch_shapes=scratch,
        compiler_params=pltpu.CompilerParams(collective_id=2, has_side_effects=True),
    )(x)


def expert_exchange_kernel(n_e, x_ref, o_ref, recv, recv_sems, send_sems):
    me_dp = lax.axis_index("dp")
    me_e = lax.axis_index("expert")
    me_t = lax.axis_index("tensor")
    barrier = pltpu.get_barrier_semaphore()
    for k in range(1, n_e):
        pl.semaphore_signal(barrier, 1, device_id=(me_dp, lax.rem(me_e + k, n_e), me_t),
                            device_id_type=MESH_ID)
    pl.semaphore_wait(barrier, n_e - 1)
    copies = []
    for k in range(1, n_e):
        target = lax.rem(me_e + k, n_e)
        copy = pltpu.make_async_remote_copy(
            src_ref=x_ref.at[target],
            dst_ref=recv.at[me_e],
            send_sem=send_sems.at[k - 1],
            recv_sem=recv_sems.at[k - 1],
            device_id=(me_dp, target, me_t),
            device_id_type=MESH_ID,
        )
        copy.start()
        copies.append(copy)
    o_ref[me_e] = x_ref[me_e]
    for k in range(1, n_e):
        copies[k - 1].wait_recv()
        source = lax.rem(me_e + n_e - k, n_e)
        o_ref[source] = recv[source]
    for copy in copies:
        copy.wait_send()


def expert_exchange(x, collective):
    n_e = x.shape[0]
    return pl.pallas_call(
        functools.partial(expert_exchange_kernel, n_e),
        out_shape=jax.ShapeDtypeStruct(x.shape, x.dtype),
        in_specs=[pl.BlockSpec(memory_space=pltpu.VMEM)],
        out_specs=pl.BlockSpec(memory_space=pltpu.VMEM),
        scratch_shapes=[
            pltpu.VMEM(x.shape, x.dtype),
            pltpu.SemaphoreType.DMA((n_e - 1,)),
            pltpu.SemaphoreType.DMA((n_e - 1,)),
        ],
        compiler_params=pltpu.CompilerParams(collective_id=collective, has_side_effects=True),
    )(x)


def gather_feed_phase(n, me, step_to, chunk, send_sems, recv_sems, first_sem, process, own_too):
    copies = []
    for s in range(n - 1):
        c = lax.rem(me + n * 2 - step_to[1] * s, n)
        if s > 0:
            copies[-1].wait_recv()
        copy = pltpu.make_async_remote_copy(
            src_ref=chunk(c),
            dst_ref=chunk(c),
            send_sem=send_sems.at[first_sem + s],
            recv_sem=recv_sems.at[first_sem + s],
            device_id=step_to[0],
            device_id_type=MESH_ID,
        )
        copy.start()
        copies.append(copy)
        if s > 0 or own_too:
            process(c)
        yield copies
    copies[-1].wait_recv()
    process(lax.rem(me + n * 2 - step_to[1] * (n - 1), n))
    yield copies


def expert_front_kernel(n_dp, n_t, widths, order, x_ref, wg_ref, wu_ref, o_ref, *scratch):
    recv_sems, send_sems = scratch[-2], scratch[-1]
    gate_acc, up_acc = scratch[-4], scratch[-3]
    bufs = scratch[:-4]
    me_dp = lax.axis_index("dp")
    me_t = lax.axis_index("tensor")
    me_e = lax.axis_index("expert")
    rows = x_ref.shape[0]

    def dp_dev(d):
        return (lax.rem(me_dp + n_dp + d, n_dp), me_e, me_t)

    def t_dev(d):
        return (me_dp, me_e, lax.rem(me_t + n_t + d, n_t))

    gate_acc[...] = jnp.zeros_like(gate_acc)
    up_acc[...] = jnp.zeros_like(up_acc)
    for block in range(4):
        cols = pl.ds(sum(widths[:block]), widths[block])
        if block < 2:
            bufs[block][me_t, me_dp] = x_ref[:, cols]
        else:
            bufs[block][me_dp, me_t] = x_ref[:, cols]

    barrier = pltpu.get_barrier_semaphore()
    for dev in (dp_dev(1), dp_dev(-1), t_dev(1), t_dev(-1)):
        pl.semaphore_signal(barrier, 1, device_id=dev, device_id_type=MESH_ID)
    pl.semaphore_wait(barrier, 4)

    def feed(piece, row_chunk, cols):
        start = pl.multiple_of(row_chunk * rows, 16)
        v = piece[...]
        gate_acc[pl.ds(start, rows), :] += jnp.dot(v, wg_ref[cols, :], preferred_element_type=jnp.float32)
        up_acc[pl.ds(start, rows), :] += jnp.dot(v, wu_ref[cols, :], preferred_element_type=jnp.float32)

    streams = []
    sem_at = 0
    for block in range(4):
        direction = 1 if block % 2 == 0 else -1
        g = bufs[block]
        cols = pl.ds(sum(widths[:block]), widths[block])
        if block < 2:
            def p1(c, g=g, cols=cols):
                feed(g.at[me_t, c], c * n_t + me_t, cols)

            def p2(c, g=g, cols=cols):
                def body(d, carry):
                    feed(g.at[c, d], d * n_t + c, cols)
                    return carry
                lax.fori_loop(0, n_dp, body, 0)
            first = (n_dp, me_dp, (dp_dev(direction), direction), lambda c, g=g: g.at[me_t, c], p1)
            second = (n_t, me_t, (t_dev(direction), direction), lambda c, g=g: g.at[c], p2)
        else:
            def p1(c, g=g, cols=cols):
                feed(g.at[me_dp, c], me_dp * n_t + c, cols)

            def p2(c, g=g, cols=cols):
                def body(t, carry):
                    feed(g.at[c, t], c * n_t + t, cols)
                    return carry
                lax.fori_loop(0, n_t, body, 0)
            first = (n_t, me_t, (t_dev(direction), direction), lambda c, g=g: g.at[me_dp, c], p1)
            second = (n_dp, me_dp, (dp_dev(direction), direction), lambda c, g=g: g.at[c], p2)

        def stream(first=first, second=second, base=sem_at):
            n1, me1, to1, chunk1, proc1 = first
            copies = []
            for copies in gather_feed_phase(n1, me1, to1, chunk1, send_sems, recv_sems, base, proc1, True):
                yield
            done1 = copies
            n2, me2, to2, chunk2, proc2 = second
            for copies in gather_feed_phase(n2, me2, to2, chunk2, send_sems, recv_sems, base + n1 - 1,
                                            proc2, False):
                yield
            for copy in done1 + copies:
                copy.wait_send()

        streams.append(stream())
        sem_at += n_dp + n_t - 2

    run_in_order(streams, order)

    tile = 128

    def finish(i, carry):
        at = pl.ds(pl.multiple_of(i * tile, tile), tile)
        gate = gate_acc[at, :]
        o_ref[at, :] = (gate / (1.0 + jnp.exp(-gate)) * up_acc[at, :]).astype(o_ref.dtype)
        return carry

    lax.fori_loop(0, o_ref.shape[0] // tile, finish, 0)


def expert_front(x, gate_w, up_w, n_dp, n_t):
    rows, model_width = x.shape
    inner = gate_w.shape[1]
    widths, order = split_plan(n_dp, n_t, rows, model_width, False)
    scratch = [
        pltpu.VMEM((n_t, n_dp, rows, widths[0]), jnp.bfloat16),
        pltpu.VMEM((n_t, n_dp, rows, widths[1]), jnp.bfloat16),
        pltpu.VMEM((n_dp, n_t, rows, widths[2]), jnp.bfloat16),
        pltpu.VMEM((n_dp, n_t, rows, widths[3]), jnp.bfloat16),
        pltpu.VMEM((n_dp * n_t * rows, inner), jnp.float32),
        pltpu.VMEM((n_dp * n_t * rows, inner), jnp.float32),
    ]
    copies = 4 * (n_dp + n_t - 2)
    scratch += [pltpu.SemaphoreType.DMA((copies,)), pltpu.SemaphoreType.DMA((copies,))]
    return pl.pallas_call(
        functools.partial(expert_front_kernel, n_dp, n_t, tuple(widths), tuple(order)),
        out_shape=jax.ShapeDtypeStruct((n_dp * n_t * rows, inner), jnp.bfloat16),
        in_specs=[pl.BlockSpec(memory_space=pltpu.VMEM)] * 3,
        out_specs=pl.BlockSpec(memory_space=pltpu.VMEM),
        scratch_shapes=scratch,
        compiler_params=pltpu.CompilerParams(
            collective_id=1, has_side_effects=True, vmem_limit_bytes=60 * 1024 * 1024
        ),
    )(x, gate_w, up_w)


def moe_sum(hidden, down, n_dp, n_t):
    rows, model_width = hidden.shape[0] // (n_dp * n_t), down.shape[1]
    widths, order = split_plan(n_dp, n_t, rows, model_width, True)
    scratch = []
    for block in range(4):
        width = widths[block]
        if block < 2:
            n1, lead, n2 = n_dp, n_t, n_t
        else:
            n1, lead, n2 = n_t, n_dp, n_dp
        scratch += [
            pltpu.VMEM((n1 - 1, lead, rows, width), jnp.bfloat16),
            pltpu.VMEM((lead, rows, width), jnp.bfloat16),
            pltpu.VMEM((lead, rows, width), jnp.float32),
            pltpu.VMEM((n2 - 1, 1, rows, width), jnp.bfloat16),
            pltpu.VMEM((1, rows, width), jnp.bfloat16),
        ]
    copies = 4 * (n_dp + n_t - 2)
    scratch += [pltpu.SemaphoreType.DMA((copies,)), pltpu.SemaphoreType.DMA((copies,))]
    return pl.pallas_call(
        functools.partial(moe_sum_kernel, n_dp, n_t, tuple(widths), tuple(order)),
        out_shape=jax.ShapeDtypeStruct((rows, model_width), jnp.bfloat16),
        in_specs=[pl.BlockSpec(memory_space=pltpu.VMEM)] * 2,
        out_specs=pl.BlockSpec(memory_space=pltpu.VMEM),
        scratch_shapes=scratch,
        compiler_params=pltpu.CompilerParams(
            collective_id=0, has_side_effects=True, vmem_limit_bytes=60 * 1024 * 1024
        ),
    )(hidden, down)


def normalize(parts):
    highest = reduce(
        jnp.maximum,
        [
            jnp.max(jnp.where(visible, scores, -jnp.inf), axis=-1, keepdims=True)
            for scores, visible in parts
        ],
    )
    portions = [jnp.where(visible, jnp.exp(scores - highest), 0.0) for scores, visible in parts]
    denominator = reduce(
        jnp.add, [jnp.sum(portion, axis=-1, keepdims=True) for portion in portions]
    )
    return [(portion / denominator).astype(jnp.bfloat16) for portion in portions]


def attend(question_vectors, new_keys, new_values, key_pages, value_pages, table, spans):
    rows_all, head_count, head_width = question_vectors.shape
    kv_heads = new_keys.shape[1]
    group_size = head_count // kv_heads
    single_count = spans.shape[0] - 1
    page_count = table.shape[1]
    page_width = key_pages.shape[2]
    context = page_count * page_width
    inverse_root = 1.0 / math.sqrt(head_width)
    pick = (table[..., None] == jnp.arange(key_pages.shape[0], dtype=table.dtype)).astype(key_pages.dtype)
    page_keys = jnp.einsum(
        "rmp,pkab->rmkab", pick, key_pages, preferred_element_type=jnp.float32
    ).astype(key_pages.dtype)
    page_values = jnp.einsum(
        "rmp,pkab->rmkab", pick, value_pages, preferred_element_type=jnp.float32
    ).astype(value_pages.dtype)
    grouped = question_vectors.reshape(rows_all, kv_heads, group_size, head_width)
    positions = jnp.arange(context, dtype=jnp.int32)
    single_q = grouped[:single_count]
    cache_dec = (
        jnp.einsum(
            "rkgh,rmkph->rkgmp",
            single_q,
            page_keys[:single_count],
            preferred_element_type=jnp.float32,
        ).reshape(single_count, kv_heads, group_size, context)
        * inverse_root
    )
    seen_dec = (positions[None, :] < spans[:single_count, None])[:, None, None, :]
    own_dec = (
        jnp.einsum(
            "rkgh,rkh->rkg", single_q, new_keys[:single_count], preferred_element_type=jnp.float32
        )[..., None]
        * inverse_root
    )
    weight_cache, weight_own = normalize(
        [(cache_dec, seen_dec), (own_dec, jnp.full(own_dec.shape, True))]
    )
    out_dec = jnp.einsum(
        "rkgmp,rmkph->rkgh",
        weight_cache.reshape(single_count, kv_heads, group_size, page_count, page_width),
        page_values[:single_count],
        preferred_element_type=jnp.float32,
    )
    out_dec = (
        out_dec
        + weight_own.astype(jnp.float32)
        * new_values[:single_count].astype(jnp.float32)[:, :, None, :]
    )
    prompt_q = grouped[single_count:]
    prompt_rows = rows_all - single_count
    cache_pro = (
        jnp.einsum(
            "rkgh,mkph->rkgmp",
            prompt_q,
            page_keys[single_count],
            preferred_element_type=jnp.float32,
        ).reshape(prompt_rows, kv_heads, group_size, context)
        * inverse_root
    )
    seen_pro = (positions < spans[single_count])[None, None, None, :]
    new_pro = (
        jnp.einsum(
            "rkgh,mkh->rkgm", prompt_q, new_keys[single_count:], preferred_element_type=jnp.float32
        )
        * inverse_root
    )
    prompt_index = jnp.arange(prompt_rows, dtype=jnp.int32)
    causal = (prompt_index[:, None] >= prompt_index[None, :])[:, None, None, :]
    weight_cpro, weight_npro = normalize([(cache_pro, seen_pro), (new_pro, causal)])
    out_pro = jnp.einsum(
        "rkgmp,mkph->rkgh",
        weight_cpro.reshape(prompt_rows, kv_heads, group_size, page_count, page_width),
        page_values[single_count],
        preferred_element_type=jnp.float32,
    )
    out_pro = out_pro + jnp.einsum(
        "rkgm,mkh->rkgh", weight_npro, new_values[single_count:], preferred_element_type=jnp.float32
    )
    joined = jnp.concatenate([out_dec, out_pro], axis=0).astype(jnp.bfloat16)
    return joined.reshape(rows_all, head_count * head_width)


def slot_table(member, ranking, keeping, slot_count):
    slot_hit = (
        ranking[:, :, None, None] == jnp.arange(slot_count, dtype=jnp.int32)[None, None, None, :]
    )
    return ((member[..., None] > 0) & keeping[:, :, None, None] & slot_hit).astype(jnp.bfloat16)


def expert_pass(send, gating_matrices, expand_matrices, contract_matrices):
    specialist_index, slot_count, model_width = send.shape
    local_count = gating_matrices.shape[0]
    assert local_count == 1
    arrived = expert_exchange(send, 3).reshape(specialist_index * slot_count, model_width)
    inner = gating_matrices.shape[1]
    padded = -(-inner // 128) * 128
    widen = ((0, padded - inner), (0, 0))
    hidden = expert_front(
        arrived,
        jnp.pad(gating_matrices[0], widen).T,
        jnp.pad(expand_matrices[0], widen).T,
        lax.axis_size("dp"),
        lax.axis_size("tensor"),
    )
    down = jnp.pad(contract_matrices[0], widen)
    n_dp, n_t = lax.axis_size("dp"), lax.axis_size("tensor")
    summed = moe_sum(hidden, down, n_dp, n_t)
    return expert_exchange(summed.reshape(specialist_index, slot_count, model_width), 4)


def local(
    skip_stream_entry,
    question_vectors,
    fresh_lookup_vectors,
    fresh_content_vectors,
    stored_lookup_sheets,
    stored_content_sheets,
    sequence_sheet_map,
    stored_position_counts,
    attention_merge_matrix,
    premix_scale_factor,
    chosen_specialists,
    selection_shares,
    allowed_placements,
    favored_specialist,
    gating_matrices,
    expand_matrices,
    contract_matrices,
):
    token_count = chosen_specialists.shape[0]
    specialist_index = allowed_placements.shape[0]
    picked = (
        chosen_specialists[:, :, None]
        == jnp.arange(specialist_index, dtype=jnp.int32)[None, None, :]
    ).astype(jnp.int32)
    flat_routes = picked.reshape(token_count * 2, specialist_index)
    busiest_specialist = favored_specialist[0]
    before = (jnp.cumsum(flat_routes, axis=0) - flat_routes).reshape(
        token_count, 2, specialist_index
    )
    ranking = jnp.sum(before * picked, axis=2)
    placement_ceiling = jnp.where(
        jnp.arange(specialist_index, dtype=jnp.int32) == busiest_specialist,
        PLACEMENT_MOST,
        allowed_placements,
    )
    keeping = ranking < jnp.sum(picked * placement_ceiling[None, None, :], axis=2)
    row_total = question_vectors.shape[0]
    heads_out = attend(
        question_vectors.reshape(row_total, -1, HD),
        fresh_lookup_vectors.reshape(row_total, -1, HD),
        fresh_content_vectors.reshape(row_total, -1, HD),
        stored_lookup_sheets,
        stored_content_sheets,
        sequence_sheet_map,
        stored_position_counts,
    )
    own_attn = head_sum(
        jnp.dot(heads_out, attention_merge_matrix, preferred_element_type=jnp.float32).astype(
            jnp.bfloat16
        ),
        lax.axis_size("tensor"),
    ).astype(jnp.float32)
    stream = (skip_stream_entry.astype(jnp.float32) + own_attn).astype(jnp.bfloat16)
    wide = stream.astype(jnp.float32)
    squares = jnp.mean(wide * wide, axis=1, keepdims=True)
    normed = (wide * lax.rsqrt(squares + 1e-05) * premix_scale_factor.astype(jnp.float32)).astype(
        jnp.bfloat16
    )
    main_slots = PLACEMENT_MOST
    table_main = slot_table(picked, ranking, keeping, main_slots)
    send = jnp.einsum(
        "nkes,nd->esd", table_main, normed, preferred_element_type=jnp.float32
    ).astype(jnp.bfloat16)
    expert_out = expert_pass(send, gating_matrices, expand_matrices, contract_matrices)
    chosen = jnp.einsum("nkes,esd->nkd", table_main, expert_out, preferred_element_type=jnp.float32)
    mixed = jnp.sum(selection_shares[:, :, None] * chosen, axis=1)
    return (wide + mixed).astype(jnp.bfloat16)


def solution(mesh):
    placed = (
        P(("dp", "expert", "tensor"), None),
        P(("dp", "expert"), "tensor"),
        P(("dp", "expert"), "tensor"),
        P(("dp", "expert"), "tensor"),
        P(("dp", "expert"), "tensor", None, None),
        P(("dp", "expert"), "tensor", None, None),
        P(("dp", "expert"), None),
        P(("dp", "expert")),
        P("tensor", None),
        P(),
        P(("dp", "expert", "tensor"), None),
        P(("dp", "expert", "tensor"), None),
        P(),
        P(),
        P("expert", ("dp", "tensor"), None),
        P("expert", ("dp", "tensor"), None),
        P("expert", ("dp", "tensor"), None),
    )
    return jax.shard_map(
        local,
        mesh=mesh,
        in_specs=placed,
        out_specs=P(("dp", "expert", "tensor"), None),
        check_vma=False,
    )
```

```python
from functools import reduce
import functools
import math

import jax
import jax.numpy as jnp
from jax import lax
from jax.experimental import pallas as pl
from jax.experimental.pallas import tpu as pltpu
from jax.sharding import PartitionSpec as P

HD = 128
PLACEMENT_MOST = 6


MESH_ID = pl.DeviceIdType.MESH


def plan_order(events, rate=50000.0, latency=1.5, per_step=0.3):
    ready = [0.0] * len(events)
    at = [0] * len(events)
    free = {}
    clock = 0.0
    order = []
    while True:
        live = [i for i in range(len(events)) if at[i] < len(events[i])]
        if not live:
            return order, clock
        i = min(live, key=lambda k: (ready[k], k))
        clock = max(clock, ready[i]) + per_step
        send = events[i][at[i]]
        if send is None:
            ready[i] = clock
        else:
            link, size = send
            start = max(clock, free.get(link, 0.0))
            free[link] = start + size / rate
            ready[i] = free[link] + latency
        order.append(i)
        at[i] += 1


def ring_events(n1, n2, link1, link2, size1, size2):
    return [(link1, size1)] * (n1 - 1) + [None] + [(link2, size2)] * (n2 - 1) + [None]


def split_plan(n_dp, n_t, rows, model_width, reduce):
    best = None
    for first_dp in range(128, model_width // 2, 128):
        widths = [first_dp, first_dp, model_width // 2 - first_dp, model_width // 2 - first_dp]
        events = []
        for block, width in enumerate(widths):
            unit = rows * width * 2
            sign = "+" if block % 2 == 0 else "-"
            if block < 2:
                big1, big2 = (n_t * unit, unit) if reduce else (unit, n_dp * unit)
                events.append(ring_events(n_dp, n_t, "z" + sign, "y" + sign, big1, big2))
            else:
                big1, big2 = (n_dp * unit, unit) if reduce else (unit, n_t * unit)
                events.append(ring_events(n_t, n_dp, "y" + sign, "z" + sign, big1, big2))
        order, finish = plan_order(events)
        if best is None or finish < best[0]:
            best = (finish, widths, order)
    return best[1], best[2]


def run_in_order(streams, order):
    for i in order:
        next(streams[i])
    for st in streams:
        for _ in st:
            pass


def ring_phase(n, me, step_to, own, chunk_lead, recv, send0, send_sems, recv_sems, first_sem, finish):
    copies = []
    for s in range(n - 1):
        c = lax.rem(me + n * 2 - step_to[1] * (s + 1), n)
        if s == 0:
            for i in range(chunk_lead):
                send0[i] = own(c, i).astype(send0.dtype)
            src = send0
        else:
            copies[-1].wait_recv()
            for i in range(chunk_lead):
                recv[s - 1, i] = (own(c, i) + recv[s - 1, i].astype(jnp.float32)).astype(recv.dtype)
            src = recv.at[s - 1]
        copy = pltpu.make_async_remote_copy(
            src_ref=src,
            dst_ref=recv.at[s],
            send_sem=send_sems.at[first_sem + s],
            recv_sem=recv_sems.at[first_sem + s],
            device_id=step_to[0],
            device_id_type=MESH_ID,
        )
        copy.start()
        copies.append(copy)
        yield copies
    copies[-1].wait_recv()
    for i in range(chunk_lead):
        finish(i, own(me, i) + recv[n - 2, i].astype(jnp.float32))
    yield copies


def block_product(h_ref, w_ref, chunk, cols, rows):
    start = pl.multiple_of(chunk * rows, 16)
    product = jnp.dot(h_ref[pl.ds(start, rows), :], w_ref[:, cols], preferred_element_type=jnp.float32)
    return product.astype(jnp.bfloat16).astype(jnp.float32)


def moe_sum_kernel(n_dp, n_t, widths, order, h_ref, w_ref, o_ref, *scratch):
    recv_sems, send_sems = scratch[-2], scratch[-1]
    bufs = scratch[:-2]
    me_dp = lax.axis_index("dp")
    me_t = lax.axis_index("tensor")
    me_e = lax.axis_index("expert")

    def dp_dev(d):
        return (lax.rem(me_dp + n_dp + d, n_dp), me_e, me_t)

    def t_dev(d):
        return (me_dp, me_e, lax.rem(me_t + n_t + d, n_t))

    barrier = pltpu.get_barrier_semaphore()
    for dev in (dp_dev(1), dp_dev(-1), t_dev(1), t_dev(-1)):
        pl.semaphore_signal(barrier, 1, device_id=dev, device_id_type=MESH_ID)
    pl.semaphore_wait(barrier, 4)

    streams = []
    sem_at = 0
    for block in range(4):
        cols = pl.ds(sum(widths[:block]), widths[block])
        direction = 1 if block % 2 == 0 else -1
        r1, s1, acc, r2, s2 = bufs[block * 5: block * 5 + 5]
        if block < 2:
            first = (n_dp, me_dp, (dp_dev(direction), direction), n_t)
            own1 = lambda c, i, cols=cols: block_product(h_ref, w_ref, c * n_t + i, cols, o_ref.shape[0])
            second = (n_t, me_t, (t_dev(direction), direction))
        else:
            first = (n_t, me_t, (t_dev(direction), direction), n_dp)
            own1 = lambda c, i, cols=cols: block_product(h_ref, w_ref, i * n_t + c, cols, o_ref.shape[0])
            second = (n_dp, me_dp, (dp_dev(direction), direction))

        def fin1(i, v, acc=acc):
            acc[i] = v

        def fin2(i, v, cols=cols):
            o_ref[:, cols] = v.astype(o_ref.dtype)

        own2 = lambda c, i, acc=acc: acc[c]

        def stream(first=first, second=second, own1=own1, own2=own2, r1=r1, s1=s1, r2=r2, s2=s2,
                   fin1=fin1, fin2=fin2, base=sem_at):
            n1, me1, to1, lead = first
            copies = []
            for copies in ring_phase(n1, me1, to1, own1, lead, r1, s1, send_sems, recv_sems, base, fin1):
                yield
            done1 = copies
            n2, me2, to2 = second
            for copies in ring_phase(n2, me2, to2, own2, 1, r2, s2, send_sems, recv_sems, base + n1 - 1,
                                     lambda i, v: fin2(i, v)):
                yield
            for copy in done1 + copies:
                copy.wait_send()

        streams.append(stream())
        sem_at += n_dp + n_t - 2

    run_in_order(streams, order)


def gather_phase(n, me, step_to, chunk, send_sems, recv_sems, first_sem):
    copies = []
    for s in range(n - 1):
        c = lax.rem(me + n * 2 - step_to[1] * s, n)
        if s > 0:
            copies[-1].wait_recv()
        copy = pltpu.make_async_remote_copy(
            src_ref=chunk(c),
            dst_ref=chunk(c),
            send_sem=send_sems.at[first_sem + s],
            recv_sem=recv_sems.at[first_sem + s],
            device_id=step_to[0],
            device_id_type=MESH_ID,
        )
        copy.start()
        copies.append(copy)
        yield copies
    copies[-1].wait_recv()
    yield copies


def row_gather_kernel(n_dp, n_t, widths, order, x_ref, o_ref, *scratch):
    recv_sems, send_sems = scratch[-2], scratch[-1]
    bufs = scratch[:-2]
    me_dp = lax.axis_index("dp")
    me_t = lax.axis_index("tensor")
    me_e = lax.axis_index("expert")
    rows = x_ref.shape[0]

    def dp_dev(d):
        return (lax.rem(me_dp + n_dp + d, n_dp), me_e, me_t)

    def t_dev(d):
        return (me_dp, me_e, lax.rem(me_t + n_t + d, n_t))

    for block in range(4):
        cols = pl.ds(sum(widths[:block]), widths[block])
        if block < 2:
            bufs[block][me_t, me_dp] = x_ref[:, cols]
        else:
            bufs[block][me_dp, me_t] = x_ref[:, cols]

    barrier = pltpu.get_barrier_semaphore()
    for dev in (dp_dev(1), dp_dev(-1), t_dev(1), t_dev(-1)):
        pl.semaphore_signal(barrier, 1, device_id=dev, device_id_type=MESH_ID)
    pl.semaphore_wait(barrier, 4)

    streams = []
    sem_at = 0
    for block in range(4):
        direction = 1 if block % 2 == 0 else -1
        g = bufs[block]
        if block < 2:
            first = (n_dp, me_dp, (dp_dev(direction), direction), lambda c, g=g: g.at[me_t, c])
            second = (n_t, me_t, (t_dev(direction), direction), lambda c, g=g: g.at[c])
        else:
            first = (n_t, me_t, (t_dev(direction), direction), lambda c, g=g: g.at[me_dp, c])
            second = (n_dp, me_dp, (dp_dev(direction), direction), lambda c, g=g: g.at[c])

        def stream(first=first, second=second, base=sem_at):
            n1, me1, to1, chunk1 = first
            copies = []
            for copies in gather_phase(n1, me1, to1, chunk1, send_sems, recv_sems, base):
                yield
            done1 = copies
            n2, me2, to2, chunk2 = second
            for copies in gather_phase(n2, me2, to2, chunk2, send_sems, recv_sems, base + n1 - 1):
                yield
            for copy in done1 + copies:
                copy.wait_send()

        streams.append(stream())
        sem_at += n_dp + n_t - 2

    run_in_order(streams, order)

    for block in range(4):
        cols = pl.ds(sum(widths[:block]), widths[block])
        for d in range(n_dp):
            for t in range(n_t):
                piece = bufs[block][t, d] if block < 2 else bufs[block][d, t]
                o_ref[pl.ds((d * n_t + t) * rows, rows), cols] = piece


def row_gather(x, n_dp, n_t):
    rows, model_width = x.shape
    widths, order = split_plan(n_dp, n_t, rows, model_width, False)
    scratch = [
        pltpu.VMEM((n_t, n_dp, rows, widths[0]), jnp.bfloat16),
        pltpu.VMEM((n_t, n_dp, rows, widths[1]), jnp.bfloat16),
        pltpu.VMEM((n_dp, n_t, rows, widths[2]), jnp.bfloat16),
        pltpu.VMEM((n_dp, n_t, rows, widths[3]), jnp.bfloat16),
    ]
    copies = 4 * (n_dp + n_t - 2)
    scratch += [pltpu.SemaphoreType.DMA((copies,)), pltpu.SemaphoreType.DMA((copies,))]
    return pl.pallas_call(
        functools.partial(row_gather_kernel, n_dp, n_t, tuple(widths), tuple(order)),
        out_shape=jax.ShapeDtypeStruct((n_dp * n_t * rows, model_width), jnp.bfloat16),
        in_specs=[pl.BlockSpec(memory_space=pltpu.VMEM)],
        out_specs=pl.BlockSpec(memory_space=pltpu.VMEM),
        scratch_shapes=scratch,
        compiler_params=pltpu.CompilerParams(
            collective_id=1, has_side_effects=True, vmem_limit_bytes=60 * 1024 * 1024
        ),
    )(x)


def head_sum_kernel(n_t, x_ref, o_ref, recv0, send0, recv1, send1, recv_sems, send_sems):
    me_dp = lax.axis_index("dp")
    me_e = lax.axis_index("expert")
    me_t = lax.axis_index("tensor")
    rows = o_ref.shape[0]
    width = o_ref.shape[1] // 2

    def t_dev(d):
        return (me_dp, me_e, lax.rem(me_t + n_t + d, n_t))

    barrier = pltpu.get_barrier_semaphore()
    for dev in (t_dev(1), t_dev(-1)):
        pl.semaphore_signal(barrier, 1, device_id=dev, device_id_type=MESH_ID)
    pl.semaphore_wait(barrier, 2)
    streams = []
    for block, (recv, send0_buf) in enumerate(((recv0, send0), (recv1, send1))):
        cols = pl.ds(block * width, width)
        direction = 1 if block == 0 else -1
        own = lambda c, i, cols=cols: x_ref[pl.ds(pl.multiple_of(c * rows, 8), rows), cols].astype(jnp.float32)

        def finish(i, v, cols=cols):
            o_ref[:, cols] = v.astype(o_ref.dtype)

        def stream(own=own, recv=recv, send0_buf=send0_buf, finish=finish, direction=direction, base=block):
            copies = []
            for copies in ring_phase(n_t, me_t, (t_dev(direction), direction), own, 1, recv, send0_buf,
                                     send_sems, recv_sems, base * (n_t - 1), finish):
                yield
            for copy in copies:
                copy.wait_send()

        streams.append(stream())
    run_in_order(streams, [0, 1] * n_t)


def head_sum(x, n_t):
    rows, model_width = x.shape[0] // n_t, x.shape[1]
    width = model_width // 2
    scratch = []
    for _ in range(2):
        scratch += [
            pltpu.VMEM((n_t - 1, 1, rows, width), jnp.bfloat16),
            pltpu.VMEM((1, rows, width), jnp.bfloat16),
        ]
    copies = 2 * (n_t - 1)
    scratch += [pltpu.SemaphoreType.DMA((copies,)), pltpu.SemaphoreType.DMA((copies,))]
    return pl.pallas_call(
        functools.partial(head_sum_kernel, n_t),
        out_shape=jax.ShapeDtypeStruct((rows, model_width), jnp.bfloat16),
        in_specs=[pl.BlockSpec(memory_space=pltpu.VMEM)],
        out_specs=pl.BlockSpec(memory_space=pltpu.VMEM),
        scratch_shapes=scratch,
        compiler_params=pltpu.CompilerParams(collective_id=2, has_side_effects=True),
    )(x)


def expert_exchange_kernel(n_e, x_ref, o_ref, recv, recv_sems, send_sems):
    me_dp = lax.axis_index("dp")
    me_e = lax.axis_index("expert")
    me_t = lax.axis_index("tensor")
    barrier = pltpu.get_barrier_semaphore()
    for k in range(1, n_e):
        pl.semaphore_signal(barrier, 1, device_id=(me_dp, lax.rem(me_e + k, n_e), me_t),
                            device_id_type=MESH_ID)
    pl.semaphore_wait(barrier, n_e - 1)
    copies = []
    for k in range(1, n_e):
        target = lax.rem(me_e + k, n_e)
        copy = pltpu.make_async_remote_copy(
            src_ref=x_ref.at[target],
            dst_ref=recv.at[me_e],
            send_sem=send_sems.at[k - 1],
            recv_sem=recv_sems.at[k - 1],
            device_id=(me_dp, target, me_t),
            device_id_type=MESH_ID,
        )
        copy.start()
        copies.append(copy)
    o_ref[me_e] = x_ref[me_e]
    for k in range(1, n_e):
        copies[k - 1].wait_recv()
        source = lax.rem(me_e + n_e - k, n_e)
        o_ref[source] = recv[source]
    for copy in copies:
        copy.wait_send()


def expert_exchange(x, collective):
    n_e = x.shape[0]
    return pl.pallas_call(
        functools.partial(expert_exchange_kernel, n_e),
        out_shape=jax.ShapeDtypeStruct(x.shape, x.dtype),
        in_specs=[pl.BlockSpec(memory_space=pltpu.VMEM)],
        out_specs=pl.BlockSpec(memory_space=pltpu.VMEM),
        scratch_shapes=[
            pltpu.VMEM(x.shape, x.dtype),
            pltpu.SemaphoreType.DMA((n_e - 1,)),
            pltpu.SemaphoreType.DMA((n_e - 1,)),
        ],
        compiler_params=pltpu.CompilerParams(collective_id=collective, has_side_effects=True),
    )(x)


def gather_feed_phase(n, me, step_to, chunk, send_sems, recv_sems, first_sem, process, own_too):
    copies = []
    for s in range(n - 1):
        c = lax.rem(me + n * 2 - step_to[1] * s, n)
        if s > 0:
            copies[-1].wait_recv()
        copy = pltpu.make_async_remote_copy(
            src_ref=chunk(c),
            dst_ref=chunk(c),
            send_sem=send_sems.at[first_sem + s],
            recv_sem=recv_sems.at[first_sem + s],
            device_id=step_to[0],
            device_id_type=MESH_ID,
        )
        copy.start()
        copies.append(copy)
        if s > 0 or own_too:
            process(c)
        yield copies
    copies[-1].wait_recv()
    process(lax.rem(me + n * 2 - step_to[1] * (n - 1), n))
    yield copies


def expert_front_kernel(n_dp, n_t, widths, order, x_ref, wg_ref, wu_ref, o_ref, *scratch):
    recv_sems, send_sems = scratch[-2], scratch[-1]
    gate_acc, up_acc = scratch[-4], scratch[-3]
    bufs = scratch[:-4]
    me_dp = lax.axis_index("dp")
    me_t = lax.axis_index("tensor")
    me_e = lax.axis_index("expert")
    rows = x_ref.shape[0]

    def dp_dev(d):
        return (lax.rem(me_dp + n_dp + d, n_dp), me_e, me_t)

    def t_dev(d):
        return (me_dp, me_e, lax.rem(me_t + n_t + d, n_t))

    gate_acc[...] = jnp.zeros_like(gate_acc)
    up_acc[...] = jnp.zeros_like(up_acc)
    for block in range(4):
        cols = pl.ds(sum(widths[:block]), widths[block])
        if block < 2:
            bufs[block][me_t, me_dp] = x_ref[:, cols]
        else:
            bufs[block][me_dp, me_t] = x_ref[:, cols]

    barrier = pltpu.get_barrier_semaphore()
    for dev in (dp_dev(1), dp_dev(-1), t_dev(1), t_dev(-1)):
        pl.semaphore_signal(barrier, 1, device_id=dev, device_id_type=MESH_ID)
    pl.semaphore_wait(barrier, 4)

    def feed(piece, row_chunk, cols):
        start = pl.multiple_of(row_chunk * rows, 16)
        v = piece[...]
        dims = (((1,), (1,)), ((), ()))
        gate_acc[pl.ds(start, rows), :] += lax.dot_general(
            v, wg_ref[:, cols], dims, preferred_element_type=jnp.float32)
        up_acc[pl.ds(start, rows), :] += lax.dot_general(
            v, wu_ref[:, cols], dims, preferred_element_type=jnp.float32)

    streams = []
    sem_at = 0
    for block in range(4):
        direction = 1 if block % 2 == 0 else -1
        g = bufs[block]
        cols = pl.ds(sum(widths[:block]), widths[block])
        if block < 2:
            def p1(c, g=g, cols=cols):
                feed(g.at[me_t, c], c * n_t + me_t, cols)

            def p2(c, g=g, cols=cols):
                def body(d, carry):
                    feed(g.at[c, d], d * n_t + c, cols)
                    return carry
                lax.fori_loop(0, n_dp, body, 0)
            first = (n_dp, me_dp, (dp_dev(direction), direction), lambda c, g=g: g.at[me_t, c], p1)
            second = (n_t, me_t, (t_dev(direction), direction), lambda c, g=g: g.at[c], p2)
        else:
            def p1(c, g=g, cols=cols):
                feed(g.at[me_dp, c], me_dp * n_t + c, cols)

            def p2(c, g=g, cols=cols):
                def body(t, carry):
                    feed(g.at[c, t], c * n_t + t, cols)
                    return carry
                lax.fori_loop(0, n_t, body, 0)
            first = (n_t, me_t, (t_dev(direction), direction), lambda c, g=g: g.at[me_dp, c], p1)
            second = (n_dp, me_dp, (dp_dev(direction), direction), lambda c, g=g: g.at[c], p2)

        def stream(first=first, second=second, base=sem_at):
            n1, me1, to1, chunk1, proc1 = first
            copies = []
            for copies in gather_feed_phase(n1, me1, to1, chunk1, send_sems, recv_sems, base, proc1, True):
                yield
            done1 = copies
            n2, me2, to2, chunk2, proc2 = second
            for copies in gather_feed_phase(n2, me2, to2, chunk2, send_sems, recv_sems, base + n1 - 1,
                                            proc2, False):
                yield
            for copy in done1 + copies:
                copy.wait_send()

        streams.append(stream())
        sem_at += n_dp + n_t - 2

    run_in_order(streams, order)

    tile = 128

    def finish(i, carry):
        at = pl.ds(pl.multiple_of(i * tile, tile), tile)
        gate = gate_acc[at, :]
        o_ref[at, :] = (gate / (1.0 + jnp.exp(-gate)) * up_acc[at, :]).astype(o_ref.dtype)
        return carry

    lax.fori_loop(0, o_ref.shape[0] // tile, finish, 0)


def expert_front(x, gate_w, up_w, n_dp, n_t):
    rows, model_width = x.shape
    inner = gate_w.shape[0]
    widths, order = split_plan(n_dp, n_t, rows, model_width, False)
    scratch = [
        pltpu.VMEM((n_t, n_dp, rows, widths[0]), jnp.bfloat16),
        pltpu.VMEM((n_t, n_dp, rows, widths[1]), jnp.bfloat16),
        pltpu.VMEM((n_dp, n_t, rows, widths[2]), jnp.bfloat16),
        pltpu.VMEM((n_dp, n_t, rows, widths[3]), jnp.bfloat16),
        pltpu.VMEM((n_dp * n_t * rows, inner), jnp.float32),
        pltpu.VMEM((n_dp * n_t * rows, inner), jnp.float32),
    ]
    copies = 4 * (n_dp + n_t - 2)
    scratch += [pltpu.SemaphoreType.DMA((copies,)), pltpu.SemaphoreType.DMA((copies,))]
    return pl.pallas_call(
        functools.partial(expert_front_kernel, n_dp, n_t, tuple(widths), tuple(order)),
        out_shape=jax.ShapeDtypeStruct((n_dp * n_t * rows, inner), jnp.bfloat16),
        in_specs=[pl.BlockSpec(memory_space=pltpu.VMEM)] * 3,
        out_specs=pl.BlockSpec(memory_space=pltpu.VMEM),
        scratch_shapes=scratch,
        compiler_params=pltpu.CompilerParams(
            collective_id=1, has_side_effects=True, vmem_limit_bytes=60 * 1024 * 1024
        ),
    )(x, gate_w, up_w)


def moe_sum(hidden, down, n_dp, n_t):
    rows, model_width = hidden.shape[0] // (n_dp * n_t), down.shape[1]
    widths, order = split_plan(n_dp, n_t, rows, model_width, True)
    scratch = []
    for block in range(4):
        width = widths[block]
        if block < 2:
            n1, lead, n2 = n_dp, n_t, n_t
        else:
            n1, lead, n2 = n_t, n_dp, n_dp
        scratch += [
            pltpu.VMEM((n1 - 1, lead, rows, width), jnp.bfloat16),
            pltpu.VMEM((lead, rows, width), jnp.bfloat16),
            pltpu.VMEM((lead, rows, width), jnp.float32),
            pltpu.VMEM((n2 - 1, 1, rows, width), jnp.bfloat16),
            pltpu.VMEM((1, rows, width), jnp.bfloat16),
        ]
    copies = 4 * (n_dp + n_t - 2)
    scratch += [pltpu.SemaphoreType.DMA((copies,)), pltpu.SemaphoreType.DMA((copies,))]
    return pl.pallas_call(
        functools.partial(moe_sum_kernel, n_dp, n_t, tuple(widths), tuple(order)),
        out_shape=jax.ShapeDtypeStruct((rows, model_width), jnp.bfloat16),
        in_specs=[pl.BlockSpec(memory_space=pltpu.VMEM)] * 2,
        out_specs=pl.BlockSpec(memory_space=pltpu.VMEM),
        scratch_shapes=scratch,
        compiler_params=pltpu.CompilerParams(
            collective_id=0, has_side_effects=True, vmem_limit_bytes=60 * 1024 * 1024
        ),
    )(hidden, down)


def normalize(parts):
    highest = reduce(
        jnp.maximum,
        [
            jnp.max(jnp.where(visible, scores, -jnp.inf), axis=-1, keepdims=True)
            for scores, visible in parts
        ],
    )
    portions = [jnp.where(visible, jnp.exp(scores - highest), 0.0) for scores, visible in parts]
    denominator = reduce(
        jnp.add, [jnp.sum(portion, axis=-1, keepdims=True) for portion in portions]
    )
    return [(portion / denominator).astype(jnp.bfloat16) for portion in portions]


def attend(question_vectors, new_keys, new_values, key_pages, value_pages, table, spans):
    rows_all, head_count, head_width = question_vectors.shape
    kv_heads = new_keys.shape[1]
    group_size = head_count // kv_heads
    single_count = spans.shape[0] - 1
    page_count = table.shape[1]
    page_width = key_pages.shape[2]
    context = page_count * page_width
    inverse_root = 1.0 / math.sqrt(head_width)
    pick = (table[..., None] == jnp.arange(key_pages.shape[0], dtype=table.dtype)).astype(key_pages.dtype)
    page_keys = jnp.einsum(
        "rmp,pkab->rmkab", pick, key_pages, preferred_element_type=jnp.float32
    ).astype(key_pages.dtype)
    page_values = jnp.einsum(
        "rmp,pkab->rmkab", pick, value_pages, preferred_element_type=jnp.float32
    ).astype(value_pages.dtype)
    grouped = question_vectors.reshape(rows_all, kv_heads, group_size, head_width)
    positions = jnp.arange(context, dtype=jnp.int32)
    single_q = grouped[:single_count]
    cache_dec = (
        jnp.einsum(
            "rkgh,rmkph->rkgmp",
            single_q,
            page_keys[:single_count],
            preferred_element_type=jnp.float32,
        ).reshape(single_count, kv_heads, group_size, context)
        * inverse_root
    )
    seen_dec = (positions[None, :] < spans[:single_count, None])[:, None, None, :]
    own_dec = (
        jnp.einsum(
            "rkgh,rkh->rkg", single_q, new_keys[:single_count], preferred_element_type=jnp.float32
        )[..., None]
        * inverse_root
    )
    weight_cache, weight_own = normalize(
        [(cache_dec, seen_dec), (own_dec, jnp.full(own_dec.shape, True))]
    )
    out_dec = jnp.einsum(
        "rkgmp,rmkph->rkgh",
        weight_cache.reshape(single_count, kv_heads, group_size, page_count, page_width),
        page_values[:single_count],
        preferred_element_type=jnp.float32,
    )
    out_dec = (
        out_dec
        + weight_own.astype(jnp.float32)
        * new_values[:single_count].astype(jnp.float32)[:, :, None, :]
    )
    prompt_q = grouped[single_count:]
    prompt_rows = rows_all - single_count
    cache_pro = (
        jnp.einsum(
            "rkgh,mkph->rkgmp",
            prompt_q,
            page_keys[single_count],
            preferred_element_type=jnp.float32,
        ).reshape(prompt_rows, kv_heads, group_size, context)
        * inverse_root
    )
    seen_pro = (positions < spans[single_count])[None, None, None, :]
    new_pro = (
        jnp.einsum(
            "rkgh,mkh->rkgm", prompt_q, new_keys[single_count:], preferred_element_type=jnp.float32
        )
        * inverse_root
    )
    prompt_index = jnp.arange(prompt_rows, dtype=jnp.int32)
    causal = (prompt_index[:, None] >= prompt_index[None, :])[:, None, None, :]
    weight_cpro, weight_npro = normalize([(cache_pro, seen_pro), (new_pro, causal)])
    out_pro = jnp.einsum(
        "rkgmp,mkph->rkgh",
        weight_cpro.reshape(prompt_rows, kv_heads, group_size, page_count, page_width),
        page_values[single_count],
        preferred_element_type=jnp.float32,
    )
    out_pro = out_pro + jnp.einsum(
        "rkgm,mkh->rkgh", weight_npro, new_values[single_count:], preferred_element_type=jnp.float32
    )
    joined = jnp.concatenate([out_dec, out_pro], axis=0).astype(jnp.bfloat16)
    return joined.reshape(rows_all, head_count * head_width)


def slot_table(member, ranking, keeping, slot_count):
    slot_hit = (
        ranking[:, :, None, None] == jnp.arange(slot_count, dtype=jnp.int32)[None, None, None, :]
    )
    return ((member[..., None] > 0) & keeping[:, :, None, None] & slot_hit).astype(jnp.bfloat16)


def expert_pass(send, gating_matrices, expand_matrices, contract_matrices):
    specialist_index, slot_count, model_width = send.shape
    local_count = gating_matrices.shape[0]
    assert local_count == 1
    arrived = expert_exchange(send, 3).reshape(specialist_index * slot_count, model_width)
    hidden = expert_front(
        arrived,
        gating_matrices[0],
        expand_matrices[0],
        lax.axis_size("dp"),
        lax.axis_size("tensor"),
    )
    down = contract_matrices[0]
    n_dp, n_t = lax.axis_size("dp"), lax.axis_size("tensor")
    summed = moe_sum(hidden, down, n_dp, n_t)
    return expert_exchange(summed.reshape(specialist_index, slot_count, model_width), 4)


def local(
    skip_stream_entry,
    question_vectors,
    fresh_lookup_vectors,
    fresh_content_vectors,
    stored_lookup_sheets,
    stored_content_sheets,
    sequence_sheet_map,
    stored_position_counts,
    attention_merge_matrix,
    premix_scale_factor,
    chosen_specialists,
    selection_shares,
    allowed_placements,
    favored_specialist,
    gating_matrices,
    expand_matrices,
    contract_matrices,
):
    token_count = chosen_specialists.shape[0]
    specialist_index = allowed_placements.shape[0]
    picked = (
        chosen_specialists[:, :, None]
        == jnp.arange(specialist_index, dtype=jnp.int32)[None, None, :]
    ).astype(jnp.int32)
    flat_routes = picked.reshape(token_count * 2, specialist_index)
    busiest_specialist = favored_specialist[0]
    before = (jnp.cumsum(flat_routes, axis=0) - flat_routes).reshape(
        token_count, 2, specialist_index
    )
    ranking = jnp.sum(before * picked, axis=2)
    placement_ceiling = jnp.where(
        jnp.arange(specialist_index, dtype=jnp.int32) == busiest_specialist,
        PLACEMENT_MOST,
        allowed_placements,
    )
    keeping = ranking < jnp.sum(picked * placement_ceiling[None, None, :], axis=2)
    row_total = question_vectors.shape[0]
    heads_out = attend(
        question_vectors.reshape(row_total, -1, HD),
        fresh_lookup_vectors.reshape(row_total, -1, HD),
        fresh_content_vectors.reshape(row_total, -1, HD),
        stored_lookup_sheets,
        stored_content_sheets,
        sequence_sheet_map,
        stored_position_counts,
    )
    own_attn = head_sum(
        jnp.dot(heads_out, attention_merge_matrix, preferred_element_type=jnp.float32).astype(
            jnp.bfloat16
        ),
        lax.axis_size("tensor"),
    ).astype(jnp.float32)
    stream = (skip_stream_entry.astype(jnp.float32) + own_attn).astype(jnp.bfloat16)
    wide = stream.astype(jnp.float32)
    squares = jnp.mean(wide * wide, axis=1, keepdims=True)
    normed = (wide * lax.rsqrt(squares + 1e-05) * premix_scale_factor.astype(jnp.float32)).astype(
        jnp.bfloat16
    )
    main_slots = PLACEMENT_MOST
    table_main = slot_table(picked, ranking, keeping, main_slots)
    send = jnp.einsum(
        "nkes,nd->esd", table_main, normed, preferred_element_type=jnp.float32
    ).astype(jnp.bfloat16)
    expert_out = expert_pass(send, gating_matrices, expand_matrices, contract_matrices)
    chosen = jnp.einsum("nkes,esd->nkd", table_main, expert_out, preferred_element_type=jnp.float32)
    mixed = jnp.sum(selection_shares[:, :, None] * chosen, axis=1)
    return (wide + mixed).astype(jnp.bfloat16)


def solution(mesh):
    placed = (
        P(("dp", "expert", "tensor"), None),
        P(("dp", "expert"), "tensor"),
        P(("dp", "expert"), "tensor"),
        P(("dp", "expert"), "tensor"),
        P(("dp", "expert"), "tensor", None, None),
        P(("dp", "expert"), "tensor", None, None),
        P(("dp", "expert"), None),
        P(("dp", "expert")),
        P("tensor", None),
        P(),
        P(("dp", "expert", "tensor"), None),
        P(("dp", "expert", "tensor"), None),
        P(),
        P(),
        P("expert", ("dp", "tensor"), None),
        P("expert", ("dp", "tensor"), None),
        P("expert", ("dp", "tensor"), None),
    )
    return jax.shard_map(
        local,
        mesh=mesh,
        in_specs=placed,
        out_specs=P(("dp", "expert", "tensor"), None),
        check_vma=False,
    )
```

```python
from functools import reduce
import functools
import math

import jax
import jax.numpy as jnp
from jax import lax
from jax.experimental import pallas as pl
from jax.experimental.pallas import tpu as pltpu
from jax.sharding import PartitionSpec as P

HD = 128
PLACEMENT_MOST = 6


MESH_ID = pl.DeviceIdType.MESH


def plan_order(events, rate=50000.0, latency=1.5, per_step=0.3):
    ready = [0.0] * len(events)
    at = [0] * len(events)
    free = {}
    clock = 0.0
    order = []
    while True:
        live = [i for i in range(len(events)) if at[i] < len(events[i])]
        if not live:
            return order, clock
        i = min(live, key=lambda k: (ready[k], k))
        clock = max(clock, ready[i]) + per_step
        send = events[i][at[i]]
        if send is None:
            ready[i] = clock
        else:
            link, size = send
            start = max(clock, free.get(link, 0.0))
            free[link] = start + size / rate
            ready[i] = free[link] + latency
        order.append(i)
        at[i] += 1


def ring_events(n1, n2, link1, link2, size1, size2):
    return [(link1, size1)] * (n1 - 1) + [None] + [(link2, size2)] * (n2 - 1) + [None]


def split_plan(n_dp, n_t, rows, model_width, reduce, per_step=0.3):
    best = None
    for first_dp in range(128, model_width // 2, 128):
        widths = [first_dp, first_dp, model_width // 2 - first_dp, model_width // 2 - first_dp]
        events = []
        for block, width in enumerate(widths):
            unit = rows * width * 2
            sign = "+" if block % 2 == 0 else "-"
            if block < 2:
                big1, big2 = (n_t * unit, unit) if reduce else (unit, n_dp * unit)
                events.append(ring_events(n_dp, n_t, "z" + sign, "y" + sign, big1, big2))
            else:
                big1, big2 = (n_dp * unit, unit) if reduce else (unit, n_t * unit)
                events.append(ring_events(n_t, n_dp, "y" + sign, "z" + sign, big1, big2))
        order, finish = plan_order(events, per_step=per_step)
        if best is None or finish < best[0]:
            best = (finish, widths, order)
    return best[1], best[2]


def run_in_order(streams, order):
    for i in order:
        next(streams[i])
    for st in streams:
        for _ in st:
            pass


def ring_phase(n, me, step_to, own, chunk_lead, recv, send0, send_sems, recv_sems, first_sem, finish):
    copies = []
    for s in range(n - 1):
        c = lax.rem(me + n * 2 - step_to[1] * (s + 1), n)
        if s == 0:
            for i in range(chunk_lead):
                send0[i] = own(c, i).astype(send0.dtype)
            src = send0
        else:
            copies[-1].wait_recv()
            for i in range(chunk_lead):
                recv[s - 1, i] = (own(c, i) + recv[s - 1, i].astype(jnp.float32)).astype(recv.dtype)
            src = recv.at[s - 1]
        copy = pltpu.make_async_remote_copy(
            src_ref=src,
            dst_ref=recv.at[s],
            send_sem=send_sems.at[first_sem + s],
            recv_sem=recv_sems.at[first_sem + s],
            device_id=step_to[0],
            device_id_type=MESH_ID,
        )
        copy.start()
        copies.append(copy)
        yield copies
    copies[-1].wait_recv()
    for i in range(chunk_lead):
        finish(i, own(me, i) + recv[n - 2, i].astype(jnp.float32))
    yield copies


def block_product(h_ref, w_ref, chunk, cols, rows):
    start = pl.multiple_of(chunk * rows, 16)
    product = jnp.dot(h_ref[pl.ds(start, rows), :], w_ref[:, cols], preferred_element_type=jnp.float32)
    return product.astype(jnp.bfloat16).astype(jnp.float32)


def moe_sum_kernel(n_dp, n_t, widths, order, h_ref, w_ref, o_ref, *scratch):
    recv_sems, send_sems = scratch[-2], scratch[-1]
    bufs = scratch[:-2]
    me_dp = lax.axis_index("dp")
    me_t = lax.axis_index("tensor")
    me_e = lax.axis_index("expert")

    def dp_dev(d):
        return (lax.rem(me_dp + n_dp + d, n_dp), me_e, me_t)

    def t_dev(d):
        return (me_dp, me_e, lax.rem(me_t + n_t + d, n_t))

    barrier = pltpu.get_barrier_semaphore()
    for dev in (dp_dev(1), dp_dev(-1), t_dev(1), t_dev(-1)):
        pl.semaphore_signal(barrier, 1, device_id=dev, device_id_type=MESH_ID)
    pl.semaphore_wait(barrier, 4)

    streams = []
    sem_at = 0
    for block in range(4):
        cols = pl.ds(sum(widths[:block]), widths[block])
        direction = 1 if block % 2 == 0 else -1
        r1, s1, acc, r2, s2 = bufs[block * 5: block * 5 + 5]
        if block < 2:
            first = (n_dp, me_dp, (dp_dev(direction), direction), n_t)
            own1 = lambda c, i, cols=cols: block_product(h_ref, w_ref, c * n_t + i, cols, o_ref.shape[0])
            second = (n_t, me_t, (t_dev(direction), direction))
        else:
            first = (n_t, me_t, (t_dev(direction), direction), n_dp)
            own1 = lambda c, i, cols=cols: block_product(h_ref, w_ref, i * n_t + c, cols, o_ref.shape[0])
            second = (n_dp, me_dp, (dp_dev(direction), direction))

        def fin1(i, v, acc=acc):
            acc[i] = v

        def fin2(i, v, cols=cols):
            o_ref[:, cols] = v.astype(o_ref.dtype)

        own2 = lambda c, i, acc=acc: acc[c]

        def stream(first=first, second=second, own1=own1, own2=own2, r1=r1, s1=s1, r2=r2, s2=s2,
                   fin1=fin1, fin2=fin2, base=sem_at):
            n1, me1, to1, lead = first
            copies = []
            for copies in ring_phase(n1, me1, to1, own1, lead, r1, s1, send_sems, recv_sems, base, fin1):
                yield
            done1 = copies
            n2, me2, to2 = second
            for copies in ring_phase(n2, me2, to2, own2, 1, r2, s2, send_sems, recv_sems, base + n1 - 1,
                                     lambda i, v: fin2(i, v)):
                yield
            for copy in done1 + copies:
                copy.wait_send()

        streams.append(stream())
        sem_at += n_dp + n_t - 2

    run_in_order(streams, order)


def gather_phase(n, me, step_to, chunk, send_sems, recv_sems, first_sem):
    copies = []
    for s in range(n - 1):
        c = lax.rem(me + n * 2 - step_to[1] * s, n)
        if s > 0:
            copies[-1].wait_recv()
        copy = pltpu.make_async_remote_copy(
            src_ref=chunk(c),
            dst_ref=chunk(c),
            send_sem=send_sems.at[first_sem + s],
            recv_sem=recv_sems.at[first_sem + s],
            device_id=step_to[0],
            device_id_type=MESH_ID,
        )
        copy.start()
        copies.append(copy)
        yield copies
    copies[-1].wait_recv()
    yield copies


def row_gather_kernel(n_dp, n_t, widths, order, x_ref, o_ref, *scratch):
    recv_sems, send_sems = scratch[-2], scratch[-1]
    bufs = scratch[:-2]
    me_dp = lax.axis_index("dp")
    me_t = lax.axis_index("tensor")
    me_e = lax.axis_index("expert")
    rows = x_ref.shape[0]

    def dp_dev(d):
        return (lax.rem(me_dp + n_dp + d, n_dp), me_e, me_t)

    def t_dev(d):
        return (me_dp, me_e, lax.rem(me_t + n_t + d, n_t))

    for block in range(4):
        cols = pl.ds(sum(widths[:block]), widths[block])
        if block < 2:
            bufs[block][me_t, me_dp] = x_ref[:, cols]
        else:
            bufs[block][me_dp, me_t] = x_ref[:, cols]

    barrier = pltpu.get_barrier_semaphore()
    for dev in (dp_dev(1), dp_dev(-1), t_dev(1), t_dev(-1)):
        pl.semaphore_signal(barrier, 1, device_id=dev, device_id_type=MESH_ID)
    pl.semaphore_wait(barrier, 4)

    streams = []
    sem_at = 0
    for block in range(4):
        direction = 1 if block % 2 == 0 else -1
        g = bufs[block]
        if block < 2:
            first = (n_dp, me_dp, (dp_dev(direction), direction), lambda c, g=g: g.at[me_t, c])
            second = (n_t, me_t, (t_dev(direction), direction), lambda c, g=g: g.at[c])
        else:
            first = (n_t, me_t, (t_dev(direction), direction), lambda c, g=g: g.at[me_dp, c])
            second = (n_dp, me_dp, (dp_dev(direction), direction), lambda c, g=g: g.at[c])

        def stream(first=first, second=second, base=sem_at):
            n1, me1, to1, chunk1 = first
            copies = []
            for copies in gather_phase(n1, me1, to1, chunk1, send_sems, recv_sems, base):
                yield
            done1 = copies
            n2, me2, to2, chunk2 = second
            for copies in gather_phase(n2, me2, to2, chunk2, send_sems, recv_sems, base + n1 - 1):
                yield
            for copy in done1 + copies:
                copy.wait_send()

        streams.append(stream())
        sem_at += n_dp + n_t - 2

    run_in_order(streams, order)

    for block in range(4):
        cols = pl.ds(sum(widths[:block]), widths[block])
        for d in range(n_dp):
            for t in range(n_t):
                piece = bufs[block][t, d] if block < 2 else bufs[block][d, t]
                o_ref[pl.ds((d * n_t + t) * rows, rows), cols] = piece


def row_gather(x, n_dp, n_t):
    rows, model_width = x.shape
    widths, order = split_plan(n_dp, n_t, rows, model_width, False)
    scratch = [
        pltpu.VMEM((n_t, n_dp, rows, widths[0]), jnp.bfloat16),
        pltpu.VMEM((n_t, n_dp, rows, widths[1]), jnp.bfloat16),
        pltpu.VMEM((n_dp, n_t, rows, widths[2]), jnp.bfloat16),
        pltpu.VMEM((n_dp, n_t, rows, widths[3]), jnp.bfloat16),
    ]
    copies = 4 * (n_dp + n_t - 2)
    scratch += [pltpu.SemaphoreType.DMA((copies,)), pltpu.SemaphoreType.DMA((copies,))]
    return pl.pallas_call(
        functools.partial(row_gather_kernel, n_dp, n_t, tuple(widths), tuple(order)),
        out_shape=jax.ShapeDtypeStruct((n_dp * n_t * rows, model_width), jnp.bfloat16),
        in_specs=[pl.BlockSpec(memory_space=pltpu.VMEM)],
        out_specs=pl.BlockSpec(memory_space=pltpu.VMEM),
        scratch_shapes=scratch,
        compiler_params=pltpu.CompilerParams(
            collective_id=1, has_side_effects=True, vmem_limit_bytes=60 * 1024 * 1024
        ),
    )(x)


def head_sum_kernel(n_t, x_ref, o_ref, recv0, send0, recv1, send1, recv_sems, send_sems):
    me_dp = lax.axis_index("dp")
    me_e = lax.axis_index("expert")
    me_t = lax.axis_index("tensor")
    rows = o_ref.shape[0]
    width = o_ref.shape[1] // 2

    def t_dev(d):
        return (me_dp, me_e, lax.rem(me_t + n_t + d, n_t))

    barrier = pltpu.get_barrier_semaphore()
    for dev in (t_dev(1), t_dev(-1)):
        pl.semaphore_signal(barrier, 1, device_id=dev, device_id_type=MESH_ID)
    pl.semaphore_wait(barrier, 2)
    streams = []
    for block, (recv, send0_buf) in enumerate(((recv0, send0), (recv1, send1))):
        cols = pl.ds(block * width, width)
        direction = 1 if block == 0 else -1
        own = lambda c, i, cols=cols: x_ref[pl.ds(pl.multiple_of(c * rows, 8), rows), cols].astype(jnp.float32)

        def finish(i, v, cols=cols):
            o_ref[:, cols] = v.astype(o_ref.dtype)

        def stream(own=own, recv=recv, send0_buf=send0_buf, finish=finish, direction=direction, base=block):
            copies = []
            for copies in ring_phase(n_t, me_t, (t_dev(direction), direction), own, 1, recv, send0_buf,
                                     send_sems, recv_sems, base * (n_t - 1), finish):
                yield
            for copy in copies:
                copy.wait_send()

        streams.append(stream())
    run_in_order(streams, [0, 1] * n_t)


def head_sum(x, n_t):
    rows, model_width = x.shape[0] // n_t, x.shape[1]
    width = model_width // 2
    scratch = []
    for _ in range(2):
        scratch += [
            pltpu.VMEM((n_t - 1, 1, rows, width), jnp.bfloat16),
            pltpu.VMEM((1, rows, width), jnp.bfloat16),
        ]
    copies = 2 * (n_t - 1)
    scratch += [pltpu.SemaphoreType.DMA((copies,)), pltpu.SemaphoreType.DMA((copies,))]
    return pl.pallas_call(
        functools.partial(head_sum_kernel, n_t),
        out_shape=jax.ShapeDtypeStruct((rows, model_width), jnp.bfloat16),
        in_specs=[pl.BlockSpec(memory_space=pltpu.VMEM)],
        out_specs=pl.BlockSpec(memory_space=pltpu.VMEM),
        scratch_shapes=scratch,
        compiler_params=pltpu.CompilerParams(collective_id=2, has_side_effects=True),
    )(x)


def expert_exchange_kernel(n_e, x_ref, o_ref, recv, recv_sems, send_sems):
    me_dp = lax.axis_index("dp")
    me_e = lax.axis_index("expert")
    me_t = lax.axis_index("tensor")
    barrier = pltpu.get_barrier_semaphore()
    for k in range(1, n_e):
        pl.semaphore_signal(barrier, 1, device_id=(me_dp, lax.rem(me_e + k, n_e), me_t),
                            device_id_type=MESH_ID)
    pl.semaphore_wait(barrier, n_e - 1)
    copies = []
    for k in range(1, n_e):
        target = lax.rem(me_e + k, n_e)
        copy = pltpu.make_async_remote_copy(
            src_ref=x_ref.at[target],
            dst_ref=recv.at[me_e],
            send_sem=send_sems.at[k - 1],
            recv_sem=recv_sems.at[k - 1],
            device_id=(me_dp, target, me_t),
            device_id_type=MESH_ID,
        )
        copy.start()
        copies.append(copy)
    o_ref[me_e] = x_ref[me_e]
    for k in range(1, n_e):
        copies[k - 1].wait_recv()
        source = lax.rem(me_e + n_e - k, n_e)
        o_ref[source] = recv[source]
    for copy in copies:
        copy.wait_send()


def expert_exchange(x, collective):
    n_e = x.shape[0]
    return pl.pallas_call(
        functools.partial(expert_exchange_kernel, n_e),
        out_shape=jax.ShapeDtypeStruct(x.shape, x.dtype),
        in_specs=[pl.BlockSpec(memory_space=pltpu.VMEM)],
        out_specs=pl.BlockSpec(memory_space=pltpu.VMEM),
        scratch_shapes=[
            pltpu.VMEM(x.shape, x.dtype),
            pltpu.SemaphoreType.DMA((n_e - 1,)),
            pltpu.SemaphoreType.DMA((n_e - 1,)),
        ],
        compiler_params=pltpu.CompilerParams(collective_id=collective, has_side_effects=True),
    )(x)


def gather_feed_phase(n, me, step_to, chunk, send_sems, recv_sems, first_sem, process, own_too):
    copies = []
    for s in range(n - 1):
        c = lax.rem(me + n * 2 - step_to[1] * s, n)
        if s > 0:
            copies[-1].wait_recv()
        copy = pltpu.make_async_remote_copy(
            src_ref=chunk(c),
            dst_ref=chunk(c),
            send_sem=send_sems.at[first_sem + s],
            recv_sem=recv_sems.at[first_sem + s],
            device_id=step_to[0],
            device_id_type=MESH_ID,
        )
        copy.start()
        copies.append(copy)
        if s > 0 or own_too:
            process(c)
        yield copies
    copies[-1].wait_recv()
    process(lax.rem(me + n * 2 - step_to[1] * (n - 1), n))
    yield copies


def expert_front_kernel(n_dp, n_t, widths, order, x_ref, wg_ref, wu_ref, o_ref, *scratch):
    recv_sems, send_sems = scratch[-2], scratch[-1]
    gate_acc, up_acc = scratch[-4], scratch[-3]
    bufs = scratch[:-4]
    me_dp = lax.axis_index("dp")
    me_t = lax.axis_index("tensor")
    me_e = lax.axis_index("expert")
    rows = x_ref.shape[0]

    def dp_dev(d):
        return (lax.rem(me_dp + n_dp + d, n_dp), me_e, me_t)

    def t_dev(d):
        return (me_dp, me_e, lax.rem(me_t + n_t + d, n_t))

    gate_acc[...] = jnp.zeros_like(gate_acc)
    up_acc[...] = jnp.zeros_like(up_acc)
    for block in range(4):
        cols = pl.ds(sum(widths[:block]), widths[block])
        if block < 2:
            bufs[block][me_t, me_dp] = x_ref[:, cols]
        else:
            bufs[block][me_dp, me_t] = x_ref[:, cols]

    barrier = pltpu.get_barrier_semaphore()
    for dev in (dp_dev(1), dp_dev(-1), t_dev(1), t_dev(-1)):
        pl.semaphore_signal(barrier, 1, device_id=dev, device_id_type=MESH_ID)
    pl.semaphore_wait(barrier, 4)

    def feed(piece, row_chunk, cols):
        start = pl.multiple_of(row_chunk * rows, 16)
        v = piece[...]
        dims = (((1,), (1,)), ((), ()))
        gate_acc[pl.ds(start, rows), :] += lax.dot_general(
            v, wg_ref[:, cols], dims, preferred_element_type=jnp.float32)
        up_acc[pl.ds(start, rows), :] += lax.dot_general(
            v, wu_ref[:, cols], dims, preferred_element_type=jnp.float32)

    streams = []
    sem_at = 0
    for block in range(4):
        direction = 1 if block % 2 == 0 else -1
        g = bufs[block]
        cols = pl.ds(sum(widths[:block]), widths[block])
        if block < 2:
            def p1(c, g=g, cols=cols):
                feed(g.at[me_t, c], c * n_t + me_t, cols)

            def p2(c, g=g, cols=cols):
                def body(d, carry):
                    feed(g.at[c, d], d * n_t + c, cols)
                    return carry
                lax.fori_loop(0, n_dp, body, 0)
            first = (n_dp, me_dp, (dp_dev(direction), direction), lambda c, g=g: g.at[me_t, c], p1)
            second = (n_t, me_t, (t_dev(direction), direction), lambda c, g=g: g.at[c], p2)
        else:
            def p1(c, g=g, cols=cols):
                feed(g.at[me_dp, c], me_dp * n_t + c, cols)

            def p2(c, g=g, cols=cols):
                def body(t, carry):
                    feed(g.at[c, t], c * n_t + t, cols)
                    return carry
                lax.fori_loop(0, n_t, body, 0)
            first = (n_t, me_t, (t_dev(direction), direction), lambda c, g=g: g.at[me_dp, c], p1)
            second = (n_dp, me_dp, (dp_dev(direction), direction), lambda c, g=g: g.at[c], p2)

        def stream(first=first, second=second, base=sem_at):
            n1, me1, to1, chunk1, proc1 = first
            copies = []
            for copies in gather_feed_phase(n1, me1, to1, chunk1, send_sems, recv_sems, base, proc1, True):
                yield
            done1 = copies
            n2, me2, to2, chunk2, proc2 = second
            for copies in gather_feed_phase(n2, me2, to2, chunk2, send_sems, recv_sems, base + n1 - 1,
                                            proc2, False):
                yield
            for copy in done1 + copies:
                copy.wait_send()

        streams.append(stream())
        sem_at += n_dp + n_t - 2

    run_in_order(streams, order)

    tile = 128

    def finish(i, carry):
        at = pl.ds(pl.multiple_of(i * tile, tile), tile)
        gate = gate_acc[at, :]
        o_ref[at, :] = (gate / (1.0 + jnp.exp(-gate)) * up_acc[at, :]).astype(o_ref.dtype)
        return carry

    lax.fori_loop(0, o_ref.shape[0] // tile, finish, 0)


def expert_front(x, gate_w, up_w, n_dp, n_t):
    rows, model_width = x.shape
    inner = gate_w.shape[0]
    widths, order = split_plan(n_dp, n_t, rows, model_width, False, per_step=1.0)
    scratch = [
        pltpu.VMEM((n_t, n_dp, rows, widths[0]), jnp.bfloat16),
        pltpu.VMEM((n_t, n_dp, rows, widths[1]), jnp.bfloat16),
        pltpu.VMEM((n_dp, n_t, rows, widths[2]), jnp.bfloat16),
        pltpu.VMEM((n_dp, n_t, rows, widths[3]), jnp.bfloat16),
        pltpu.VMEM((n_dp * n_t * rows, inner), jnp.float32),
        pltpu.VMEM((n_dp * n_t * rows, inner), jnp.float32),
    ]
    copies = 4 * (n_dp + n_t - 2)
    scratch += [pltpu.SemaphoreType.DMA((copies,)), pltpu.SemaphoreType.DMA((copies,))]
    return pl.pallas_call(
        functools.partial(expert_front_kernel, n_dp, n_t, tuple(widths), tuple(order)),
        out_shape=jax.ShapeDtypeStruct((n_dp * n_t * rows, inner), jnp.bfloat16),
        in_specs=[pl.BlockSpec(memory_space=pltpu.VMEM)] * 3,
        out_specs=pl.BlockSpec(memory_space=pltpu.VMEM),
        scratch_shapes=scratch,
        compiler_params=pltpu.CompilerParams(
            collective_id=1, has_side_effects=True, vmem_limit_bytes=60 * 1024 * 1024
        ),
    )(x, gate_w, up_w)


def moe_sum(hidden, down, n_dp, n_t):
    rows, model_width = hidden.shape[0] // (n_dp * n_t), down.shape[1]
    widths, order = split_plan(n_dp, n_t, rows, model_width, True)
    scratch = []
    for block in range(4):
        width = widths[block]
        if block < 2:
            n1, lead, n2 = n_dp, n_t, n_t
        else:
            n1, lead, n2 = n_t, n_dp, n_dp
        scratch += [
            pltpu.VMEM((n1 - 1, lead, rows, width), jnp.bfloat16),
            pltpu.VMEM((lead, rows, width), jnp.bfloat16),
            pltpu.VMEM((lead, rows, width), jnp.float32),
            pltpu.VMEM((n2 - 1, 1, rows, width), jnp.bfloat16),
            pltpu.VMEM((1, rows, width), jnp.bfloat16),
        ]
    copies = 4 * (n_dp + n_t - 2)
    scratch += [pltpu.SemaphoreType.DMA((copies,)), pltpu.SemaphoreType.DMA((copies,))]
    return pl.pallas_call(
        functools.partial(moe_sum_kernel, n_dp, n_t, tuple(widths), tuple(order)),
        out_shape=jax.ShapeDtypeStruct((rows, model_width), jnp.bfloat16),
        in_specs=[pl.BlockSpec(memory_space=pltpu.VMEM)] * 2,
        out_specs=pl.BlockSpec(memory_space=pltpu.VMEM),
        scratch_shapes=scratch,
        compiler_params=pltpu.CompilerParams(
            collective_id=0, has_side_effects=True, vmem_limit_bytes=60 * 1024 * 1024
        ),
    )(hidden, down)


def normalize(parts):
    highest = reduce(
        jnp.maximum,
        [
            jnp.max(jnp.where(visible, scores, -jnp.inf), axis=-1, keepdims=True)
            for scores, visible in parts
        ],
    )
    portions = [jnp.where(visible, jnp.exp(scores - highest), 0.0) for scores, visible in parts]
    denominator = reduce(
        jnp.add, [jnp.sum(portion, axis=-1, keepdims=True) for portion in portions]
    )
    return [(portion / denominator).astype(jnp.bfloat16) for portion in portions]


def attend(question_vectors, new_keys, new_values, key_pages, value_pages, table, spans):
    rows_all, head_count, head_width = question_vectors.shape
    kv_heads = new_keys.shape[1]
    group_size = head_count // kv_heads
    single_count = spans.shape[0] - 1
    page_count = table.shape[1]
    page_width = key_pages.shape[2]
    context = page_count * page_width
    inverse_root = 1.0 / math.sqrt(head_width)
    pick = (table[..., None] == jnp.arange(key_pages.shape[0], dtype=table.dtype)).astype(key_pages.dtype)
    page_keys = jnp.einsum(
        "rmp,pkab->rmkab", pick, key_pages, preferred_element_type=jnp.float32
    ).astype(key_pages.dtype)
    page_values = jnp.einsum(
        "rmp,pkab->rmkab", pick, value_pages, preferred_element_type=jnp.float32
    ).astype(value_pages.dtype)
    grouped = question_vectors.reshape(rows_all, kv_heads, group_size, head_width)
    positions = jnp.arange(context, dtype=jnp.int32)
    single_q = grouped[:single_count]
    cache_dec = (
        jnp.einsum(
            "rkgh,rmkph->rkgmp",
            single_q,
            page_keys[:single_count],
            preferred_element_type=jnp.float32,
        ).reshape(single_count, kv_heads, group_size, context)
        * inverse_root
    )
    seen_dec = (positions[None, :] < spans[:single_count, None])[:, None, None, :]
    own_dec = (
        jnp.einsum(
            "rkgh,rkh->rkg", single_q, new_keys[:single_count], preferred_element_type=jnp.float32
        )[..., None]
        * inverse_root
    )
    weight_cache, weight_own = normalize(
        [(cache_dec, seen_dec), (own_dec, jnp.full(own_dec.shape, True))]
    )
    out_dec = jnp.einsum(
        "rkgmp,rmkph->rkgh",
        weight_cache.reshape(single_count, kv_heads, group_size, page_count, page_width),
        page_values[:single_count],
        preferred_element_type=jnp.float32,
    )
    out_dec = (
        out_dec
        + weight_own.astype(jnp.float32)
        * new_values[:single_count].astype(jnp.float32)[:, :, None, :]
    )
    prompt_q = grouped[single_count:]
    prompt_rows = rows_all - single_count
    cache_pro = (
        jnp.einsum(
            "rkgh,mkph->rkgmp",
            prompt_q,
            page_keys[single_count],
            preferred_element_type=jnp.float32,
        ).reshape(prompt_rows, kv_heads, group_size, context)
        * inverse_root
    )
    seen_pro = (positions < spans[single_count])[None, None, None, :]
    new_pro = (
        jnp.einsum(
            "rkgh,mkh->rkgm", prompt_q, new_keys[single_count:], preferred_element_type=jnp.float32
        )
        * inverse_root
    )
    prompt_index = jnp.arange(prompt_rows, dtype=jnp.int32)
    causal = (prompt_index[:, None] >= prompt_index[None, :])[:, None, None, :]
    weight_cpro, weight_npro = normalize([(cache_pro, seen_pro), (new_pro, causal)])
    out_pro = jnp.einsum(
        "rkgmp,mkph->rkgh",
        weight_cpro.reshape(prompt_rows, kv_heads, group_size, page_count, page_width),
        page_values[single_count],
        preferred_element_type=jnp.float32,
    )
    out_pro = out_pro + jnp.einsum(
        "rkgm,mkh->rkgh", weight_npro, new_values[single_count:], preferred_element_type=jnp.float32
    )
    joined = jnp.concatenate([out_dec, out_pro], axis=0).astype(jnp.bfloat16)
    return joined.reshape(rows_all, head_count * head_width)


def slot_table(member, ranking, keeping, slot_count):
    slot_hit = (
        ranking[:, :, None, None] == jnp.arange(slot_count, dtype=jnp.int32)[None, None, None, :]
    )
    return ((member[..., None] > 0) & keeping[:, :, None, None] & slot_hit).astype(jnp.bfloat16)


def expert_pass(send, gating_matrices, expand_matrices, contract_matrices):
    specialist_index, slot_count, model_width = send.shape
    local_count = gating_matrices.shape[0]
    assert local_count == 1
    arrived = expert_exchange(send, 3).reshape(specialist_index * slot_count, model_width)
    hidden = expert_front(
        arrived,
        gating_matrices[0],
        expand_matrices[0],
        lax.axis_size("dp"),
        lax.axis_size("tensor"),
    )
    down = contract_matrices[0]
    n_dp, n_t = lax.axis_size("dp"), lax.axis_size("tensor")
    summed = moe_sum(hidden, down, n_dp, n_t)
    return expert_exchange(summed.reshape(specialist_index, slot_count, model_width), 4)


def local(
    skip_stream_entry,
    question_vectors,
    fresh_lookup_vectors,
    fresh_content_vectors,
    stored_lookup_sheets,
    stored_content_sheets,
    sequence_sheet_map,
    stored_position_counts,
    attention_merge_matrix,
    premix_scale_factor,
    chosen_specialists,
    selection_shares,
    allowed_placements,
    favored_specialist,
    gating_matrices,
    expand_matrices,
    contract_matrices,
):
    token_count = chosen_specialists.shape[0]
    specialist_index = allowed_placements.shape[0]
    picked = (
        chosen_specialists[:, :, None]
        == jnp.arange(specialist_index, dtype=jnp.int32)[None, None, :]
    ).astype(jnp.int32)
    flat_routes = picked.reshape(token_count * 2, specialist_index)
    busiest_specialist = favored_specialist[0]
    before = (jnp.cumsum(flat_routes, axis=0) - flat_routes).reshape(
        token_count, 2, specialist_index
    )
    ranking = jnp.sum(before * picked, axis=2)
    placement_ceiling = jnp.where(
        jnp.arange(specialist_index, dtype=jnp.int32) == busiest_specialist,
        PLACEMENT_MOST,
        allowed_placements,
    )
    keeping = ranking < jnp.sum(picked * placement_ceiling[None, None, :], axis=2)
    row_total = question_vectors.shape[0]
    heads_out = attend(
        question_vectors.reshape(row_total, -1, HD),
        fresh_lookup_vectors.reshape(row_total, -1, HD),
        fresh_content_vectors.reshape(row_total, -1, HD),
        stored_lookup_sheets,
        stored_content_sheets,
        sequence_sheet_map,
        stored_position_counts,
    )
    own_attn = head_sum(
        jnp.dot(heads_out, attention_merge_matrix, preferred_element_type=jnp.float32).astype(
            jnp.bfloat16
        ),
        lax.axis_size("tensor"),
    ).astype(jnp.float32)
    stream = (skip_stream_entry.astype(jnp.float32) + own_attn).astype(jnp.bfloat16)
    wide = stream.astype(jnp.float32)
    squares = jnp.mean(wide * wide, axis=1, keepdims=True)
    normed = (wide * lax.rsqrt(squares + 1e-05) * premix_scale_factor.astype(jnp.float32)).astype(
        jnp.bfloat16
    )
    main_slots = PLACEMENT_MOST
    table_main = slot_table(picked, ranking, keeping, main_slots)
    send = jnp.einsum(
        "nkes,nd->esd", table_main, normed, preferred_element_type=jnp.float32
    ).astype(jnp.bfloat16)
    expert_out = expert_pass(send, gating_matrices, expand_matrices, contract_matrices)
    chosen = jnp.einsum("nkes,esd->nkd", table_main, expert_out, preferred_element_type=jnp.float32)
    mixed = jnp.sum(selection_shares[:, :, None] * chosen, axis=1)
    return (wide + mixed).astype(jnp.bfloat16)


def solution(mesh):
    placed = (
        P(("dp", "expert", "tensor"), None),
        P(("dp", "expert"), "tensor"),
        P(("dp", "expert"), "tensor"),
        P(("dp", "expert"), "tensor"),
        P(("dp", "expert"), "tensor", None, None),
        P(("dp", "expert"), "tensor", None, None),
        P(("dp", "expert"), None),
        P(("dp", "expert")),
        P("tensor", None),
        P(),
        P(("dp", "expert", "tensor"), None),
        P(("dp", "expert", "tensor"), None),
        P(),
        P(),
        P("expert", ("dp", "tensor"), None),
        P("expert", ("dp", "tensor"), None),
        P("expert", ("dp", "tensor"), None),
    )
    return jax.shard_map(
        local,
        mesh=mesh,
        in_specs=placed,
        out_specs=P(("dp", "expert", "tensor"), None),
        check_vma=False,
    )
```

```python
from functools import reduce
import functools
import math

import jax
import jax.numpy as jnp
from jax import lax
from jax.experimental import pallas as pl
from jax.experimental.pallas import tpu as pltpu
from jax.sharding import PartitionSpec as P

HD = 128
PLACEMENT_MOST = 6


MESH_ID = pl.DeviceIdType.MESH


def plan_order(events, rate=50000.0, latency=1.5, per_step=0.3):
    ready = [0.0] * len(events)
    at = [0] * len(events)
    free = {}
    clock = 0.0
    order = []
    while True:
        live = [i for i in range(len(events)) if at[i] < len(events[i])]
        if not live:
            return order, clock
        i = min(live, key=lambda k: (ready[k], k))
        clock = max(clock, ready[i]) + per_step
        send = events[i][at[i]]
        if send is None:
            ready[i] = clock
        else:
            link, size = send
            start = max(clock, free.get(link, 0.0))
            free[link] = start + size / rate
            ready[i] = free[link] + latency
        order.append(i)
        at[i] += 1


def ring_events(n1, n2, link1, link2, size1, size2):
    return [(link1, size1)] * (n1 - 1) + [None] + [(link2, size2)] * (n2 - 1) + [None]


def split_plan(n_dp, n_t, rows, model_width, reduce, per_step=0.3):
    best = None
    for first_dp in range(128, model_width // 2, 128):
        widths = [first_dp, first_dp, model_width // 2 - first_dp, model_width // 2 - first_dp]
        events = []
        for block, width in enumerate(widths):
            unit = rows * width * 2
            sign = "+" if block % 2 == 0 else "-"
            if block < 2:
                big1, big2 = (n_t * unit, unit) if reduce else (unit, n_dp * unit)
                events.append(ring_events(n_dp, n_t, "z" + sign, "y" + sign, big1, big2))
            else:
                big1, big2 = (n_dp * unit, unit) if reduce else (unit, n_t * unit)
                events.append(ring_events(n_t, n_dp, "y" + sign, "z" + sign, big1, big2))
        order, finish = plan_order(events, per_step=per_step)
        if best is None or finish < best[0]:
            best = (finish, widths, order)
    return best[1], best[2]


def run_in_order(streams, order):
    for i in order:
        next(streams[i])
    for st in streams:
        for _ in st:
            pass


def ring_phase(n, me, step_to, own, chunk_lead, recv, send0, send_sems, recv_sems, first_sem, finish):
    copies = []
    for s in range(n - 1):
        c = lax.rem(me + n * 2 - step_to[1] * (s + 1), n)
        if s == 0:
            for i in range(chunk_lead):
                send0[i] = own(c, i).astype(send0.dtype)
            src = send0
        else:
            copies[-1].wait_recv()
            for i in range(chunk_lead):
                recv[s - 1, i] = (own(c, i) + recv[s - 1, i].astype(jnp.float32)).astype(recv.dtype)
            src = recv.at[s - 1]
        copy = pltpu.make_async_remote_copy(
            src_ref=src,
            dst_ref=recv.at[s],
            send_sem=send_sems.at[first_sem + s],
            recv_sem=recv_sems.at[first_sem + s],
            device_id=step_to[0],
            device_id_type=MESH_ID,
        )
        copy.start()
        copies.append(copy)
        yield copies
    copies[-1].wait_recv()
    for i in range(chunk_lead):
        finish(i, own(me, i) + recv[n - 2, i].astype(jnp.float32))
    yield copies


def block_product(h_ref, w_ref, chunk, cols, rows):
    start = pl.multiple_of(chunk * rows, 16)
    product = jnp.dot(h_ref[pl.ds(start, rows), :], w_ref[:, cols], preferred_element_type=jnp.float32)
    return product.astype(jnp.bfloat16).astype(jnp.float32)


def moe_sum_kernel(n_dp, n_t, widths, order, h_ref, w_ref, o_ref, *scratch):
    recv_sems, send_sems = scratch[-2], scratch[-1]
    bufs = scratch[:-2]
    me_dp = lax.axis_index("dp")
    me_t = lax.axis_index("tensor")
    me_e = lax.axis_index("expert")

    def dp_dev(d):
        return (lax.rem(me_dp + n_dp + d, n_dp), me_e, me_t)

    def t_dev(d):
        return (me_dp, me_e, lax.rem(me_t + n_t + d, n_t))

    barrier = pltpu.get_barrier_semaphore()
    for dev in (dp_dev(1), dp_dev(-1), t_dev(1), t_dev(-1)):
        pl.semaphore_signal(barrier, 1, device_id=dev, device_id_type=MESH_ID)
    pl.semaphore_wait(barrier, 4)

    streams = []
    sem_at = 0
    for block in range(4):
        cols = pl.ds(sum(widths[:block]), widths[block])
        direction = 1 if block % 2 == 0 else -1
        r1, s1, acc, r2, s2 = bufs[block * 5: block * 5 + 5]
        if block < 2:
            first = (n_dp, me_dp, (dp_dev(direction), direction), n_t)
            own1 = lambda c, i, cols=cols: block_product(h_ref, w_ref, c * n_t + i, cols, o_ref.shape[0])
            second = (n_t, me_t, (t_dev(direction), direction))
        else:
            first = (n_t, me_t, (t_dev(direction), direction), n_dp)
            own1 = lambda c, i, cols=cols: block_product(h_ref, w_ref, i * n_t + c, cols, o_ref.shape[0])
            second = (n_dp, me_dp, (dp_dev(direction), direction))

        def fin1(i, v, acc=acc):
            acc[i] = v

        def fin2(i, v, cols=cols):
            o_ref[:, cols] = v.astype(o_ref.dtype)

        own2 = lambda c, i, acc=acc: acc[c]

        def stream(first=first, second=second, own1=own1, own2=own2, r1=r1, s1=s1, r2=r2, s2=s2,
                   fin1=fin1, fin2=fin2, base=sem_at):
            n1, me1, to1, lead = first
            copies = []
            for copies in ring_phase(n1, me1, to1, own1, lead, r1, s1, send_sems, recv_sems, base, fin1):
                yield
            done1 = copies
            n2, me2, to2 = second
            for copies in ring_phase(n2, me2, to2, own2, 1, r2, s2, send_sems, recv_sems, base + n1 - 1,
                                     lambda i, v: fin2(i, v)):
                yield
            for copy in done1 + copies:
                copy.wait_send()

        streams.append(stream())
        sem_at += n_dp + n_t - 2

    run_in_order(streams, order)


def gather_phase(n, me, step_to, chunk, send_sems, recv_sems, first_sem):
    copies = []
    for s in range(n - 1):
        c = lax.rem(me + n * 2 - step_to[1] * s, n)
        if s > 0:
            copies[-1].wait_recv()
        copy = pltpu.make_async_remote_copy(
            src_ref=chunk(c),
            dst_ref=chunk(c),
            send_sem=send_sems.at[first_sem + s],
            recv_sem=recv_sems.at[first_sem + s],
            device_id=step_to[0],
            device_id_type=MESH_ID,
        )
        copy.start()
        copies.append(copy)
        yield copies
    copies[-1].wait_recv()
    yield copies


def row_gather_kernel(n_dp, n_t, widths, order, x_ref, o_ref, *scratch):
    recv_sems, send_sems = scratch[-2], scratch[-1]
    bufs = scratch[:-2]
    me_dp = lax.axis_index("dp")
    me_t = lax.axis_index("tensor")
    me_e = lax.axis_index("expert")
    rows = x_ref.shape[0]

    def dp_dev(d):
        return (lax.rem(me_dp + n_dp + d, n_dp), me_e, me_t)

    def t_dev(d):
        return (me_dp, me_e, lax.rem(me_t + n_t + d, n_t))

    for block in range(4):
        cols = pl.ds(sum(widths[:block]), widths[block])
        if block < 2:
            bufs[block][me_t, me_dp] = x_ref[:, cols]
        else:
            bufs[block][me_dp, me_t] = x_ref[:, cols]

    barrier = pltpu.get_barrier_semaphore()
    for dev in (dp_dev(1), dp_dev(-1), t_dev(1), t_dev(-1)):
        pl.semaphore_signal(barrier, 1, device_id=dev, device_id_type=MESH_ID)
    pl.semaphore_wait(barrier, 4)

    streams = []
    sem_at = 0
    for block in range(4):
        direction = 1 if block % 2 == 0 else -1
        g = bufs[block]
        if block < 2:
            first = (n_dp, me_dp, (dp_dev(direction), direction), lambda c, g=g: g.at[me_t, c])
            second = (n_t, me_t, (t_dev(direction), direction), lambda c, g=g: g.at[c])
        else:
            first = (n_t, me_t, (t_dev(direction), direction), lambda c, g=g: g.at[me_dp, c])
            second = (n_dp, me_dp, (dp_dev(direction), direction), lambda c, g=g: g.at[c])

        def stream(first=first, second=second, base=sem_at):
            n1, me1, to1, chunk1 = first
            copies = []
            for copies in gather_phase(n1, me1, to1, chunk1, send_sems, recv_sems, base):
                yield
            done1 = copies
            n2, me2, to2, chunk2 = second
            for copies in gather_phase(n2, me2, to2, chunk2, send_sems, recv_sems, base + n1 - 1):
                yield
            for copy in done1 + copies:
                copy.wait_send()

        streams.append(stream())
        sem_at += n_dp + n_t - 2

    run_in_order(streams, order)

    for block in range(4):
        cols = pl.ds(sum(widths[:block]), widths[block])
        for d in range(n_dp):
            for t in range(n_t):
                piece = bufs[block][t, d] if block < 2 else bufs[block][d, t]
                o_ref[pl.ds((d * n_t + t) * rows, rows), cols] = piece


def row_gather(x, n_dp, n_t):
    rows, model_width = x.shape
    widths, order = split_plan(n_dp, n_t, rows, model_width, False)
    scratch = [
        pltpu.VMEM((n_t, n_dp, rows, widths[0]), jnp.bfloat16),
        pltpu.VMEM((n_t, n_dp, rows, widths[1]), jnp.bfloat16),
        pltpu.VMEM((n_dp, n_t, rows, widths[2]), jnp.bfloat16),
        pltpu.VMEM((n_dp, n_t, rows, widths[3]), jnp.bfloat16),
    ]
    copies = 4 * (n_dp + n_t - 2)
    scratch += [pltpu.SemaphoreType.DMA((copies,)), pltpu.SemaphoreType.DMA((copies,))]
    return pl.pallas_call(
        functools.partial(row_gather_kernel, n_dp, n_t, tuple(widths), tuple(order)),
        out_shape=jax.ShapeDtypeStruct((n_dp * n_t * rows, model_width), jnp.bfloat16),
        in_specs=[pl.BlockSpec(memory_space=pltpu.VMEM)],
        out_specs=pl.BlockSpec(memory_space=pltpu.VMEM),
        scratch_shapes=scratch,
        compiler_params=pltpu.CompilerParams(
            collective_id=1, has_side_effects=True, vmem_limit_bytes=60 * 1024 * 1024
        ),
    )(x)


def head_sum_kernel(n_t, x_ref, o_ref, recv0, send0, recv1, send1, recv_sems, send_sems):
    me_dp = lax.axis_index("dp")
    me_e = lax.axis_index("expert")
    me_t = lax.axis_index("tensor")
    rows = o_ref.shape[0]
    width = o_ref.shape[1] // 2

    def t_dev(d):
        return (me_dp, me_e, lax.rem(me_t + n_t + d, n_t))

    barrier = pltpu.get_barrier_semaphore()
    for dev in (t_dev(1), t_dev(-1)):
        pl.semaphore_signal(barrier, 1, device_id=dev, device_id_type=MESH_ID)
    pl.semaphore_wait(barrier, 2)
    streams = []
    for block, (recv, send0_buf) in enumerate(((recv0, send0), (recv1, send1))):
        cols = pl.ds(block * width, width)
        direction = 1 if block == 0 else -1
        own = lambda c, i, cols=cols: x_ref[pl.ds(pl.multiple_of(c * rows, 8), rows), cols].astype(jnp.float32)

        def finish(i, v, cols=cols):
            o_ref[:, cols] = v.astype(o_ref.dtype)

        def stream(own=own, recv=recv, send0_buf=send0_buf, finish=finish, direction=direction, base=block):
            copies = []
            for copies in ring_phase(n_t, me_t, (t_dev(direction), direction), own, 1, recv, send0_buf,
                                     send_sems, recv_sems, base * (n_t - 1), finish):
                yield
            for copy in copies:
                copy.wait_send()

        streams.append(stream())
    run_in_order(streams, [0, 1] * n_t)


def head_sum(x, n_t):
    rows, model_width = x.shape[0] // n_t, x.shape[1]
    width = model_width // 2
    scratch = []
    for _ in range(2):
        scratch += [
            pltpu.VMEM((n_t - 1, 1, rows, width), jnp.bfloat16),
            pltpu.VMEM((1, rows, width), jnp.bfloat16),
        ]
    copies = 2 * (n_t - 1)
    scratch += [pltpu.SemaphoreType.DMA((copies,)), pltpu.SemaphoreType.DMA((copies,))]
    return pl.pallas_call(
        functools.partial(head_sum_kernel, n_t),
        out_shape=jax.ShapeDtypeStruct((rows, model_width), jnp.bfloat16),
        in_specs=[pl.BlockSpec(memory_space=pltpu.VMEM)],
        out_specs=pl.BlockSpec(memory_space=pltpu.VMEM),
        scratch_shapes=scratch,
        compiler_params=pltpu.CompilerParams(collective_id=2, has_side_effects=True),
    )(x)


def expert_exchange_kernel(n_e, x_ref, o_ref, recv, recv_sems, send_sems):
    me_dp = lax.axis_index("dp")
    me_e = lax.axis_index("expert")
    me_t = lax.axis_index("tensor")
    barrier = pltpu.get_barrier_semaphore()
    for k in range(1, n_e):
        pl.semaphore_signal(barrier, 1, device_id=(me_dp, lax.rem(me_e + k, n_e), me_t),
                            device_id_type=MESH_ID)
    pl.semaphore_wait(barrier, n_e - 1)
    copies = []
    for k in range(1, n_e):
        target = lax.rem(me_e + k, n_e)
        copy = pltpu.make_async_remote_copy(
            src_ref=x_ref.at[target],
            dst_ref=recv.at[me_e],
            send_sem=send_sems.at[k - 1],
            recv_sem=recv_sems.at[k - 1],
            device_id=(me_dp, target, me_t),
            device_id_type=MESH_ID,
        )
        copy.start()
        copies.append(copy)
    o_ref[me_e] = x_ref[me_e]
    for k in range(1, n_e):
        copies[k - 1].wait_recv()
        source = lax.rem(me_e + n_e - k, n_e)
        o_ref[source] = recv[source]
    for copy in copies:
        copy.wait_send()


def expert_exchange(x, collective):
    n_e = x.shape[0]
    return pl.pallas_call(
        functools.partial(expert_exchange_kernel, n_e),
        out_shape=jax.ShapeDtypeStruct(x.shape, x.dtype),
        in_specs=[pl.BlockSpec(memory_space=pltpu.VMEM)],
        out_specs=pl.BlockSpec(memory_space=pltpu.VMEM),
        scratch_shapes=[
            pltpu.VMEM(x.shape, x.dtype),
            pltpu.SemaphoreType.DMA((n_e - 1,)),
            pltpu.SemaphoreType.DMA((n_e - 1,)),
        ],
        compiler_params=pltpu.CompilerParams(collective_id=collective, has_side_effects=True),
    )(x)


def gather_feed_phase(n, me, step_to, chunk, send_sems, recv_sems, first_sem, process, own_too):
    copies = []
    for s in range(n - 1):
        c = lax.rem(me + n * 2 - step_to[1] * s, n)
        if s > 0:
            copies[-1].wait_recv()
        copy = pltpu.make_async_remote_copy(
            src_ref=chunk(c),
            dst_ref=chunk(c),
            send_sem=send_sems.at[first_sem + s],
            recv_sem=recv_sems.at[first_sem + s],
            device_id=step_to[0],
            device_id_type=MESH_ID,
        )
        copy.start()
        copies.append(copy)
        if s > 0 or own_too:
            process(c)
        yield copies
    copies[-1].wait_recv()
    process(lax.rem(me + n * 2 - step_to[1] * (n - 1), n))
    yield copies


def expert_front_kernel(n_dp, n_t, widths, order, x_ref, wg_ref, wu_ref, o_ref, *scratch):
    recv_sems, send_sems = scratch[-2], scratch[-1]
    gate_acc, up_acc = scratch[-4], scratch[-3]
    bufs = scratch[:-4]
    me_dp = lax.axis_index("dp")
    me_t = lax.axis_index("tensor")
    me_e = lax.axis_index("expert")
    rows = x_ref.shape[0]

    def dp_dev(d):
        return (lax.rem(me_dp + n_dp + d, n_dp), me_e, me_t)

    def t_dev(d):
        return (me_dp, me_e, lax.rem(me_t + n_t + d, n_t))

    gate_acc[...] = jnp.zeros_like(gate_acc)
    up_acc[...] = jnp.zeros_like(up_acc)
    for block in range(4):
        cols = pl.ds(sum(widths[:block]), widths[block])
        if block < 2:
            bufs[block][me_t, me_dp] = x_ref[:, cols]
        else:
            bufs[block][me_dp, me_t] = x_ref[:, cols]

    barrier = pltpu.get_barrier_semaphore()
    for dev in (dp_dev(1), dp_dev(-1), t_dev(1), t_dev(-1)):
        pl.semaphore_signal(barrier, 1, device_id=dev, device_id_type=MESH_ID)
    pl.semaphore_wait(barrier, 4)

    def feed(piece, row_chunk, cols):
        start = pl.multiple_of(row_chunk * rows, 16)
        v = piece[...]
        dims = (((1,), (1,)), ((), ()))
        gate_acc[pl.ds(start, rows), :] += lax.dot_general(
            v, wg_ref[:, cols], dims, preferred_element_type=jnp.float32)
        up_acc[pl.ds(start, rows), :] += lax.dot_general(
            v, wu_ref[:, cols], dims, preferred_element_type=jnp.float32)

    streams = []
    sem_at = 0
    for block in range(4):
        direction = 1 if block % 2 == 0 else -1
        g = bufs[block]
        cols = pl.ds(sum(widths[:block]), widths[block])
        if block < 2:
            def p1(c, g=g, cols=cols):
                feed(g.at[me_t, c], c * n_t + me_t, cols)

            def p2(c, g=g, cols=cols):
                def body(d, carry):
                    feed(g.at[c, d], d * n_t + c, cols)
                    return carry
                lax.fori_loop(0, n_dp, body, 0)
            first = (n_dp, me_dp, (dp_dev(direction), direction), lambda c, g=g: g.at[me_t, c], p1)
            second = (n_t, me_t, (t_dev(direction), direction), lambda c, g=g: g.at[c], p2)
        else:
            def p1(c, g=g, cols=cols):
                feed(g.at[me_dp, c], me_dp * n_t + c, cols)

            def p2(c, g=g, cols=cols):
                def body(t, carry):
                    feed(g.at[c, t], c * n_t + t, cols)
                    return carry
                lax.fori_loop(0, n_t, body, 0)
            first = (n_t, me_t, (t_dev(direction), direction), lambda c, g=g: g.at[me_dp, c], p1)
            second = (n_dp, me_dp, (dp_dev(direction), direction), lambda c, g=g: g.at[c], p2)

        def stream(first=first, second=second, base=sem_at):
            n1, me1, to1, chunk1, proc1 = first
            copies = []
            for copies in gather_feed_phase(n1, me1, to1, chunk1, send_sems, recv_sems, base, proc1, True):
                yield
            done1 = copies
            n2, me2, to2, chunk2, proc2 = second
            for copies in gather_feed_phase(n2, me2, to2, chunk2, send_sems, recv_sems, base + n1 - 1,
                                            proc2, False):
                yield
            for copy in done1 + copies:
                copy.wait_send()

        streams.append(stream())
        sem_at += n_dp + n_t - 2

    run_in_order(streams, order)

    tile = 128

    def finish(i, carry):
        at = pl.ds(pl.multiple_of(i * tile, tile), tile)
        gate = gate_acc[at, :]
        o_ref[at, :] = (gate / (1.0 + jnp.exp(-gate)) * up_acc[at, :]).astype(o_ref.dtype)
        return carry

    lax.fori_loop(0, o_ref.shape[0] // tile, finish, 0)


def expert_front(x, gate_w, up_w, n_dp, n_t):
    rows, model_width = x.shape
    inner = gate_w.shape[0]
    widths, order = split_plan(n_dp, n_t, rows, model_width, False, per_step=1.0)
    scratch = [
        pltpu.VMEM((n_t, n_dp, rows, widths[0]), jnp.bfloat16),
        pltpu.VMEM((n_t, n_dp, rows, widths[1]), jnp.bfloat16),
        pltpu.VMEM((n_dp, n_t, rows, widths[2]), jnp.bfloat16),
        pltpu.VMEM((n_dp, n_t, rows, widths[3]), jnp.bfloat16),
        pltpu.VMEM((n_dp * n_t * rows, inner), jnp.float32),
        pltpu.VMEM((n_dp * n_t * rows, inner), jnp.float32),
    ]
    copies = 4 * (n_dp + n_t - 2)
    scratch += [pltpu.SemaphoreType.DMA((copies,)), pltpu.SemaphoreType.DMA((copies,))]
    return pl.pallas_call(
        functools.partial(expert_front_kernel, n_dp, n_t, tuple(widths), tuple(order)),
        out_shape=jax.ShapeDtypeStruct((n_dp * n_t * rows, inner), jnp.bfloat16),
        in_specs=[pl.BlockSpec(memory_space=pltpu.VMEM)] * 3,
        out_specs=pl.BlockSpec(memory_space=pltpu.VMEM),
        scratch_shapes=scratch,
        compiler_params=pltpu.CompilerParams(
            collective_id=1, has_side_effects=True, vmem_limit_bytes=60 * 1024 * 1024
        ),
    )(x, gate_w, up_w)


def moe_sum(hidden, down, n_dp, n_t):
    rows, model_width = hidden.shape[0] // (n_dp * n_t), down.shape[1]
    widths, order = split_plan(n_dp, n_t, rows, model_width, True, per_step=1.0)
    scratch = []
    for block in range(4):
        width = widths[block]
        if block < 2:
            n1, lead, n2 = n_dp, n_t, n_t
        else:
            n1, lead, n2 = n_t, n_dp, n_dp
        scratch += [
            pltpu.VMEM((n1 - 1, lead, rows, width), jnp.bfloat16),
            pltpu.VMEM((lead, rows, width), jnp.bfloat16),
            pltpu.VMEM((lead, rows, width), jnp.float32),
            pltpu.VMEM((n2 - 1, 1, rows, width), jnp.bfloat16),
            pltpu.VMEM((1, rows, width), jnp.bfloat16),
        ]
    copies = 4 * (n_dp + n_t - 2)
    scratch += [pltpu.SemaphoreType.DMA((copies,)), pltpu.SemaphoreType.DMA((copies,))]
    return pl.pallas_call(
        functools.partial(moe_sum_kernel, n_dp, n_t, tuple(widths), tuple(order)),
        out_shape=jax.ShapeDtypeStruct((rows, model_width), jnp.bfloat16),
        in_specs=[pl.BlockSpec(memory_space=pltpu.VMEM)] * 2,
        out_specs=pl.BlockSpec(memory_space=pltpu.VMEM),
        scratch_shapes=scratch,
        compiler_params=pltpu.CompilerParams(
            collective_id=0, has_side_effects=True, vmem_limit_bytes=60 * 1024 * 1024
        ),
    )(hidden, down)


def normalize(parts):
    highest = reduce(
        jnp.maximum,
        [
            jnp.max(jnp.where(visible, scores, -jnp.inf), axis=-1, keepdims=True)
            for scores, visible in parts
        ],
    )
    portions = [jnp.where(visible, jnp.exp(scores - highest), 0.0) for scores, visible in parts]
    denominator = reduce(
        jnp.add, [jnp.sum(portion, axis=-1, keepdims=True) for portion in portions]
    )
    return [(portion / denominator).astype(jnp.bfloat16) for portion in portions]


def attend(question_vectors, new_keys, new_values, key_pages, value_pages, table, spans):
    rows_all, head_count, head_width = question_vectors.shape
    kv_heads = new_keys.shape[1]
    group_size = head_count // kv_heads
    single_count = spans.shape[0] - 1
    page_count = table.shape[1]
    page_width = key_pages.shape[2]
    context = page_count * page_width
    inverse_root = 1.0 / math.sqrt(head_width)
    pick = (table[..., None] == jnp.arange(key_pages.shape[0], dtype=table.dtype)).astype(key_pages.dtype)
    page_keys = jnp.einsum(
        "rmp,pkab->rmkab", pick, key_pages, preferred_element_type=jnp.float32
    ).astype(key_pages.dtype)
    page_values = jnp.einsum(
        "rmp,pkab->rmkab", pick, value_pages, preferred_element_type=jnp.float32
    ).astype(value_pages.dtype)
    grouped = question_vectors.reshape(rows_all, kv_heads, group_size, head_width)
    positions = jnp.arange(context, dtype=jnp.int32)
    single_q = grouped[:single_count]
    cache_dec = (
        jnp.einsum(
            "rkgh,rmkph->rkgmp",
            single_q,
            page_keys[:single_count],
            preferred_element_type=jnp.float32,
        ).reshape(single_count, kv_heads, group_size, context)
        * inverse_root
    )
    seen_dec = (positions[None, :] < spans[:single_count, None])[:, None, None, :]
    own_dec = (
        jnp.einsum(
            "rkgh,rkh->rkg", single_q, new_keys[:single_count], preferred_element_type=jnp.float32
        )[..., None]
        * inverse_root
    )
    weight_cache, weight_own = normalize(
        [(cache_dec, seen_dec), (own_dec, jnp.full(own_dec.shape, True))]
    )
    out_dec = jnp.einsum(
        "rkgmp,rmkph->rkgh",
        weight_cache.reshape(single_count, kv_heads, group_size, page_count, page_width),
        page_values[:single_count],
        preferred_element_type=jnp.float32,
    )
    out_dec = (
        out_dec
        + weight_own.astype(jnp.float32)
        * new_values[:single_count].astype(jnp.float32)[:, :, None, :]
    )
    prompt_q = grouped[single_count:]
    prompt_rows = rows_all - single_count
    cache_pro = (
        jnp.einsum(
            "rkgh,mkph->rkgmp",
            prompt_q,
            page_keys[single_count],
            preferred_element_type=jnp.float32,
        ).reshape(prompt_rows, kv_heads, group_size, context)
        * inverse_root
    )
    seen_pro = (positions < spans[single_count])[None, None, None, :]
    new_pro = (
        jnp.einsum(
            "rkgh,mkh->rkgm", prompt_q, new_keys[single_count:], preferred_element_type=jnp.float32
        )
        * inverse_root
    )
    prompt_index = jnp.arange(prompt_rows, dtype=jnp.int32)
    causal = (prompt_index[:, None] >= prompt_index[None, :])[:, None, None, :]
    weight_cpro, weight_npro = normalize([(cache_pro, seen_pro), (new_pro, causal)])
    out_pro = jnp.einsum(
        "rkgmp,mkph->rkgh",
        weight_cpro.reshape(prompt_rows, kv_heads, group_size, page_count, page_width),
        page_values[single_count],
        preferred_element_type=jnp.float32,
    )
    out_pro = out_pro + jnp.einsum(
        "rkgm,mkh->rkgh", weight_npro, new_values[single_count:], preferred_element_type=jnp.float32
    )
    joined = jnp.concatenate([out_dec, out_pro], axis=0).astype(jnp.bfloat16)
    return joined.reshape(rows_all, head_count * head_width)


def slot_table(member, ranking, keeping, slot_count):
    slot_hit = (
        ranking[:, :, None, None] == jnp.arange(slot_count, dtype=jnp.int32)[None, None, None, :]
    )
    return ((member[..., None] > 0) & keeping[:, :, None, None] & slot_hit).astype(jnp.bfloat16)


def expert_pass(send, gating_matrices, expand_matrices, contract_matrices):
    specialist_index, slot_count, model_width = send.shape
    local_count = gating_matrices.shape[0]
    assert local_count == 1
    arrived = expert_exchange(send, 3).reshape(specialist_index * slot_count, model_width)
    hidden = expert_front(
        arrived,
        gating_matrices[0],
        expand_matrices[0],
        lax.axis_size("dp"),
        lax.axis_size("tensor"),
    )
    down = contract_matrices[0]
    n_dp, n_t = lax.axis_size("dp"), lax.axis_size("tensor")
    summed = moe_sum(hidden, down, n_dp, n_t)
    return expert_exchange(summed.reshape(specialist_index, slot_count, model_width), 4)


def local(
    skip_stream_entry,
    question_vectors,
    fresh_lookup_vectors,
    fresh_content_vectors,
    stored_lookup_sheets,
    stored_content_sheets,
    sequence_sheet_map,
    stored_position_counts,
    attention_merge_matrix,
    premix_scale_factor,
    chosen_specialists,
    selection_shares,
    allowed_placements,
    favored_specialist,
    gating_matrices,
    expand_matrices,
    contract_matrices,
):
    token_count = chosen_specialists.shape[0]
    specialist_index = allowed_placements.shape[0]
    picked = (
        chosen_specialists[:, :, None]
        == jnp.arange(specialist_index, dtype=jnp.int32)[None, None, :]
    ).astype(jnp.int32)
    flat_routes = picked.reshape(token_count * 2, specialist_index)
    busiest_specialist = favored_specialist[0]
    before = (jnp.cumsum(flat_routes, axis=0) - flat_routes).reshape(
        token_count, 2, specialist_index
    )
    ranking = jnp.sum(before * picked, axis=2)
    placement_ceiling = jnp.where(
        jnp.arange(specialist_index, dtype=jnp.int32) == busiest_specialist,
        PLACEMENT_MOST,
        allowed_placements,
    )
    keeping = ranking < jnp.sum(picked * placement_ceiling[None, None, :], axis=2)
    row_total = question_vectors.shape[0]
    heads_out = attend(
        question_vectors.reshape(row_total, -1, HD),
        fresh_lookup_vectors.reshape(row_total, -1, HD),
        fresh_content_vectors.reshape(row_total, -1, HD),
        stored_lookup_sheets,
        stored_content_sheets,
        sequence_sheet_map,
        stored_position_counts,
    )
    own_attn = head_sum(
        jnp.dot(heads_out, attention_merge_matrix, preferred_element_type=jnp.float32).astype(
            jnp.bfloat16
        ),
        lax.axis_size("tensor"),
    ).astype(jnp.float32)
    stream = (skip_stream_entry.astype(jnp.float32) + own_attn).astype(jnp.bfloat16)
    wide = stream.astype(jnp.float32)
    squares = jnp.mean(wide * wide, axis=1, keepdims=True)
    normed = (wide * lax.rsqrt(squares + 1e-05) * premix_scale_factor.astype(jnp.float32)).astype(
        jnp.bfloat16
    )
    main_slots = PLACEMENT_MOST
    table_main = slot_table(picked, ranking, keeping, main_slots)
    send = jnp.einsum(
        "nkes,nd->esd", table_main, normed, preferred_element_type=jnp.float32
    ).astype(jnp.bfloat16)
    expert_out = expert_pass(send, gating_matrices, expand_matrices, contract_matrices)
    chosen = jnp.einsum("nkes,esd->nkd", table_main, expert_out, preferred_element_type=jnp.float32)
    mixed = jnp.sum(selection_shares[:, :, None] * chosen, axis=1)
    return (wide + mixed).astype(jnp.bfloat16)


def solution(mesh):
    placed = (
        P(("dp", "expert", "tensor"), None),
        P(("dp", "expert"), "tensor"),
        P(("dp", "expert"), "tensor"),
        P(("dp", "expert"), "tensor"),
        P(("dp", "expert"), "tensor", None, None),
        P(("dp", "expert"), "tensor", None, None),
        P(("dp", "expert"), None),
        P(("dp", "expert")),
        P("tensor", None),
        P(),
        P(("dp", "expert", "tensor"), None),
        P(("dp", "expert", "tensor"), None),
        P(),
        P(),
        P("expert", ("dp", "tensor"), None),
        P("expert", ("dp", "tensor"), None),
        P("expert", ("dp", "tensor"), None),
    )
    return jax.shard_map(
        local,
        mesh=mesh,
        in_specs=placed,
        out_specs=P(("dp", "expert", "tensor"), None),
        check_vma=False,
    )
```
